32 devices in a mesh: ep: 16 (over z, x, core), etp: 2 (over y).
Axes of the slice: x: 2, y: 2, z: 4, core: 2. Of those that a mesh axis runs over, the one named last changes fastest.
Arguments:
- tokens: bfloat16 [2048, 4096], P('ep', 'etp'), may hold values from -6 to 6
- grad_out: bfloat16 [2048, 4096], P('ep', 'etp'), may hold values from -1.5 to 1.5
- gates: float32 [2048, 8], P('ep'), may hold values from 0.05 to 0.5
- expert_ids: int32 [2048, 8], P('ep'), may hold values from 0 to 15, all different within a row; in each aligned block of 128 rows (0 to 127, 128 to 255, ...) at most 72 rows name the same one
- gate_proj: bfloat16 [16, 4096, 1536], P('ep', None, 'etp'), may hold values from -0.09375 to 0.09375
- up_proj: bfloat16 [16, 4096, 1536], P('ep', None, 'etp'), may hold values from -0.09375 to 0.09375
- down_proj: bfloat16 [16, 1536, 4096], P('ep', 'etp'), may hold values from -0.15625 to 0.15625
Outputs:
- layer_out: bfloat16 [2048, 4096], P('ep', 'etp')
- token_grad: bfloat16 [2048, 4096], P('ep', 'etp')
- slot_gate_grad: float32 [2048, 8], P('ep')
The draws below stay inside these ranges and needn't reach their ends.
Inputs may be any that keep to these rules, and one draw needn't show every extreme that they name: `expert_ids`: each row names 8 different experts. Within the rows of one index of ep (aligned blocks of 128 rows) no expert is named by more than 72 rows, and in every draw some expert is named by exactly 72 rows of some block.
All inputs are finite; a program needn't handle non-finite values.
Results may differ from the reference program's by a relative error of at most 0.015.
Values may be sent and summed in bfloat16 or wider, within the bound.
A program may use at most 128 MiB of HBM per device.

```python
import math
import jax
import jax.numpy as jnp
import numpy as np
from jax import lax

D = 4096
HID = 1536
TOP = 8
TOK_DEV = 128
TOKENS = 2048
EXPERTS = 16
HQ = 768
CAP = 72
N_EP = 16
N_ETP = 2


def level_of(own_key, extent, shards, least, top_value):
    def one(dim, blocks):
        steps = jax.random.uniform(jax.random.fold_in(jax.random.fold_in(own_key, 6), dim), (blocks,), jnp.float32, least / len(shards), top_value / len(shards))
        return jnp.repeat(jnp.exp(steps), extent[dim] // blocks).reshape((-1,) + (1,) * (len(extent) - dim - 1))

    gain = one(*shards[0])
    for cut in shards[1:]:
        gain = gain * one(*cut)
    return gain


def deal_out(key, own, number, rows, count, top, bound, slope):
    sequence = jax.random.permutation(key, count)
    crowded, usual = shares(count, rows * top, bound, slope, True), shares(count, rows * top, bound, slope, False)
    places = jnp.arange(count)

    def named(tallies, rotation):
        used = int((tallies > 0).sum())
        fixed = max(1, used // 4)
        shifted = fixed + (places - fixed + rotation * (used - fixed)) % max(1, count - fixed)
        return jnp.zeros((count,), jnp.int32).at[sequence[jnp.where(places < fixed, places, shifted)]].set(jnp.asarray(tallies, jnp.int32))

    tallies = jnp.where(number % 4 == 0, named(crowded, number // 4), named(usual, number - number // 4 - 1))
    mixed = jax.random.permutation(jax.random.fold_in(own, 3), count)
    source_of, receiver = mixed[0:count // 2 * 2:2], mixed[1:count // 2 * 2:2]
    margin = jnp.minimum(tallies[source_of] - 1, bound - tallies[receiver]) // 2
    margin = jnp.where((source_of == sequence[0]) | (receiver == sequence[0]) | (tallies[receiver] == 0), 0, jnp.maximum(margin, 0))
    shifted = jax.random.randint(jax.random.fold_in(own, 4), (count // 2,), 0, 1 << 20) % (margin + 1)
    tallies = tallies.at[source_of].add(-shifted).at[receiver].add(shifted)
    items = jnp.searchsorted(jnp.cumsum(tallies), jnp.arange(rows * top), side="right").astype(jnp.int32)
    grid = items.reshape(top, rows).T
    grid = grid[jax.random.permutation(jax.random.fold_in(own, 1), rows)]
    rotation = jax.random.randint(jax.random.fold_in(own, 2), (rows, 1), 0, top)
    return jnp.take_along_axis(grid, (jnp.arange(top)[None, :] + rotation) % top, axis=1)


def shares(amount, total, reach, lean, full):
    portions = [(1 << 20) // math.isqrt(standing ** lean) + 1 for standing in range(1, amount + 1)]
    largest = reach if full else min(reach, max(-(-total // amount), total * portions[0] // sum(portions)))
    least = 1 if total - largest >= amount - 1 else 0
    holding, surplus = [largest] + [least] * (amount - 1), total - largest - least * (amount - 1)
    while surplus > 0:
        movable = [i for i in range(1, amount) if holding[i] < largest] or [i for i in range(1, amount) if holding[i] < reach]
        pool, left = sum([portions[i] for i in movable]), surplus
        for i in movable:
            addition = min(reach - holding[i], max(1, left * portions[i] // pool), surplus)
            holding[i] = holding[i] + addition
            surplus = surplus - addition
    return np.array(holding)


def normal_values(key, shape, width, limit, cuts=(), held_as=jnp.bfloat16):
    values = jax.random.normal(key, shape, jnp.float32) * width
    if len(cuts) > 0:
        values = level_of(key, shape, cuts, -0.22, 0.18) * values
    return jnp.clip(values, min=-limit, max=limit).astype(held_as)


def setup_inputs(seed: int = 0) -> dict:
    seeds = jax.random.split(jax.random.key(seed), 8)
    tokens = normal_values(seeds[0], (TOKENS, D), 1.0, 6.0, ((0, 16), (1, 2)))
    grad_out = normal_values(seeds[1], (TOKENS, D), 0.25, 1.5, ((0, 16), (1, 2)))
    gates = jnp.clip(jnp.exp(math.log(0.5) - 2.3025851 * jax.random.uniform(seeds[2], (TOKENS, TOP), jnp.float32) ** level_of(seeds[2], (TOKENS, TOP), ((0, 16),), -0.2, 0.2)), 0.05, 0.5)
    expert_ids_keys = jax.random.split(jax.random.fold_in(seeds[3], 1), TOKENS // TOK_DEV)
    expert_ids_turns = jax.random.permutation(jax.random.fold_in(seeds[3], 3), TOKENS // TOK_DEV)
    expert_ids = jax.vmap(lambda own, number: deal_out(jax.random.fold_in(seeds[3], 2), own, number, TOK_DEV, EXPERTS, TOP, CAP, 1))(expert_ids_keys, expert_ids_turns).reshape((TOKENS, TOP))
    gate_proj = normal_values(seeds[4], (EXPERTS, D, HID), D ** -0.5, 0.09375, ((0, 16), (2, 2)))
    up_proj = normal_values(seeds[5], (EXPERTS, D, HID), D ** -0.5, 0.09375, ((0, 16), (2, 2)))
    down_proj = normal_values(seeds[6], (EXPERTS, HID, D), HID ** -0.5, 0.15625, ((0, 16), (1, 2)))
    return dict(tokens=tokens, grad_out=grad_out, gates=gates, expert_ids=expert_ids, gate_proj=gate_proj, up_proj=up_proj, down_proj=down_proj)


def reference(tokens, grad_out, gates, expert_ids, gate_proj, up_proj, down_proj):
    rows_total = TOKENS * TOP
    slots_all = N_EP * CAP
    flat_ids = expert_ids.reshape(N_EP, TOK_DEV * TOP)
    onehot = (flat_ids[:, :, None] == jnp.arange(EXPERTS, dtype=jnp.int32)[None, None, :]).astype(jnp.int32)
    before = jnp.cumsum(onehot, axis=1) - onehot
    slot_pos = jnp.sum(before * onehot, axis=2)
    source = jnp.arange(N_EP, dtype=jnp.int32)[:, None]
    target = (flat_ids * slots_all + source * CAP + slot_pos).reshape(rows_total).astype(jnp.int32)
    row_table = jnp.full((EXPERTS * slots_all,), rows_total, jnp.int32)
    row_table = row_table.at[target].set(jnp.arange(rows_total, dtype=jnp.int32)).reshape(EXPERTS, slots_all)
    gate_flat = gates.reshape(rows_total)

    def one_expert(expert):
        copy_idx = row_table[expert]
        is_live = copy_idx < rows_total
        safe_idx = jnp.minimum(copy_idx, rows_total - 1)
        token_idx = safe_idx // TOP
        token_rows = jnp.where(is_live[:, None], tokens[token_idx], jnp.zeros((), tokens.dtype))
        gate_rows = jnp.where(is_live, gate_flat[safe_idx], jnp.zeros((), jnp.float32))
        signal = (gate_rows[:, None] * grad_out[token_idx].astype(jnp.float32)).astype(jnp.bfloat16)
        gate_mat = gate_proj[expert]
        up_mat = up_proj[expert]
        down_mat = down_proj[expert]
        gate_pre = jnp.dot(token_rows, gate_mat, preferred_element_type=jnp.float32)
        up_pre = jnp.dot(token_rows, up_mat, preferred_element_type=jnp.float32)
        sigmoid_gate = jax.nn.sigmoid(gate_pre)
        hidden = (gate_pre * sigmoid_gate * up_pre).astype(jnp.bfloat16)
        grouped = hidden.astype(jnp.float32).reshape(slots_all, N_ETP, HQ)
        down_grouped = down_mat.astype(jnp.float32).reshape(N_ETP, HQ, D)
        part_out = jnp.einsum("rgh,ghd->rgd", grouped, down_grouped).astype(jnp.bfloat16)
        part_out = lax.optimization_barrier(part_out)
        copy_out = jnp.sum(part_out.astype(jnp.float32), axis=1).astype(jnp.bfloat16)
        hidden_grad = jnp.dot(signal, down_mat.T, preferred_element_type=jnp.float32)
        gate_grad = (hidden_grad * up_pre * sigmoid_gate * (1.0 + gate_pre * (1.0 - sigmoid_gate))).astype(jnp.bfloat16)
        up_grad = (hidden_grad * gate_pre * sigmoid_gate).astype(jnp.bfloat16)
        gate_groups = gate_grad.astype(jnp.float32).reshape(slots_all, N_ETP, HQ)
        up_groups = up_grad.astype(jnp.float32).reshape(slots_all, N_ETP, HQ)
        gate_cols = gate_mat.astype(jnp.float32).reshape(D, N_ETP, HQ)
        up_cols = up_mat.astype(jnp.float32).reshape(D, N_ETP, HQ)
        part_in = jnp.einsum("rgh,dgh->rgd", gate_groups, gate_cols) + jnp.einsum("rgh,dgh->rgd", up_groups, up_cols)
        part_in = lax.optimization_barrier(part_in.astype(jnp.bfloat16))
        copy_in = jnp.sum(part_in.astype(jnp.float32), axis=1).astype(jnp.bfloat16)
        return copy_out, copy_in

    out_all, in_all = lax.map(one_expert, jnp.arange(EXPERTS, dtype=jnp.int32))
    out_flat = out_all.reshape(EXPERTS * slots_all, D)
    in_flat = in_all.reshape(EXPERTS * slots_all, D)
    target_tok = target.reshape(TOKENS, TOP)
    mixed = jnp.zeros((TOKENS, D), jnp.float32)
    input_grad = jnp.zeros((TOKENS, D), jnp.float32)
    grad_wide = grad_out.astype(jnp.float32)
    scores = []
    for slot_num in range(TOP):
        copy_out = out_flat[target_tok[:, slot_num]].astype(jnp.float32)
        mixed = mixed + gates[:, slot_num:slot_num + 1] * copy_out
        input_grad = input_grad + in_flat[target_tok[:, slot_num]].astype(jnp.float32)
        scores.append(jnp.sum(grad_wide * copy_out, axis=1))
    return mixed.astype(jnp.bfloat16), input_grad.astype(jnp.bfloat16), jnp.stack(scores, axis=1)
```

```python
import functools
import math

import jax
import jax.numpy as jnp
import numpy as np
from jax import lax
from jax.experimental import pallas as pl
from jax.experimental.pallas import tpu as pltpu
from jax.sharding import PartitionSpec as P

BF = jnp.bfloat16
F32 = jnp.float32
MESH = pl.DeviceIdType.MESH


class Place:
    def __init__(self, ring, groups):
        self.ring, self.groups = ring, groups
        self.depth = math.gcd(ring, 4)
        self.cols = ring // self.depth
        me = lax.axis_index("ep")
        self.g = lax.axis_index("etp")
        self.core = lax.rem(me, 2)
        chip = me // 2
        x, z = lax.rem(chip, self.cols), chip // self.cols
        self.p = x * self.depth + z + lax.rem(x, 2) * (self.depth - 1 - 2 * z)

    def at(self, offset):
        return lax.rem(self.p + offset + self.ring, self.ring)

    def chip(self, offset):
        pos = self.at(offset)
        x, t = pos // self.depth, lax.rem(pos, self.depth)
        z = t + lax.rem(x, 2) * (self.depth - 1 - 2 * t)
        return ((z * self.cols + x) * 2 + self.core, self.g)

    def sibling(self):
        return (lax.axis_index("ep") + 1 - 2 * self.core, self.g)

    def group(self, j):
        return lax.rem(self.g + j, self.groups)

    def partner(self, j):
        return (lax.axis_index("ep"), self.group(j))

    def greet(self, with_sibling):
        barrier = pltpu.get_barrier_semaphore()
        others = [self.chip(1), self.chip(-1)] + [self.partner(j) for j in range(1, self.groups)]
        if with_sibling:
            others.append(self.sibling())
        for other in others:
            pl.semaphore_signal(barrier, inc=1, device_id=other, device_id_type=MESH)
        pl.semaphore_wait(barrier, len(others))


def remote(src, dst, send, recv, where):
    return pltpu.make_async_remote_copy(
        src_ref=src, dst_ref=dst, send_sem=send, recv_sem=recv, device_id=where, device_id_type=MESH
    )


def gather_kernel(
    ring, groups, tok_ref, grad_ref, tok, tok_sib, grad, grad_sib, local_sem, first, rings, fans, late
):
    at = Place(ring, groups)
    at.greet(True)
    g = at.g
    sib = at.sibling()
    own_tok = pltpu.make_async_copy(tok_ref, tok.at[g, at.p], local_sem.at[0])
    own_grad = pltpu.make_async_copy(grad_ref, grad.at[g, at.p], local_sem.at[1])
    own_tok.start()
    own_grad.start()
    heads = []
    for j in range(1, groups):
        head = remote(
            grad_ref, grad.at[g, at.p], first.at[0, j - 1], first.at[1, j - 1], at.partner(j)
        )
        head.start()
        heads.append(head)
    own_tok.wait()

    def back(d, s):
        return at.at(-s if d == 0 else s)

    fan_y, fan_s, fan_t = {}, {}, {}

    def fan_tok(s):
        for d in range(2):
            b = back(d, s)
            fan_y[s, d] = []
            for j in range(1, groups):
                c = remote(
                    tok.at[g, b, d],
                    tok.at[g, b, d],
                    fans.at[0, j, d, s],
                    fans.at[1, j, d, s],
                    at.partner(j),
                )
                c.start()
                fan_y[s, d].append(c)

    def fan_grad(s):
        for d in range(2):
            b = back(d, s)
            c = remote(
                grad.at[:, b, d], grad_sib.at[:, b, d], fans.at[0, 0, d, s], fans.at[1, 0, d, s], sib
            )
            c.start()
            fan_s[s, d] = c

    def fan_late(s):
        for d in range(2):
            b = back(d, s)
            for c in fan_y[s, d]:
                c.wait_recv()
            c = remote(tok.at[:, b, d], tok_sib.at[:, b, d], late.at[0, d, s], late.at[1, d, s], sib)
            c.start()
            fan_t[s, d] = c

    hops = {}

    def hop(kind, d, s):
        b = back(d, s - 1)
        block = tok.at[g, b, d] if kind == 0 else grad.at[:, b, d]
        if s > 1:
            hops[kind, d, s - 1].wait_recv()
        if s < ring:
            c = remote(
                block,
                block,
                rings.at[0, kind, d, s - 1],
                rings.at[1, kind, d, s - 1],
                at.chip(1 if d == 0 else -1),
            )
            c.start()
            hops[kind, d, s] = c

    for s in range(1, ring + 1):
        hop(0, 0, s)
        hop(0, 1, s)
        if s == 1:
            own_grad.wait()
            for head in heads:
                head.wait_recv()
        if s < ring:
            fan_tok(s - 1)
        hop(1, 0, s)
        hop(1, 1, s)
        if s < ring:
            fan_grad(s - 1)
        if s >= 2:
            fan_late(s - 2)
    fan_tok(ring - 1)
    fan_grad(ring - 1)
    fan_late(ring - 1)
    for c in list(fan_s.values()) + list(fan_t.values()):
        c.wait()
    for group in fan_y.values():
        for c in group:
            c.wait_send()
    for c in list(hops.values()) + heads:
        c.wait_send()


def gather(tokens, grad_out, ring, groups):
    rows, width = tokens.shape
    half = rows // 2
    full = jax.ShapeDtypeStruct((groups, ring, 2, half, width), BF)
    dma = pltpu.SemaphoreType.DMA
    hbm = pl.BlockSpec(memory_space=pltpu.HBM)
    return pl.pallas_call(
        functools.partial(gather_kernel, ring, groups),
        out_shape=(full,) * 4,
        in_specs=[hbm, hbm],
        out_specs=(hbm,) * 4,
        scratch_shapes=[
            dma((2,)),
            dma((2, groups - 1)),
            dma((2, 2, 2, ring - 1)),
            dma((2, groups, 2, ring)),
            dma((2, 2, ring)),
        ],
        compiler_params=pltpu.CompilerParams(collective_id=0, has_side_effects=True),
    )(tokens.reshape(2, half, width), grad_out.reshape(2, half, width))


def scatter_kernel(
    ring, groups, s_out, s_in, res_out, res_in, v_out, v_in, r_out, r_in, y_in, y_out, loads, rings, ys, tail
):
    at = Place(ring, groups)
    g = at.g
    half = v_in.shape[2]

    def dest(d, s):
        return at.at(-s if d == 0 else s)

    load_out, load_in, swap = {}, {}, {}
    for s in range(1, ring + 1):
        for d in range(2):
            b = dest(d, s)
            load_out[s, d] = pltpu.make_async_copy(
                s_out.at[:, b, d], v_out.at[:, b, d], loads.at[0, d, s - 1]
            )
            load_in[s, d] = pltpu.make_async_copy(s_in.at[g, b, d], v_in.at[b, d], loads.at[1, d, s - 1])
            load_out[s, d].start()
            load_in[s, d].start()
    at.greet(False)
    for s in range(1, ring + 1):
        for d in range(2):
            b = dest(d, s)
            swap[s, d] = []
            for j in range(1, groups):
                c = remote(
                    s_in.at[at.group(j), b, d],
                    y_in.at[j - 1, b, d],
                    ys.at[0, j - 1, d, s - 1],
                    ys.at[1, j - 1, d, s - 1],
                    at.partner(j),
                )
                c.start()
                swap[s, d].append(c)

    def total(target, others):
        @pl.loop(0, half // 16)
        def _(i):
            rows = pl.ds(pl.multiple_of(i * 16, 16), 16)
            acc = target[rows, :].astype(F32)
            for other in others:
                acc = acc + other[rows, :].astype(F32)
            target[rows, :] = acc.astype(BF)

    hop_out, hop_in = {}, {}
    for s in range(1, ring + 1):
        for d in range(2):
            b = dest(d, s)
            load_out[s, d].wait()
            if s > 1:
                hop_out[s - 1, d].wait_recv()
                for q in range(groups):
                    total(v_out.at[q, b, d], [r_out.at[d, s - 2, q]])
            if s < ring:
                c = remote(
                    v_out.at[:, b, d],
                    r_out.at[d, s - 1],
                    rings.at[0, 0, d, s - 1],
                    rings.at[1, 0, d, s - 1],
                    at.chip(1 if d == 0 else -1),
                )
                c.start()
                hop_out[s, d] = c
        if s == ring:
            ends = []
            for d in range(2):
                for j in range(1, groups):
                    c = remote(
                        v_out.at[at.group(j), at.p, d],
                        y_out.at[j - 1, d],
                        tail.at[0, j - 1, d],
                        tail.at[1, j - 1, d],
                        at.partner(j),
                    )
                    c.start()
                    ends.append(c)
        for d in range(2):
            b = dest(d, s)
            load_in[s, d].wait()
            others = []
            for c in swap[s, d]:
                c.wait_recv()
            others = [y_in.at[j - 1, b, d] for j in range(1, groups)]
            if s > 1:
                hop_in[s - 1, d].wait_recv()
                others.append(r_in.at[d, s - 2])
            total(v_in.at[b, d], others)
            if s < ring:
                c = remote(
                    v_in.at[b, d],
                    r_in.at[d, s - 1],
                    rings.at[0, 1, d, s - 1],
                    rings.at[1, 1, d, s - 1],
                    at.chip(1 if d == 0 else -1),
                )
                c.start()
                hop_in[s, d] = c
    for d in range(2):
        res_in[d] = v_in[at.p, d]
    for c in ends:
        c.wait_recv()
    for d in range(2):
        total(v_out.at[g, at.p, d], [y_out.at[j - 1, d] for j in range(1, groups)])
        res_out[d] = v_out[g, at.p, d]
    for c in list(hop_out.values()) + list(hop_in.values()) + ends:
        c.wait_send()
    for group in swap.values():
        for c in group:
            c.wait_send()


def scatter(s_out, s_in):
    groups, ring, _, half, width = s_out.shape
    res = jax.ShapeDtypeStruct((2, half, width), BF)
    dma = pltpu.SemaphoreType.DMA
    hbm = pl.BlockSpec(memory_space=pltpu.HBM)
    vmem = pl.BlockSpec(memory_space=pltpu.VMEM)
    out, inn = pl.pallas_call(
        functools.partial(scatter_kernel, ring, groups),
        out_shape=(res, res),
        in_specs=[hbm, hbm],
        out_specs=(vmem, vmem),
        scratch_shapes=[
            pltpu.VMEM((groups, ring, 2, half, width), BF),
            pltpu.VMEM((ring, 2, half, width), BF),
            pltpu.VMEM((2, ring - 1, groups, half, width), BF),
            pltpu.VMEM((2, ring - 1, half, width), BF),
            pltpu.VMEM((groups - 1, ring, 2, half, width), BF),
            pltpu.VMEM((groups - 1, 2, half, width), BF),
            dma((2, 2, ring)),
            dma((2, 2, 2, ring - 1)),
            dma((2, groups - 1, 2, ring)),
            dma((2, groups - 1, 2)),
        ],
        compiler_params=pltpu.CompilerParams(
            collective_id=1, has_side_effects=True, vmem_limit_bytes=60 << 20
        ),
    )(s_out, s_in)
    return out.reshape(2 * half, width), inn.reshape(2 * half, width)


def dot(a, b):
    return lax.dot_general(a, b, (((1,), (0,)), ((), ())), preferred_element_type=F32)


def dot_t(a, b):
    return lax.dot_general(a, b, (((1,), (1,)), ((), ())), preferred_element_type=F32)


def first_half(groups, gate_ref, tok, grad, gate_w, up_w, down_w, score):
    width = tok.shape[2]
    cuts = [slice(g * width, (g + 1) * width) for g in range(groups)]
    gate_pre = sum(dot(tok[g], gate_w[cuts[g], :]) for g in range(groups))
    up_pre = sum(dot(tok[g], up_w[cuts[g], :]) for g in range(groups))
    raw = sum(dot_t(grad[g], down_w[:, cuts[g]]) for g in range(groups))
    gate = gate_ref[...]
    sig = jax.nn.sigmoid(gate_pre)
    act = gate_pre * sig
    hidden = act * up_pre
    score[...] = jnp.sum(hidden * raw, axis=1, keepdims=True)
    back = raw * gate
    gate_grad = back * up_pre * sig * (1.0 + gate_pre * (1.0 - sig))
    return (hidden * gate).astype(BF), gate_grad.astype(BF), (back * act).astype(BF)


def second_half(groups, hidden, gate_grad, up_grad, gate_w, up_w, down_w, out, inn, add=None):
    width = out.shape[2]
    for g in range(groups):
        cut = slice(g * width, (g + 1) * width)
        res = dot(hidden, down_w[:, cut])
        if add:
            res = res + add[0][g].astype(F32)
        out[g] = res.astype(BF)
        res = dot_t(gate_grad, gate_w[cut, :]) + dot_t(up_grad, up_w[cut, :])
        if add:
            res = res + add[1][g].astype(F32)
        inn[g] = res.astype(BF)


def whole_kernel(groups, gate, tok, grad, gate_w, up_w, down_w, out, inn, score):
    mids = first_half(groups, gate, tok, grad, gate_w, up_w, down_w, score)
    second_half(groups, *mids, gate_w, up_w, down_w, out, inn)


def begin_kernel(groups, gate, tok, grad, gate_w, up_w, down_w, hidden, gate_grad, up_grad, score):
    mids = first_half(groups, gate, tok, grad, gate_w, up_w, down_w, score)
    hidden[...], gate_grad[...], up_grad[...] = mids


def finish_kernel(groups, hidden, gate_grad, up_grad, gate_w, up_w, down_w, add_out, add_in, out, inn):
    second_half(
        groups,
        hidden[...],
        gate_grad[...],
        up_grad[...],
        gate_w,
        up_w,
        down_w,
        out,
        inn,
        (add_out, add_in),
    )


def expert(stage, shape, weights, *rows):
    groups, count, width = shape
    hid = weights[0].shape[2]
    tile = 256
    slab = (pl.BlockSpec((groups, tile, width), lambda i: (0, i, 0)), jax.ShapeDtypeStruct(shape, BF))
    column = (pl.BlockSpec((tile, 1), lambda i: (i, 0)), jax.ShapeDtypeStruct((count, 1), F32))
    units = (pl.BlockSpec((tile, hid), lambda i: (i, 0)), jax.ShapeDtypeStruct((count, hid), BF))
    fixed = [
        pl.BlockSpec((None,) + w.shape[1:], lambda i: (0, 0, 0), pipeline_mode=pl.Buffered(1))
        for w in weights
    ]
    kernel, heads, tails, results = {
        "whole": (whole_kernel, [column, slab, slab], [], [slab, slab, column]),
        "begin": (begin_kernel, [column, slab, slab], [], [units, units, units, column]),
        "finish": (finish_kernel, [units, units, units], [slab, slab], [slab, slab]),
    }[stage]
    split = len(heads)
    return pl.pallas_call(
        functools.partial(kernel, groups),
        grid=(count // tile,),
        out_shape=[r[1] for r in results],
        in_specs=[h[0] for h in heads] + fixed + [t[0] for t in tails],
        out_specs=[r[0] for r in results],
        input_output_aliases={6: 0, 7: 1} if stage == "finish" else {},
        cost_estimate=pl.CostEstimate(
            flops=(12 if stage == "whole" else 6) * count * groups * width * hid,
            bytes_accessed=8 * count * groups * width,
            transcendentals=0 if stage == "finish" else count * hid,
        ),
        compiler_params=pltpu.CompilerParams(vmem_limit_bytes=60 << 20),
    )(*rows[:split], *weights, *rows[split:])


def local(tokens, grad_out, gates, expert_ids, gate_proj, up_proj, down_proj):
    rows, width = tokens.shape
    groups = lax.axis_size("etp")
    experts = lax.axis_size("ep")
    ring = experts // 2
    core = lax.rem(lax.axis_index("ep"), 2)
    depth = math.gcd(ring, 4)
    cols = ring // depth
    order = np.zeros(ring, np.int32)
    for pos in range(ring):
        x, t = pos // depth, pos % depth
        order[pos] = (t if x % 2 == 0 else depth - 1 - t) * cols + x
    inverse = np.argsort(order)
    count = ring * rows

    onehot = expert_ids[:, :, None] == jnp.arange(experts, dtype=jnp.int32)[None, None, :]
    table = jnp.sum(jnp.where(onehot, gates[:, :, None], 0.0), axis=1)
    mine = lax.all_to_all(table.T, "ep", split_axis=0, concat_axis=0, tiled=True)
    mine = mine.reshape(ring, 2, rows)
    mine = jnp.stack([mine[int(c)] for c in order]).transpose(1, 0, 2)
    mine = jnp.where(core == 0, mine, mine[::-1])

    flat = (groups, count, width)
    tok_own, tok_sib, grad_own, grad_sib = (
        a.reshape(flat) for a in gather(tokens, grad_out, ring, groups)
    )
    swap = [(i, i ^ 1) for i in range(experts)]
    weights = (gate_proj, up_proj, down_proj)
    *mids, score_own = expert("begin", flat, weights, mine[0].reshape(count, 1), tok_own, grad_own)
    out, inn, score_sib = expert("whole", flat, weights, mine[1].reshape(count, 1), tok_sib, grad_sib)
    got = (lax.ppermute(out, "ep", swap), lax.ppermute(inn, "ep", swap))
    out, inn = expert("finish", flat, weights, *mids, *got)
    scores = [score_own.reshape(ring, rows), score_sib.reshape(ring, rows)]
    shape = (groups, ring, 2, rows // 2, width)
    layer_out, token_grad = scatter(out.reshape(shape), inn.reshape(shape))

    score = jnp.stack(scores)
    score = jnp.where(core == 0, score, score[::-1]).transpose(1, 0, 2)
    score = jnp.stack([score[int(c)] for c in inverse]).reshape(experts, rows)
    score = lax.all_to_all(score, "ep", split_axis=0, concat_axis=0, tiled=True)
    score = lax.psum(score, "etp")
    picked = jnp.sum(jnp.where(onehot, score.T[:, None, :], 0.0), axis=2)
    return layer_out, token_grad, picked


def fused_kernel(
    ring, groups, slots, tok_ref, grad_ref, gate_ref, gate_hbm, up_hbm, down_hbm,
    res_out, res_in, score, inb, sib_in,
    gate_w, up_w, down_w, st, sst, r_out, r_in, y_in, y_out,
    local_sem, head_sem, hop_t, hop_g, fan_sem, sib_t, sib_g, sib_r, swap_sem, ring_o, ring_i, tail_sem,
):
    at = Place(ring, groups)
    g = at.g
    sib = at.sibling()
    half, width = st.shape[5], st.shape[6]
    rows = 4 * half
    near = [at.chip(1), at.chip(-1)]
    cuts = [slice(q * width, (q + 1) * width) for q in range(groups)]
    mates = range(1, groups)

    def hop_tok(d, s, src=None):
        src = inb.at[s, 0, g, 0, d] if src is None else src
        return remote(src, inb.at[s + 1, 0, g, 0, d], hop_t.at[0, d, s], hop_t.at[1, d, s], near[d])

    def hop_grad(d, s):
        return remote(
            inb.at[s, 1, :, 0, d], inb.at[s + 1, 1, :, 0, d], hop_g.at[0, d, s], hop_g.at[1, d, s], near[d]
        )

    def head(j):
        return remote(
            grad_ref, inb.at[0, 1, g, 0], head_sem.at[0, j - 1], head_sem.at[1, j - 1], at.partner(j)
        )

    def fan(j, s):
        return remote(
            inb.at[s, 0, g, 0], inb.at[s, 0, g, 0], fan_sem.at[0, j - 1, s], fan_sem.at[1, j - 1, s],
            at.partner(j),
        )

    def sib_tok(s):
        return remote(inb.at[s, 0, :, 0], inb.at[s, 0, :, 1], sib_t.at[0, s], sib_t.at[1, s], sib)

    def sib_grad(s):
        return remote(inb.at[s, 1, :, 0], inb.at[s, 1, :, 1], sib_g.at[0, s], sib_g.at[1, s], sib)

    def sib_res(slot, s):
        return remote(st.at[slot, :, :, 1], sib_in.at[s], sib_r.at[0, s], sib_r.at[1, s], sib)

    def swap(j, slot, s):
        return remote(
            st.at[slot, 1, at.group(j), 0], y_in.at[s, j - 1], swap_sem.at[0, j - 1, s],
            swap_sem.at[1, j - 1, s], at.partner(j),
        )

    def send_out(d, slot, s):
        return remote(
            st.at[slot, 0, :, 0, d], r_out.at[s - 1, d], ring_o.at[0, d, s], ring_o.at[1, d, s], near[d]
        )

    def send_in(d, slot, s):
        return remote(
            st.at[slot, 1, g, 0, d], r_in.at[s - 1, d], ring_i.at[0, d, s], ring_i.at[1, d, s], near[d]
        )

    def tail(j):
        return remote(
            st.at[0, 0, at.group(j), 0], y_out.at[j - 1], tail_sem.at[0, j - 1], tail_sem.at[1, j - 1],
            at.partner(j),
        )

    def total(target, others, dest=None):
        dest = target if dest is None else dest

        @pl.loop(0, half // 16)
        def _(i):
            part = pl.ds(pl.multiple_of(i * 16, 16), 16)
            acc = target[part, :].astype(F32)
            for other in others:
                acc = acc + other[part, :].astype(F32)
            dest[part, :] = acc.astype(BF)

    def slot_of(j):
        return jnp.where(j == 0, 0, 1 + lax.rem(j + slots - 2, slots - 1))

    loads = [
        pltpu.make_async_copy(src.at[0], dst, local_sem.at[2 + k])
        for k, (src, dst) in enumerate([(gate_hbm, gate_w), (up_hbm, up_w), (down_hbm, down_w)])
    ]
    own_tok = pltpu.make_async_copy(tok_ref, inb.at[0, 0, g, 0], local_sem.at[0])
    own_grad = pltpu.make_async_copy(grad_ref, inb.at[0, 1, g, 0], local_sem.at[1])
    own_tok.start()
    own_grad.start()
    at.greet(True)
    for d in range(2):
        hop_tok(d, 0, tok_ref.at[d]).start()
    for j in mates:
        head(j).start()
    own_tok.wait()
    for j in mates:
        fan(j, 0).start()
    for load in loads:
        load.start()
    own_grad.wait()
    for j in mates:
        head(j).wait_recv()
    for d in range(2):
        hop_grad(d, 0).start()
    sib_grad(0).start()

    def free(slot, b):
        sib_res(slot, b).wait_send()
        for j in mates:
            swap(j, slot, b).wait_send()
        for d in range(2):
            send_out(d, slot, b).wait_send()
            send_in(d, slot, b).wait_send()

    @pl.loop(1, ring + 1)
    def _(i):
        j = i - 1
        slot = slot_of(j)
        for k in mates:
            fan(k, j).wait_recv()
        sib_tok(j).start()

        @pl.when(i < ring)
        def _():
            for d in range(2):
                hop_tok(d, i - 1).wait_recv()

                @pl.when(i < ring - 1)
                def _():
                    hop_tok(d, i).start()

            for k in mates:
                fan(k, i).start()
            for d in range(2):
                hop_grad(d, i - 1).wait_recv()

                @pl.when(i < ring - 1)
                def _():
                    hop_grad(d, i).start()

            sib_grad(i).start()

        @pl.when(j >= slots)
        def _():
            free(slot, j - slots + 1)

        sib_grad(j).wait_recv()
        sib_tok(j).wait_recv()
        load = pltpu.make_async_copy(inb.at[j], st.at[slot], local_sem.at[0])
        load.start()

        @pl.when(j == 0)
        def _():
            for w in loads:
                w.wait()

        load.wait()
        gate_pre = up_pre = raw = 0.0
        for q in range(groups):
            tok = st[slot, 0, q].reshape(rows, width)
            gate_pre = gate_pre + dot(tok, gate_w[cuts[q], :])
            up_pre = up_pre + dot(tok, up_w[cuts[q], :])
        for q in range(groups):
            raw = raw + dot_t(st[slot, 1, q].reshape(rows, width), down_w[:, cuts[q]])
        spots = [
            (at.chip(-j if d == 0 else j)[0] + c * (1 - 2 * at.core), d) for c in range(2) for d in range(2)
        ]
        gate = jnp.concatenate([gate_ref[e, d] for e, d in spots], axis=0)
        sig = jax.nn.sigmoid(gate_pre)
        act = gate_pre * sig
        hidden = act * up_pre
        marks = jnp.sum(hidden * raw, axis=1, keepdims=True)
        for k, (e, d) in enumerate(spots):
            score[e, d] = marks[k * half : (k + 1) * half]
        back = raw * gate
        gate_grad = (back * up_pre * sig * (1.0 + gate_pre * (1.0 - sig))).astype(BF)
        up_grad = (back * act).astype(BF)
        hidden = (hidden * gate).astype(BF)
        shape = (2, 2, half, width)
        for q in range(groups):
            st[slot, 0, q] = dot(hidden, down_w[:, cuts[q]]).astype(BF).reshape(shape)
            res = dot_t(gate_grad, gate_w[cuts[q], :]) + dot_t(up_grad, up_w[cuts[q], :])
            st[slot, 1, q] = res.astype(BF).reshape(shape)
        sib_res(slot, j).start()

        sib_res(slot, j).wait_recv()
        load = pltpu.make_async_copy(sib_in.at[j], sst, local_sem.at[1])
        load.start()
        load.wait()
        for k in mates:
            q = at.group(k)
            for d in range(2):
                total(st.at[slot, 1, q, 0, d], [sst.at[1, q, d]])
            swap(k, slot, j).start()

        def step(first):
            for d in range(2):
                if not first:
                    send_out(d, slot, j - 1).wait_recv()
                for q in range(groups):
                    total(
                        st.at[slot, 0, q, 0, d],
                        [sst.at[0, q, d]] + ([] if first else [r_out.at[j - 2, d, q]]),
                    )
                send_out(d, slot, j).start()
            for k in mates:
                swap(k, slot, j).wait_recv()
            for d in range(2):
                if not first:
                    send_in(d, slot, j - 1).wait_recv()
                total(
                    st.at[slot, 1, g, 0, d],
                    [sst.at[1, g, d]]
                    + [y_in.at[j, k - 1, d] for k in mates]
                    + ([] if first else [r_in.at[j - 2, d]]),
                )
                send_in(d, slot, j).start()

        @pl.when(j == 0)
        def _():
            for d in range(2):
                for q in range(groups):
                    total(st.at[0, 0, q, 0, d], [sst.at[0, q, d]])
                total(st.at[0, 1, g, 0, d], [sst.at[1, g, d]])

        @pl.when(j == 1)
        def _():
            step(True)

        @pl.when(j > 1)
        def _():
            step(False)

    for d in range(2):
        send_out(d, 0, ring - 1).wait_recv()
        for j in mates:
            q = at.group(j)
            total(st.at[0, 0, q, 0, d], [r_out.at[ring - 2, d, q]])
    for j in mates:
        tail(j).start()
    for d in range(2):
        total(st.at[0, 0, g, 0, d], [r_out.at[ring - 2, d, g]])
    for j in mates:
        swap(j, 0, 0).wait_recv()
    for d in range(2):
        send_in(d, 0, ring - 1).wait_recv()
        total(
            st.at[0, 1, g, 0, d],
            [y_in.at[0, j - 1, d] for j in mates] + [r_in.at[ring - 2, d]],
            res_in.at[d],
        )
    for j in mates:
        tail(j).wait_recv()
    for d in range(2):
        total(st.at[0, 0, g, 0, d], [y_out.at[j - 1, d] for j in mates], res_out.at[d])

    sib_res(0, 0).wait_send()
    for j in mates:
        swap(j, 0, 0).wait_send()
        head(j).wait_send()
        tail(j).wait_send()

    @pl.loop(max(1, ring - slots + 1), ring)
    def _(b):
        free(slot_of(b), b)

    @pl.loop(0, ring)
    def _(s):
        for j in mates:
            fan(j, s).wait_send()
        sib_tok(s).wait_send()
        sib_grad(s).wait_send()

        @pl.when(s < ring - 1)
        def _():
            for d in range(2):
                hop_tok(d, s).wait_send()
                hop_grad(d, s).wait_send()


SLOTS = 4


def fused(tokens, grad_out, gate, weights, ring, groups):
    rows, width = tokens.shape
    half = rows // 2
    depth, hid = weights[0].shape[1:]
    res = jax.ShapeDtypeStruct((2, half, width), BF)
    block = (2, groups, 2, 2, half, width)
    dma = pltpu.SemaphoreType.DMA
    hbm = pl.BlockSpec(memory_space=pltpu.HBM)
    vmem = pl.BlockSpec(memory_space=pltpu.VMEM)
    mates = groups - 1
    count = ring * 4 * half
    outs = pl.pallas_call(
        functools.partial(fused_kernel, ring, groups, SLOTS),
        out_shape=(
            res,
            res,
            jax.ShapeDtypeStruct((2 * ring, 2, half, 1), F32),
            jax.ShapeDtypeStruct((ring,) + block, BF),
            jax.ShapeDtypeStruct((ring, 2, groups, 2, half, width), BF),
        ),
        in_specs=[hbm, hbm, vmem, hbm, hbm, hbm],
        out_specs=(vmem, vmem, vmem, hbm, hbm),
        scratch_shapes=[
            pltpu.VMEM((depth, hid), BF),
            pltpu.VMEM((depth, hid), BF),
            pltpu.VMEM((hid, depth), BF),
            pltpu.VMEM((SLOTS,) + block, BF),
            pltpu.VMEM((2, groups, 2, half, width), BF),
            pltpu.VMEM((ring - 1, 2, groups, half, width), BF),
            pltpu.VMEM((ring - 1, 2, half, width), BF),
            pltpu.VMEM((ring, mates, 2, half, width), BF),
            pltpu.VMEM((mates, 2, half, width), BF),
            dma((5,)),
            dma((2, mates)),
            dma((2, 2, ring)),
            dma((2, 2, ring)),
            dma((2, mates, ring)),
            dma((2, ring)),
            dma((2, ring)),
            dma((2, ring)),
            dma((2, mates, ring)),
            dma((2, 2, ring)),
            dma((2, 2, ring)),
            dma((2, mates)),
        ],
        cost_estimate=pl.CostEstimate(
            flops=12 * count * groups * width * hid,
            bytes_accessed=16 * count * groups * width,
            transcendentals=count * hid,
        ),
        compiler_params=pltpu.CompilerParams(
            collective_id=2, has_side_effects=True, vmem_limit_bytes=63 << 20
        ),
    )(tokens.reshape(2, half, width), grad_out.reshape(2, half, width), gate, *weights)
    return outs[0].reshape(rows, width), outs[1].reshape(rows, width), outs[2]


def streamed(tokens, grad_out, gates, expert_ids, gate_proj, up_proj, down_proj):
    rows, width = tokens.shape
    groups = lax.axis_size("etp")
    experts = lax.axis_size("ep")
    ring = experts // 2
    half = rows // 2

    onehot = expert_ids[:, :, None] == jnp.arange(experts, dtype=jnp.int32)[None, None, :]
    table = jnp.sum(jnp.where(onehot, gates[:, :, None], 0.0), axis=1)
    mine = lax.all_to_all(table.T, "ep", split_axis=0, concat_axis=0, tiled=True)
    gate = mine.reshape(experts, 2, half, 1)
    layer_out, token_grad, score = fused(
        tokens, grad_out, gate, (gate_proj, up_proj, down_proj), ring, groups
    )
    score = score.reshape(experts, rows)
    score = lax.all_to_all(score, "ep", split_axis=0, concat_axis=0, tiled=True)
    score = lax.psum(score, "etp")
    picked = jnp.sum(jnp.where(onehot, score.T[:, None, :], 0.0), axis=2)
    return layer_out, token_grad, picked


def solution(mesh):
    in_specs = (
        P("ep", "etp"),
        P("ep", "etp"),
        P("ep", None),
        P("ep", None),
        P("ep", None, "etp"),
        P("ep", None, "etp"),
        P("ep", "etp", None),
    )
    out_specs = (P("ep", "etp"), P("ep", "etp"), P("ep", None))
    body = streamed if mesh.shape["ep"] <= 16 else local
    return jax.shard_map(body, mesh=mesh, in_specs=in_specs, out_specs=out_specs, check_vma=False)
```

```python
import functools
import math

import jax
import jax.numpy as jnp
import numpy as np
from jax import lax
from jax.experimental import pallas as pl
from jax.experimental.pallas import tpu as pltpu
from jax.sharding import PartitionSpec as P

BF = jnp.bfloat16
F32 = jnp.float32
MESH = pl.DeviceIdType.MESH


class Place:
    def __init__(self, ring, groups):
        self.ring, self.groups = ring, groups
        self.depth = math.gcd(ring, 4)
        self.cols = ring // self.depth
        me = lax.axis_index("ep")
        self.g = lax.axis_index("etp")
        self.core = lax.rem(me, 2)
        chip = me // 2
        x, z = lax.rem(chip, self.cols), chip // self.cols
        self.p = x * self.depth + z + lax.rem(x, 2) * (self.depth - 1 - 2 * z)

    def at(self, offset):
        return lax.rem(self.p + offset + self.ring, self.ring)

    def chip(self, offset):
        pos = self.at(offset)
        x, t = pos // self.depth, lax.rem(pos, self.depth)
        z = t + lax.rem(x, 2) * (self.depth - 1 - 2 * t)
        return ((z * self.cols + x) * 2 + self.core, self.g)

    def sibling(self):
        return (lax.axis_index("ep") + 1 - 2 * self.core, self.g)

    def group(self, j):
        return lax.rem(self.g + j, self.groups)

    def partner(self, j):
        return (lax.axis_index("ep"), self.group(j))

    def greet(self, with_sibling):
        barrier = pltpu.get_barrier_semaphore()
        others = [self.chip(1), self.chip(-1)] + [self.partner(j) for j in range(1, self.groups)]
        if with_sibling:
            others.append(self.sibling())
        for other in others:
            pl.semaphore_signal(barrier, inc=1, device_id=other, device_id_type=MESH)
        pl.semaphore_wait(barrier, len(others))


def remote(src, dst, send, recv, where):
    return pltpu.make_async_remote_copy(
        src_ref=src, dst_ref=dst, send_sem=send, recv_sem=recv, device_id=where, device_id_type=MESH
    )


def gather_kernel(
    ring, groups, tok_ref, grad_ref, tok, tok_sib, grad, grad_sib, local_sem, first, rings, fans, late
):
    at = Place(ring, groups)
    at.greet(True)
    g = at.g
    sib = at.sibling()
    own_tok = pltpu.make_async_copy(tok_ref, tok.at[g, at.p], local_sem.at[0])
    own_grad = pltpu.make_async_copy(grad_ref, grad.at[g, at.p], local_sem.at[1])
    own_tok.start()
    own_grad.start()
    heads = []
    for j in range(1, groups):
        head = remote(
            grad_ref, grad.at[g, at.p], first.at[0, j - 1], first.at[1, j - 1], at.partner(j)
        )
        head.start()
        heads.append(head)
    own_tok.wait()

    def back(d, s):
        return at.at(-s if d == 0 else s)

    fan_y, fan_s, fan_t = {}, {}, {}

    def fan_tok(s):
        for d in range(2):
            b = back(d, s)
            fan_y[s, d] = []
            for j in range(1, groups):
                c = remote(
                    tok.at[g, b, d],
                    tok.at[g, b, d],
                    fans.at[0, j, d, s],
                    fans.at[1, j, d, s],
                    at.partner(j),
                )
                c.start()
                fan_y[s, d].append(c)

    def fan_grad(s):
        for d in range(2):
            b = back(d, s)
            c = remote(
                grad.at[:, b, d], grad_sib.at[:, b, d], fans.at[0, 0, d, s], fans.at[1, 0, d, s], sib
            )
            c.start()
            fan_s[s, d] = c

    def fan_late(s):
        for d in range(2):
            b = back(d, s)
            for c in fan_y[s, d]:
                c.wait_recv()
            c = remote(tok.at[:, b, d], tok_sib.at[:, b, d], late.at[0, d, s], late.at[1, d, s], sib)
            c.start()
            fan_t[s, d] = c

    hops = {}

    def hop(kind, d, s):
        b = back(d, s - 1)
        block = tok.at[g, b, d] if kind == 0 else grad.at[:, b, d]
        if s > 1:
            hops[kind, d, s - 1].wait_recv()
        if s < ring:
            c = remote(
                block,
                block,
                rings.at[0, kind, d, s - 1],
                rings.at[1, kind, d, s - 1],
                at.chip(1 if d == 0 else -1),
            )
            c.start()
            hops[kind, d, s] = c

    for s in range(1, ring + 1):
        hop(0, 0, s)
        hop(0, 1, s)
        if s == 1:
            own_grad.wait()
            for head in heads:
                head.wait_recv()
        if s < ring:
            fan_tok(s - 1)
        hop(1, 0, s)
        hop(1, 1, s)
        if s < ring:
            fan_grad(s - 1)
        if s >= 2:
            fan_late(s - 2)
    fan_tok(ring - 1)
    fan_grad(ring - 1)
    fan_late(ring - 1)
    for c in list(fan_s.values()) + list(fan_t.values()):
        c.wait()
    for group in fan_y.values():
        for c in group:
            c.wait_send()
    for c in list(hops.values()) + heads:
        c.wait_send()


def gather(tokens, grad_out, ring, groups):
    rows, width = tokens.shape
    half = rows // 2
    full = jax.ShapeDtypeStruct((groups, ring, 2, half, width), BF)
    dma = pltpu.SemaphoreType.DMA
    hbm = pl.BlockSpec(memory_space=pltpu.HBM)
    return pl.pallas_call(
        functools.partial(gather_kernel, ring, groups),
        out_shape=(full,) * 4,
        in_specs=[hbm, hbm],
        out_specs=(hbm,) * 4,
        scratch_shapes=[
            dma((2,)),
            dma((2, groups - 1)),
            dma((2, 2, 2, ring - 1)),
            dma((2, groups, 2, ring)),
            dma((2, 2, ring)),
        ],
        compiler_params=pltpu.CompilerParams(collective_id=0, has_side_effects=True),
    )(tokens.reshape(2, half, width), grad_out.reshape(2, half, width))


def scatter_kernel(
    ring, groups, s_out, s_in, res_out, res_in, v_out, v_in, r_out, r_in, y_in, y_out, loads, rings, ys, tail
):
    at = Place(ring, groups)
    g = at.g
    half = v_in.shape[2]

    def dest(d, s):
        return at.at(-s if d == 0 else s)

    load_out, load_in, swap = {}, {}, {}
    for s in range(1, ring + 1):
        for d in range(2):
            b = dest(d, s)
            load_out[s, d] = pltpu.make_async_copy(
                s_out.at[:, b, d], v_out.at[:, b, d], loads.at[0, d, s - 1]
            )
            load_in[s, d] = pltpu.make_async_copy(s_in.at[g, b, d], v_in.at[b, d], loads.at[1, d, s - 1])
            load_out[s, d].start()
            load_in[s, d].start()
    at.greet(False)
    for s in range(1, ring + 1):
        for d in range(2):
            b = dest(d, s)
            swap[s, d] = []
            for j in range(1, groups):
                c = remote(
                    s_in.at[at.group(j), b, d],
                    y_in.at[j - 1, b, d],
                    ys.at[0, j - 1, d, s - 1],
                    ys.at[1, j - 1, d, s - 1],
                    at.partner(j),
                )
                c.start()
                swap[s, d].append(c)

    def total(target, others):
        @pl.loop(0, half // 16)
        def _(i):
            rows = pl.ds(pl.multiple_of(i * 16, 16), 16)
            acc = target[rows, :].astype(F32)
            for other in others:
                acc = acc + other[rows, :].astype(F32)
            target[rows, :] = acc.astype(BF)

    hop_out, hop_in = {}, {}
    for s in range(1, ring + 1):
        for d in range(2):
            b = dest(d, s)
            load_out[s, d].wait()
            if s > 1:
                hop_out[s - 1, d].wait_recv()
                for q in range(groups):
                    total(v_out.at[q, b, d], [r_out.at[d, s - 2, q]])
            if s < ring:
                c = remote(
                    v_out.at[:, b, d],
                    r_out.at[d, s - 1],
                    rings.at[0, 0, d, s - 1],
                    rings.at[1, 0, d, s - 1],
                    at.chip(1 if d == 0 else -1),
                )
                c.start()
                hop_out[s, d] = c
        if s == ring:
            ends = []
            for d in range(2):
                for j in range(1, groups):
                    c = remote(
                        v_out.at[at.group(j), at.p, d],
                        y_out.at[j - 1, d],
                        tail.at[0, j - 1, d],
                        tail.at[1, j - 1, d],
                        at.partner(j),
                    )
                    c.start()
                    ends.append(c)
        for d in range(2):
            b = dest(d, s)
            load_in[s, d].wait()
            others = []
            for c in swap[s, d]:
                c.wait_recv()
            others = [y_in.at[j - 1, b, d] for j in range(1, groups)]
            if s > 1:
                hop_in[s - 1, d].wait_recv()
                others.append(r_in.at[d, s - 2])
            total(v_in.at[b, d], others)
            if s < ring:
                c = remote(
                    v_in.at[b, d],
                    r_in.at[d, s - 1],
                    rings.at[0, 1, d, s - 1],
                    rings.at[1, 1, d, s - 1],
                    at.chip(1 if d == 0 else -1),
                )
                c.start()
                hop_in[s, d] = c
    for d in range(2):
        res_in[d] = v_in[at.p, d]
    for c in ends:
        c.wait_recv()
    for d in range(2):
        total(v_out.at[g, at.p, d], [y_out.at[j - 1, d] for j in range(1, groups)])
        res_out[d] = v_out[g, at.p, d]
    for c in list(hop_out.values()) + list(hop_in.values()) + ends:
        c.wait_send()
    for group in swap.values():
        for c in group:
            c.wait_send()


def scatter(s_out, s_in):
    groups, ring, _, half, width = s_out.shape
    res = jax.ShapeDtypeStruct((2, half, width), BF)
    dma = pltpu.SemaphoreType.DMA
    hbm = pl.BlockSpec(memory_space=pltpu.HBM)
    vmem = pl.BlockSpec(memory_space=pltpu.VMEM)
    out, inn = pl.pallas_call(
        functools.partial(scatter_kernel, ring, groups),
        out_shape=(res, res),
        in_specs=[hbm, hbm],
        out_specs=(vmem, vmem),
        scratch_shapes=[
            pltpu.VMEM((groups, ring, 2, half, width), BF),
            pltpu.VMEM((ring, 2, half, width), BF),
            pltpu.VMEM((2, ring - 1, groups, half, width), BF),
            pltpu.VMEM((2, ring - 1, half, width), BF),
            pltpu.VMEM((groups - 1, ring, 2, half, width), BF),
            pltpu.VMEM((groups - 1, 2, half, width), BF),
            dma((2, 2, ring)),
            dma((2, 2, 2, ring - 1)),
            dma((2, groups - 1, 2, ring)),
            dma((2, groups - 1, 2)),
        ],
        compiler_params=pltpu.CompilerParams(
            collective_id=1, has_side_effects=True, vmem_limit_bytes=60 << 20
        ),
    )(s_out, s_in)
    return out.reshape(2 * half, width), inn.reshape(2 * half, width)


def dot(a, b):
    return lax.dot_general(a, b, (((1,), (0,)), ((), ())), preferred_element_type=F32)


def dot_t(a, b):
    return lax.dot_general(a, b, (((1,), (1,)), ((), ())), preferred_element_type=F32)


def first_half(groups, gate_ref, tok, grad, gate_w, up_w, down_w, score):
    width = tok.shape[2]
    cuts = [slice(g * width, (g + 1) * width) for g in range(groups)]
    gate_pre = sum(dot(tok[g], gate_w[cuts[g], :]) for g in range(groups))
    up_pre = sum(dot(tok[g], up_w[cuts[g], :]) for g in range(groups))
    raw = sum(dot_t(grad[g], down_w[:, cuts[g]]) for g in range(groups))
    gate = gate_ref[...]
    sig = jax.nn.sigmoid(gate_pre)
    act = gate_pre * sig
    hidden = act * up_pre
    score[...] = jnp.sum(hidden * raw, axis=1, keepdims=True)
    back = raw * gate
    gate_grad = back * up_pre * sig * (1.0 + gate_pre * (1.0 - sig))
    return (hidden * gate).astype(BF), gate_grad.astype(BF), (back * act).astype(BF)


def second_half(groups, hidden, gate_grad, up_grad, gate_w, up_w, down_w, out, inn, add=None):
    width = out.shape[2]
    for g in range(groups):
        cut = slice(g * width, (g + 1) * width)
        res = dot(hidden, down_w[:, cut])
        if add:
            res = res + add[0][g].astype(F32)
        out[g] = res.astype(BF)
        res = dot_t(gate_grad, gate_w[cut, :]) + dot_t(up_grad, up_w[cut, :])
        if add:
            res = res + add[1][g].astype(F32)
        inn[g] = res.astype(BF)


def whole_kernel(groups, gate, tok, grad, gate_w, up_w, down_w, out, inn, score):
    mids = first_half(groups, gate, tok, grad, gate_w, up_w, down_w, score)
    second_half(groups, *mids, gate_w, up_w, down_w, out, inn)


def begin_kernel(groups, gate, tok, grad, gate_w, up_w, down_w, hidden, gate_grad, up_grad, score):
    mids = first_half(groups, gate, tok, grad, gate_w, up_w, down_w, score)
    hidden[...], gate_grad[...], up_grad[...] = mids


def finish_kernel(groups, hidden, gate_grad, up_grad, gate_w, up_w, down_w, add_out, add_in, out, inn):
    second_half(
        groups,
        hidden[...],
        gate_grad[...],
        up_grad[...],
        gate_w,
        up_w,
        down_w,
        out,
        inn,
        (add_out, add_in),
    )


def expert(stage, shape, weights, *rows):
    groups, count, width = shape
    hid = weights[0].shape[2]
    tile = 256
    slab = (pl.BlockSpec((groups, tile, width), lambda i: (0, i, 0)), jax.ShapeDtypeStruct(shape, BF))
    column = (pl.BlockSpec((tile, 1), lambda i: (i, 0)), jax.ShapeDtypeStruct((count, 1), F32))
    units = (pl.BlockSpec((tile, hid), lambda i: (i, 0)), jax.ShapeDtypeStruct((count, hid), BF))
    fixed = [
        pl.BlockSpec((None,) + w.shape[1:], lambda i: (0, 0, 0), pipeline_mode=pl.Buffered(1))
        for w in weights
    ]
    kernel, heads, tails, results = {
        "whole": (whole_kernel, [column, slab, slab], [], [slab, slab, column]),
        "begin": (begin_kernel, [column, slab, slab], [], [units, units, units, column]),
        "finish": (finish_kernel, [units, units, units], [slab, slab], [slab, slab]),
    }[stage]
    split = len(heads)
    return pl.pallas_call(
        functools.partial(kernel, groups),
        grid=(count // tile,),
        out_shape=[r[1] for r in results],
        in_specs=[h[0] for h in heads] + fixed + [t[0] for t in tails],
        out_specs=[r[0] for r in results],
        input_output_aliases={6: 0, 7: 1} if stage == "finish" else {},
        cost_estimate=pl.CostEstimate(
            flops=(12 if stage == "whole" else 6) * count * groups * width * hid,
            bytes_accessed=8 * count * groups * width,
            transcendentals=0 if stage == "finish" else count * hid,
        ),
        compiler_params=pltpu.CompilerParams(vmem_limit_bytes=60 << 20),
    )(*rows[:split], *weights, *rows[split:])


def local(tokens, grad_out, gates, expert_ids, gate_proj, up_proj, down_proj):
    rows, width = tokens.shape
    groups = lax.axis_size("etp")
    experts = lax.axis_size("ep")
    ring = experts // 2
    core = lax.rem(lax.axis_index("ep"), 2)
    depth = math.gcd(ring, 4)
    cols = ring // depth
    order = np.zeros(ring, np.int32)
    for pos in range(ring):
        x, t = pos // depth, pos % depth
        order[pos] = (t if x % 2 == 0 else depth - 1 - t) * cols + x
    inverse = np.argsort(order)
    count = ring * rows

    onehot = expert_ids[:, :, None] == jnp.arange(experts, dtype=jnp.int32)[None, None, :]
    table = jnp.sum(jnp.where(onehot, gates[:, :, None], 0.0), axis=1)
    mine = lax.all_to_all(table.T, "ep", split_axis=0, concat_axis=0, tiled=True)
    mine = mine.reshape(ring, 2, rows)
    mine = jnp.stack([mine[int(c)] for c in order]).transpose(1, 0, 2)
    mine = jnp.where(core == 0, mine, mine[::-1])

    flat = (groups, count, width)
    tok_own, tok_sib, grad_own, grad_sib = (
        a.reshape(flat) for a in gather(tokens, grad_out, ring, groups)
    )
    swap = [(i, i ^ 1) for i in range(experts)]
    weights = (gate_proj, up_proj, down_proj)
    *mids, score_own = expert("begin", flat, weights, mine[0].reshape(count, 1), tok_own, grad_own)
    out, inn, score_sib = expert("whole", flat, weights, mine[1].reshape(count, 1), tok_sib, grad_sib)
    got = (lax.ppermute(out, "ep", swap), lax.ppermute(inn, "ep", swap))
    out, inn = expert("finish", flat, weights, *mids, *got)
    scores = [score_own.reshape(ring, rows), score_sib.reshape(ring, rows)]
    shape = (groups, ring, 2, rows // 2, width)
    layer_out, token_grad = scatter(out.reshape(shape), inn.reshape(shape))

    score = jnp.stack(scores)
    score = jnp.where(core == 0, score, score[::-1]).transpose(1, 0, 2)
    score = jnp.stack([score[int(c)] for c in inverse]).reshape(experts, rows)
    score = lax.all_to_all(score, "ep", split_axis=0, concat_axis=0, tiled=True)
    score = lax.psum(score, "etp")
    picked = jnp.sum(jnp.where(onehot, score.T[:, None, :], 0.0), axis=2)
    return layer_out, token_grad, picked


class Stream:
    def __init__(self, ring, groups, slots, refs):
        self.ring, self.groups, self.slots = ring, groups, slots
        (
            self.tok_ref, self.grad_ref, self.gates, self.ids, self.gate_hbm, self.up_hbm, self.down_hbm,
            self.res_out, self.res_in, self.picked, self.inb, self.sib_in,
            self.gate_w, self.up_w, self.down_w, self.st, self.sst, self.r_out, self.r_in, self.y_in, self.y_out,
            self.table, self.gate_rows, self.score, self.score_in,
            self.local_sem, self.head_sem, self.hop_t, self.hop_g, self.fan_sem, self.sib_t, self.sib_g,
            self.sib_r, self.swap_sem, self.ring_o, self.ring_i, self.tail_sem, self.gate_sem, self.score_sem,
        ) = refs
        self.at = at = Place(ring, groups)
        self.g = at.g
        self.me = lax.axis_index("ep")
        self.sib = at.sibling()
        self.near = [at.chip(1), at.chip(-1)]
        self.half, self.width = self.st.shape[5], self.st.shape[6]
        self.mates = range(1, groups)
        self.others_first = [k % groups for k in range(1, groups + 1)]

    def hop_tok(self, d, s, src=None):
        src = self.inb.at[s, 0, self.g, 0, d] if src is None else src
        return remote(
            src, self.inb.at[s + 1, 0, self.g, 0, d], self.hop_t.at[0, d, s], self.hop_t.at[1, d, s], self.near[d]
        )

    def hop_grad(self, k, d, s, src=None):
        q = self.at.group(k)
        src = self.inb.at[s, 1, q, 0, d] if src is None else src
        return remote(
            src, self.inb.at[s + 1, 1, q, 0, d], self.hop_g.at[0, k, d, s], self.hop_g.at[1, k, d, s], self.near[d]
        )

    def head(self, j):
        return remote(
            self.grad_ref, self.inb.at[0, 1, self.g, 0], self.head_sem.at[0, j - 1], self.head_sem.at[1, j - 1],
            self.at.partner(j),
        )

    def fan(self, j, s):
        block = self.inb.at[s, 0, self.g, 0]
        return remote(block, block, self.fan_sem.at[0, j - 1, s], self.fan_sem.at[1, j - 1, s], self.at.partner(j))

    def sib_tok(self, k, s):
        q = self.at.group(k)
        return remote(
            self.inb.at[s, 0, q, 0], self.inb.at[s, 0, q, 1], self.sib_t.at[0, k, s], self.sib_t.at[1, k, s], self.sib
        )

    def sib_grad(self, s):
        return remote(self.inb.at[s, 1, :, 0], self.inb.at[s, 1, :, 1], self.sib_g.at[0, s], self.sib_g.at[1, s], self.sib)

    def sib_res(self, kind, slot, s):
        return remote(
            self.st.at[slot, kind, :, 1], self.sib_in.at[s, kind], self.sib_r.at[0, kind, s], self.sib_r.at[1, kind, s],
            self.sib,
        )

    def swap(self, j, slot, s):
        return remote(
            self.st.at[slot, 1, self.at.group(j), 0], self.y_in.at[s, j - 1], self.swap_sem.at[0, j - 1, s],
            self.swap_sem.at[1, j - 1, s], self.at.partner(j),
        )

    def send_out(self, k, d, slot, s):
        q = self.at.group(k)
        return remote(
            self.st.at[slot, 0, q, 0, d], self.r_out.at[s - 1, d, q], self.ring_o.at[0, k, d, s],
            self.ring_o.at[1, k, d, s], self.near[d],
        )

    def send_in(self, d, slot, s):
        return remote(
            self.st.at[slot, 1, self.g, 0, d], self.r_in.at[s - 1, d], self.ring_i.at[0, d, s], self.ring_i.at[1, d, s],
            self.near[d],
        )

    def tail(self, j):
        return remote(
            self.st.at[0, 0, self.at.group(j), 0], self.y_out.at[j - 1], self.tail_sem.at[0, j - 1],
            self.tail_sem.at[1, j - 1], self.at.partner(j),
        )

    def send_gate(self, e, row):
        return remote(
            self.table.at[e], self.gate_rows.at[row], self.gate_sem.at[0, e], self.gate_sem.at[1, row], (e, self.g)
        )

    def send_score(self, y, e, from_y, row):
        return remote(
            self.score.at[e], self.score_in.at[from_y, row], self.score_sem.at[0, y, e],
            self.score_sem.at[1, from_y, row], (e, y),
        )

    def slot_of(self, j):
        return jnp.where(j == 0, 0, 1 + lax.rem(j + self.slots - 2, self.slots - 1))

    def free(self, b):
        slot = self.slot_of(b)
        for kind in range(2):
            self.sib_res(kind, slot, b).wait_send()
        for j in self.mates:
            self.swap(j, slot, b).wait_send()
        for d in range(2):
            for k in range(self.groups):
                self.send_out(k, d, slot, b).wait_send()
            self.send_in(d, slot, b).wait_send()

    def greet_all(self):
        barrier = pltpu.get_barrier_semaphore()
        experts = 2 * self.ring

        @pl.loop(0, experts * self.groups)
        def _(i):
            e, y = i // self.groups, lax.rem(i, self.groups)

            @pl.when((e != self.me) | (y != self.g))
            def _():
                pl.semaphore_signal(barrier, inc=1, device_id=(e, y), device_id_type=MESH)

        pl.semaphore_wait(barrier, experts * self.groups - 1)

    def total(self, target, others, dest=None):
        dest = target if dest is None else dest

        @pl.loop(0, self.half // 16)
        def _(i):
            part = pl.ds(pl.multiple_of(i * 16, 16), 16)
            acc = target[part, :].astype(F32)
            for other in others:
                acc = acc + other[part, :].astype(F32)
            dest[part, :] = acc.astype(BF)

    def forward_tok(self, i):
        for d in range(2):
            self.hop_tok(d, i - 1).wait_recv()

            @pl.when(i < self.ring - 1)
            def _():
                self.hop_tok(d, i).start()

        for j in self.mates:
            self.fan(j, i).start()
        self.sib_tok(0, i).start()

    def forward_grad(self, k, i):
        for d in range(2):
            self.hop_grad(k, d, i - 1).wait_recv()

            @pl.when(i < self.ring - 1)
            def _():
                self.hop_grad(k, d, i).start()


def fused_kernel(ring, groups, slots, *refs):
    self = Stream(ring, groups, slots, refs)
    at, g, me, mates = self.at, self.g, self.me, self.mates
    st, sst, inb = self.st, self.sst, self.inb
    gate_w, up_w, down_w = self.gate_w, self.up_w, self.down_w
    half, width = self.half, self.width
    rows, experts = 4 * half, 2 * ring
    cuts = [slice(q * width, (q + 1) * width) for q in range(groups)]

    loads = [
        pltpu.make_async_copy(src.at[0], dst, self.local_sem.at[2 + k])
        for k, (src, dst) in enumerate([(self.gate_hbm, gate_w), (self.up_hbm, up_w), (self.down_hbm, down_w)])
    ]
    own_tok = pltpu.make_async_copy(self.tok_ref, inb.at[0, 0, g, 0], self.local_sem.at[0])
    own_grad = pltpu.make_async_copy(self.grad_ref, inb.at[0, 1, g, 0], self.local_sem.at[1])
    own_tok.start()
    own_grad.start()
    self.greet_all()
    for j in mates:
        self.head(j).start()
    for d in range(2):
        self.hop_tok(d, 0, self.tok_ref.at[d]).start()
    for d in range(2):
        self.hop_grad(0, d, 0, self.grad_ref.at[d]).start()
    own_tok.wait()
    for j in mates:
        self.fan(j, 0).start()
    self.sib_tok(0, 0).start()
    for load in loads:
        load.start()

    def iota(shape, axis):
        return lax.broadcasted_iota(jnp.int32, shape, axis)

    square = (2 * half, 2 * half)
    eye = iota(square, 0) == iota(square, 1)
    diag = [iota((half, 2 * half), 0) + d * half == iota((half, 2 * half), 1) for d in range(2)]

    def as_row(column, mask):
        return jnp.sum(jnp.where(mask, column, 0.0), axis=0, keepdims=True)

    def as_column(row, mask):
        return jnp.sum(jnp.where(mask, row, 0.0), axis=1, keepdims=True)

    @pl.loop(0, experts)
    def _(e):
        mine = jnp.where(self.ids[...] == e, self.gates[...], 0.0)
        self.table[e] = as_row(jnp.sum(mine, axis=1, keepdims=True), eye)
        self.score[e] = jnp.zeros((1, 2 * half), F32)

    @pl.loop(0, experts)
    def _(e):
        @pl.when(e != me)
        def _():
            self.send_gate(e, me).start()

    self.gate_rows[me] = self.table[me]
    own_grad.wait()
    for j in mates:
        self.head(j).wait_recv()
        for d in range(2):
            self.hop_grad(j, d, 0).start()
    self.sib_grad(0).start()

    self.forward_tok(1)
    for k in range(groups):
        self.forward_grad(k, 1)
    self.sib_grad(1).start()

    @pl.loop(0, experts)
    def _(e):
        @pl.when(e != me)
        def _():
            self.send_gate(e, e).wait_recv()

    for w in loads:
        w.wait()

    def finish_in(j):
        slot = self.slot_of(j)
        for k in mates:
            self.swap(k, slot, j).wait_recv()
        for d in range(2):
            target = st.at[slot, 1, g, 0, d]
            swapped = [self.y_in.at[j, k - 1, d] for k in mates]

            @pl.when(j > 1)
            def _():
                self.send_in(d, slot, j - 1).wait_recv()
                self.total(target, swapped + [self.r_in.at[j - 2, d]])

            @pl.when(j == 1)
            def _():
                self.total(target, swapped)

            self.send_in(d, slot, j).start()

    @pl.loop(2, ring + 2)
    def _(i):
        j = i - 2
        slot = self.slot_of(j)

        @pl.when(i < ring)
        def _():
            self.forward_tok(i)

        for k in mates:
            self.fan(k, j).wait_recv()
            self.sib_tok(k, j).start()

        @pl.when(j >= slots)
        def _():
            self.free(j - slots + 1)

        self.sib_grad(j).wait_recv()
        load_grad = pltpu.make_async_copy(inb.at[j, 1], st.at[slot, 1], self.local_sem.at[1])
        load_grad.start()
        for k in range(groups):
            self.sib_tok(k, j).wait_recv()
        load_tok = pltpu.make_async_copy(inb.at[j, 0], st.at[slot, 0], self.local_sem.at[0])
        load_tok.start()
        load_tok.wait()
        gate_pre = up_pre = raw = 0.0
        for q in range(groups):
            tok = st[slot, 0, q].reshape(rows, width)
            gate_pre = gate_pre + dot(tok, gate_w[cuts[q], :])
            up_pre = up_pre + dot(tok, up_w[cuts[q], :])

        @pl.when(i < ring)
        def _():
            self.forward_grad(0, i)

        load_grad.wait()
        for q in range(groups):
            raw = raw + dot_t(st[slot, 1, q].reshape(rows, width), down_w[:, cuts[q]])
        spots = [
            (at.chip(-j if d == 0 else j)[0] + c * (1 - 2 * at.core), d) for c in range(2) for d in range(2)
        ]
        gate = jnp.concatenate([as_column(self.gate_rows[e], diag[d]) for e, d in spots], axis=0)
        sig = jax.nn.sigmoid(gate_pre)
        act = gate_pre * sig
        hidden = act * up_pre
        marks = jnp.sum(hidden * raw, axis=1, keepdims=True)
        for k, (e, d) in enumerate(spots):
            self.score[e] = self.score[e] + as_row(marks[k * half : (k + 1) * half], diag[d])
        back = raw * gate
        gate_grad = (back * up_pre * sig * (1.0 + gate_pre * (1.0 - sig))).astype(BF)
        up_grad = (back * act).astype(BF)
        hidden = (hidden * gate).astype(BF)

        @pl.when(i < ring)
        def _():
            for k in mates:
                self.forward_grad(k, i)
            self.sib_grad(i).start()

        shape = (2, 2, half, width)
        for q in range(groups):
            st[slot, 0, q] = dot(hidden, down_w[:, cuts[q]]).astype(BF).reshape(shape)
        self.sib_res(0, slot, j).start()

        @pl.when(j > 1)
        def _():
            finish_in(j - 1)

        for q in range(groups):
            res = dot_t(gate_grad, gate_w[cuts[q], :]) + dot_t(up_grad, up_w[cuts[q], :])
            st[slot, 1, q] = res.astype(BF).reshape(shape)
        self.sib_res(1, slot, j).start()

        def fetch(kind):
            self.sib_res(kind, slot, j).wait_recv()
            load = pltpu.make_async_copy(self.sib_in.at[j, kind], sst.at[kind], self.local_sem.at[kind])
            load.start()
            return load

        fetched = fetch(0)
        fetched.wait()
        for k in self.others_first:
            q = at.group(k)
            for d in range(2):
                target, added = st.at[slot, 0, q, 0, d], sst.at[0, q, d]

                @pl.when(j > 1)
                def _():
                    self.send_out(k, d, slot, j - 1).wait_recv()
                    self.total(target, [added, self.r_out.at[j - 2, d, q]])

                @pl.when(j <= 1)
                def _():
                    self.total(target, [added])

                @pl.when(j > 0)
                def _():
                    self.send_out(k, d, slot, j).start()

        fetched = fetch(1)
        fetched.wait()
        for k in self.others_first:
            q = at.group(k)
            for d in range(2):
                self.total(st.at[slot, 1, q, 0, d], [sst.at[1, q, d]])
            if k > 0:
                self.swap(k, slot, j).start()

    @pl.loop(0, experts * groups)
    def _(n):
        e, y = n // groups, lax.rem(n, groups)

        @pl.when((e != me) | (y != g))
        def _():
            self.send_score(y, e, g, me).start()

    self.score_in[g, me] = self.score[me]
    finish_in(jnp.int32(ring - 1))

    for k in self.others_first:
        q = at.group(k)
        for d in range(2):
            self.send_out(k, d, 0, ring - 1).wait_recv()
            self.total(st.at[0, 0, q, 0, d], [self.r_out.at[ring - 2, d, q]])
        if k > 0:
            self.tail(k).start()
    for j in mates:
        self.swap(j, 0, 0).wait_recv()

    @pl.loop(0, experts * groups)
    def _(n):
        e, y = n // groups, lax.rem(n, groups)

        @pl.when((e != me) | (y != g))
        def _():
            self.send_score(y, e, y, e).wait_recv()

    self.picked[...] = jnp.zeros_like(self.picked)

    @pl.loop(0, experts)
    def _(e):
        row = self.score_in[0, e]
        for y in range(1, groups):
            row = row + self.score_in[y, e]
        self.picked[...] += jnp.where(self.ids[...] == e, as_column(row, eye), 0.0)

    for d in range(2):
        self.send_in(d, 0, ring - 1).wait_recv()
        self.total(
            st.at[0, 1, g, 0, d],
            [self.y_in.at[0, j - 1, d] for j in mates] + [self.r_in.at[ring - 2, d]],
            self.res_in.at[d],
        )
    for j in mates:
        self.tail(j).wait_recv()
    for d in range(2):
        self.total(st.at[0, 0, g, 0, d], [self.y_out.at[j - 1, d] for j in mates], self.res_out.at[d])

    for kind in range(2):
        self.sib_res(kind, 0, 0).wait_send()
    for j in mates:
        self.swap(j, 0, 0).wait_send()
        self.head(j).wait_send()
        self.tail(j).wait_send()

    @pl.loop(max(1, ring - slots + 1), ring)
    def _(b):
        self.free(b)

    @pl.loop(0, ring)
    def _(s):
        for j in mates:
            self.fan(j, s).wait_send()
        for k in range(groups):
            self.sib_tok(k, s).wait_send()
        self.sib_grad(s).wait_send()

        @pl.when(s < ring - 1)
        def _():
            for d in range(2):
                self.hop_tok(d, s).wait_send()
                for k in range(groups):
                    self.hop_grad(k, d, s).wait_send()

    @pl.loop(0, experts * groups)
    def _(n):
        e, y = n // groups, lax.rem(n, groups)

        @pl.when((e != me) | (y != g))
        def _():
            self.send_score(y, e, g, me).wait_send()

        @pl.when((e != me) & (y == 0))
        def _():
            self.send_gate(e, me).wait_send()


SLOTS = 4


def streamed(tokens, grad_out, gates, expert_ids, gate_proj, up_proj, down_proj):
    rows, width = tokens.shape
    groups = lax.axis_size("etp")
    experts = lax.axis_size("ep")
    ring = experts // 2
    half = rows // 2
    weights = (gate_proj, up_proj, down_proj)
    depth, hid = gate_proj.shape[1:]
    res = jax.ShapeDtypeStruct((2, half, width), BF)
    block = (2, groups, 2, 2, half, width)
    dma = pltpu.SemaphoreType.DMA
    hbm = pl.BlockSpec(memory_space=pltpu.HBM)
    vmem = pl.BlockSpec(memory_space=pltpu.VMEM)
    mates = groups - 1
    count = experts * rows
    outs = pl.pallas_call(
        functools.partial(fused_kernel, ring, groups, SLOTS),
        out_shape=(
            res,
            res,
            jax.ShapeDtypeStruct(gates.shape, F32),
            jax.ShapeDtypeStruct((ring,) + block, BF),
            jax.ShapeDtypeStruct((ring, 2, groups, 2, half, width), BF),
        ),
        in_specs=[hbm, hbm, vmem, vmem, hbm, hbm, hbm],
        out_specs=(vmem, vmem, vmem, hbm, hbm),
        scratch_shapes=[
            pltpu.VMEM((depth, hid), BF),
            pltpu.VMEM((depth, hid), BF),
            pltpu.VMEM((hid, depth), BF),
            pltpu.VMEM((SLOTS,) + block, BF),
            pltpu.VMEM((2, groups, 2, half, width), BF),
            pltpu.VMEM((ring - 1, 2, groups, half, width), BF),
            pltpu.VMEM((ring - 1, 2, half, width), BF),
            pltpu.VMEM((ring, mates, 2, half, width), BF),
            pltpu.VMEM((mates, 2, half, width), BF),
            pltpu.VMEM((experts, 1, rows), F32),
            pltpu.VMEM((experts, 1, rows), F32),
            pltpu.VMEM((experts, 1, rows), F32),
            pltpu.VMEM((groups, experts, 1, rows), F32),
            dma((5,)),
            dma((2, mates)),
            dma((2, 2, ring)),
            dma((2, groups, 2, ring)),
            dma((2, mates, ring)),
            dma((2, groups, ring)),
            dma((2, ring)),
            dma((2, 2, ring)),
            dma((2, mates, ring)),
            dma((2, groups, 2, ring)),
            dma((2, 2, ring)),
            dma((2, mates)),
            dma((2, experts)),
            dma((2, groups, experts)),
        ],
        cost_estimate=pl.CostEstimate(
            flops=12 * count * groups * width * hid,
            bytes_accessed=16 * count * groups * width,
            transcendentals=count * hid,
        ),
        compiler_params=pltpu.CompilerParams(
            collective_id=2, has_side_effects=True, vmem_limit_bytes=63 << 20
        ),
    )(tokens.reshape(2, half, width), grad_out.reshape(2, half, width), gates, expert_ids, *weights)
    return outs[0].reshape(rows, width), outs[1].reshape(rows, width), outs[2]


def solution(mesh):
    in_specs = (
        P("ep", "etp"),
        P("ep", "etp"),
        P("ep", None),
        P("ep", None),
        P("ep", None, "etp"),
        P("ep", None, "etp"),
        P("ep", "etp", None),
    )
    out_specs = (P("ep", "etp"), P("ep", "etp"), P("ep", None))
    body = streamed if mesh.shape["ep"] <= 16 else local
    return jax.shard_map(body, mesh=mesh, in_specs=in_specs, out_specs=out_specs, check_vma=False)
```

```python
import functools
import math

import jax
import jax.numpy as jnp
import numpy as np
from jax import lax
from jax.experimental import pallas as pl
from jax.experimental.pallas import tpu as pltpu
from jax.sharding import PartitionSpec as P

BF = jnp.bfloat16
F32 = jnp.float32
MESH = pl.DeviceIdType.MESH


class Place:
    def __init__(self, ring, groups):
        self.ring, self.groups = ring, groups
        self.depth = math.gcd(ring, 4)
        self.cols = ring // self.depth
        me = lax.axis_index("ep")
        self.g = lax.axis_index("etp")
        self.core = lax.rem(me, 2)
        chip = me // 2
        x, z = lax.rem(chip, self.cols), chip // self.cols
        self.p = x * self.depth + z + lax.rem(x, 2) * (self.depth - 1 - 2 * z)

    def at(self, offset):
        return lax.rem(self.p + offset + self.ring, self.ring)

    def chip(self, offset):
        pos = self.at(offset)
        x, t = pos // self.depth, lax.rem(pos, self.depth)
        z = t + lax.rem(x, 2) * (self.depth - 1 - 2 * t)
        return ((z * self.cols + x) * 2 + self.core, self.g)

    def sibling(self):
        return (lax.axis_index("ep") + 1 - 2 * self.core, self.g)

    def group(self, j):
        return lax.rem(self.g + j, self.groups)

    def partner(self, j):
        return (lax.axis_index("ep"), self.group(j))

    def greet(self, with_sibling):
        barrier = pltpu.get_barrier_semaphore()
        others = [self.chip(1), self.chip(-1)] + [self.partner(j) for j in range(1, self.groups)]
        if with_sibling:
            others.append(self.sibling())
        for other in others:
            pl.semaphore_signal(barrier, inc=1, device_id=other, device_id_type=MESH)
        pl.semaphore_wait(barrier, len(others))


def remote(src, dst, send, recv, where):
    return pltpu.make_async_remote_copy(
        src_ref=src, dst_ref=dst, send_sem=send, recv_sem=recv, device_id=where, device_id_type=MESH
    )


def gather_kernel(
    ring, groups, tok_ref, grad_ref, tok, tok_sib, grad, grad_sib, local_sem, first, rings, fans, late
):
    at = Place(ring, groups)
    at.greet(True)
    g = at.g
    sib = at.sibling()
    own_tok = pltpu.make_async_copy(tok_ref, tok.at[g, at.p], local_sem.at[0])
    own_grad = pltpu.make_async_copy(grad_ref, grad.at[g, at.p], local_sem.at[1])
    own_tok.start()
    own_grad.start()
    heads = []
    for j in range(1, groups):
        head = remote(
            grad_ref, grad.at[g, at.p], first.at[0, j - 1], first.at[1, j - 1], at.partner(j)
        )
        head.start()
        heads.append(head)
    own_tok.wait()

    def back(d, s):
        return at.at(-s if d == 0 else s)

    fan_y, fan_s, fan_t = {}, {}, {}

    def fan_tok(s):
        for d in range(2):
            b = back(d, s)
            fan_y[s, d] = []
            for j in range(1, groups):
                c = remote(
                    tok.at[g, b, d],
                    tok.at[g, b, d],
                    fans.at[0, j, d, s],
                    fans.at[1, j, d, s],
                    at.partner(j),
                )
                c.start()
                fan_y[s, d].append(c)

    def fan_grad(s):
        for d in range(2):
            b = back(d, s)
            c = remote(
                grad.at[:, b, d], grad_sib.at[:, b, d], fans.at[0, 0, d, s], fans.at[1, 0, d, s], sib
            )
            c.start()
            fan_s[s, d] = c

    def fan_late(s):
        for d in range(2):
            b = back(d, s)
            for c in fan_y[s, d]:
                c.wait_recv()
            c = remote(tok.at[:, b, d], tok_sib.at[:, b, d], late.at[0, d, s], late.at[1, d, s], sib)
            c.start()
            fan_t[s, d] = c

    hops = {}

    def hop(kind, d, s):
        b = back(d, s - 1)
        block = tok.at[g, b, d] if kind == 0 else grad.at[:, b, d]
        if s > 1:
            hops[kind, d, s - 1].wait_recv()
        if s < ring:
            c = remote(
                block,
                block,
                rings.at[0, kind, d, s - 1],
                rings.at[1, kind, d, s - 1],
                at.chip(1 if d == 0 else -1),
            )
            c.start()
            hops[kind, d, s] = c

    for s in range(1, ring + 1):
        hop(0, 0, s)
        hop(0, 1, s)
        if s == 1:
            own_grad.wait()
            for head in heads:
                head.wait_recv()
        if s < ring:
            fan_tok(s - 1)
        hop(1, 0, s)
        hop(1, 1, s)
        if s < ring:
            fan_grad(s - 1)
        if s >= 2:
            fan_late(s - 2)
    fan_tok(ring - 1)
    fan_grad(ring - 1)
    fan_late(ring - 1)
    for c in list(fan_s.values()) + list(fan_t.values()):
        c.wait()
    for group in fan_y.values():
        for c in group:
            c.wait_send()
    for c in list(hops.values()) + heads:
        c.wait_send()


def gather(tokens, grad_out, ring, groups):
    rows, width = tokens.shape
    half = rows // 2
    full = jax.ShapeDtypeStruct((groups, ring, 2, half, width), BF)
    dma = pltpu.SemaphoreType.DMA
    hbm = pl.BlockSpec(memory_space=pltpu.HBM)
    return pl.pallas_call(
        functools.partial(gather_kernel, ring, groups),
        out_shape=(full,) * 4,
        in_specs=[hbm, hbm],
        out_specs=(hbm,) * 4,
        scratch_shapes=[
            dma((2,)),
            dma((2, groups - 1)),
            dma((2, 2, 2, ring - 1)),
            dma((2, groups, 2, ring)),
            dma((2, 2, ring)),
        ],
        compiler_params=pltpu.CompilerParams(collective_id=0, has_side_effects=True),
    )(tokens.reshape(2, half, width), grad_out.reshape(2, half, width))


def scatter_kernel(
    ring, groups, s_out, s_in, res_out, res_in, v_out, v_in, r_out, r_in, y_in, y_out, loads, rings, ys, tail
):
    at = Place(ring, groups)
    g = at.g
    half = v_in.shape[2]

    def dest(d, s):
        return at.at(-s if d == 0 else s)

    load_out, load_in, swap = {}, {}, {}
    for s in range(1, ring + 1):
        for d in range(2):
            b = dest(d, s)
            load_out[s, d] = pltpu.make_async_copy(
                s_out.at[:, b, d], v_out.at[:, b, d], loads.at[0, d, s - 1]
            )
            load_in[s, d] = pltpu.make_async_copy(s_in.at[g, b, d], v_in.at[b, d], loads.at[1, d, s - 1])
            load_out[s, d].start()
            load_in[s, d].start()
    at.greet(False)
    for s in range(1, ring + 1):
        for d in range(2):
            b = dest(d, s)
            swap[s, d] = []
            for j in range(1, groups):
                c = remote(
                    s_in.at[at.group(j), b, d],
                    y_in.at[j - 1, b, d],
                    ys.at[0, j - 1, d, s - 1],
                    ys.at[1, j - 1, d, s - 1],
                    at.partner(j),
                )
                c.start()
                swap[s, d].append(c)

    def total(target, others):
        @pl.loop(0, half // 16)
        def _(i):
            rows = pl.ds(pl.multiple_of(i * 16, 16), 16)
            acc = target[rows, :].astype(F32)
            for other in others:
                acc = acc + other[rows, :].astype(F32)
            target[rows, :] = acc.astype(BF)

    hop_out, hop_in = {}, {}
    for s in range(1, ring + 1):
        for d in range(2):
            b = dest(d, s)
            load_out[s, d].wait()
            if s > 1:
                hop_out[s - 1, d].wait_recv()
                for q in range(groups):
                    total(v_out.at[q, b, d], [r_out.at[d, s - 2, q]])
            if s < ring:
                c = remote(
                    v_out.at[:, b, d],
                    r_out.at[d, s - 1],
                    rings.at[0, 0, d, s - 1],
                    rings.at[1, 0, d, s - 1],
                    at.chip(1 if d == 0 else -1),
                )
                c.start()
                hop_out[s, d] = c
        if s == ring:
            ends = []
            for d in range(2):
                for j in range(1, groups):
                    c = remote(
                        v_out.at[at.group(j), at.p, d],
                        y_out.at[j - 1, d],
                        tail.at[0, j - 1, d],
                        tail.at[1, j - 1, d],
                        at.partner(j),
                    )
                    c.start()
                    ends.append(c)
        for d in range(2):
            b = dest(d, s)
            load_in[s, d].wait()
            others = []
            for c in swap[s, d]:
                c.wait_recv()
            others = [y_in.at[j - 1, b, d] for j in range(1, groups)]
            if s > 1:
                hop_in[s - 1, d].wait_recv()
                others.append(r_in.at[d, s - 2])
            total(v_in.at[b, d], others)
            if s < ring:
                c = remote(
                    v_in.at[b, d],
                    r_in.at[d, s - 1],
                    rings.at[0, 1, d, s - 1],
                    rings.at[1, 1, d, s - 1],
                    at.chip(1 if d == 0 else -1),
                )
                c.start()
                hop_in[s, d] = c
    for d in range(2):
        res_in[d] = v_in[at.p, d]
    for c in ends:
        c.wait_recv()
    for d in range(2):
        total(v_out.at[g, at.p, d], [y_out.at[j - 1, d] for j in range(1, groups)])
        res_out[d] = v_out[g, at.p, d]
    for c in list(hop_out.values()) + list(hop_in.values()) + ends:
        c.wait_send()
    for group in swap.values():
        for c in group:
            c.wait_send()


def scatter(s_out, s_in):
    groups, ring, _, half, width = s_out.shape
    res = jax.ShapeDtypeStruct((2, half, width), BF)
    dma = pltpu.SemaphoreType.DMA
    hbm = pl.BlockSpec(memory_space=pltpu.HBM)
    vmem = pl.BlockSpec(memory_space=pltpu.VMEM)
    out, inn = pl.pallas_call(
        functools.partial(scatter_kernel, ring, groups),
        out_shape=(res, res),
        in_specs=[hbm, hbm],
        out_specs=(vmem, vmem),
        scratch_shapes=[
            pltpu.VMEM((groups, ring, 2, half, width), BF),
            pltpu.VMEM((ring, 2, half, width), BF),
            pltpu.VMEM((2, ring - 1, groups, half, width), BF),
            pltpu.VMEM((2, ring - 1, half, width), BF),
            pltpu.VMEM((groups - 1, ring, 2, half, width), BF),
            pltpu.VMEM((groups - 1, 2, half, width), BF),
            dma((2, 2, ring)),
            dma((2, 2, 2, ring - 1)),
            dma((2, groups - 1, 2, ring)),
            dma((2, groups - 1, 2)),
        ],
        compiler_params=pltpu.CompilerParams(
            collective_id=1, has_side_effects=True, vmem_limit_bytes=60 << 20
        ),
    )(s_out, s_in)
    return out.reshape(2 * half, width), inn.reshape(2 * half, width)


def dot(a, b):
    return lax.dot_general(a, b, (((1,), (0,)), ((), ())), preferred_element_type=F32)


def dot_t(a, b):
    return lax.dot_general(a, b, (((1,), (1,)), ((), ())), preferred_element_type=F32)


def first_half(groups, gate_ref, tok, grad, gate_w, up_w, down_w, score):
    width = tok.shape[2]
    cuts = [slice(g * width, (g + 1) * width) for g in range(groups)]
    gate_pre = sum(dot(tok[g], gate_w[cuts[g], :]) for g in range(groups))
    up_pre = sum(dot(tok[g], up_w[cuts[g], :]) for g in range(groups))
    raw = sum(dot_t(grad[g], down_w[:, cuts[g]]) for g in range(groups))
    gate = gate_ref[...]
    sig = jax.nn.sigmoid(gate_pre)
    act = gate_pre * sig
    hidden = act * up_pre
    score[...] = jnp.sum(hidden * raw, axis=1, keepdims=True)
    back = raw * gate
    gate_grad = back * up_pre * sig * (1.0 + gate_pre * (1.0 - sig))
    return (hidden * gate).astype(BF), gate_grad.astype(BF), (back * act).astype(BF)


def second_half(groups, hidden, gate_grad, up_grad, gate_w, up_w, down_w, out, inn, add=None):
    width = out.shape[2]
    for g in range(groups):
        cut = slice(g * width, (g + 1) * width)
        res = dot(hidden, down_w[:, cut])
        if add:
            res = res + add[0][g].astype(F32)
        out[g] = res.astype(BF)
        res = dot_t(gate_grad, gate_w[cut, :]) + dot_t(up_grad, up_w[cut, :])
        if add:
            res = res + add[1][g].astype(F32)
        inn[g] = res.astype(BF)


def whole_kernel(groups, gate, tok, grad, gate_w, up_w, down_w, out, inn, score):
    mids = first_half(groups, gate, tok, grad, gate_w, up_w, down_w, score)
    second_half(groups, *mids, gate_w, up_w, down_w, out, inn)


def begin_kernel(groups, gate, tok, grad, gate_w, up_w, down_w, hidden, gate_grad, up_grad, score):
    mids = first_half(groups, gate, tok, grad, gate_w, up_w, down_w, score)
    hidden[...], gate_grad[...], up_grad[...] = mids


def finish_kernel(groups, hidden, gate_grad, up_grad, gate_w, up_w, down_w, add_out, add_in, out, inn):
    second_half(
        groups,
        hidden[...],
        gate_grad[...],
        up_grad[...],
        gate_w,
        up_w,
        down_w,
        out,
        inn,
        (add_out, add_in),
    )


def expert(stage, shape, weights, *rows):
    groups, count, width = shape
    hid = weights[0].shape[2]
    tile = 256
    slab = (pl.BlockSpec((groups, tile, width), lambda i: (0, i, 0)), jax.ShapeDtypeStruct(shape, BF))
    column = (pl.BlockSpec((tile, 1), lambda i: (i, 0)), jax.ShapeDtypeStruct((count, 1), F32))
    units = (pl.BlockSpec((tile, hid), lambda i: (i, 0)), jax.ShapeDtypeStruct((count, hid), BF))
    fixed = [
        pl.BlockSpec((None,) + w.shape[1:], lambda i: (0, 0, 0), pipeline_mode=pl.Buffered(1))
        for w in weights
    ]
    kernel, heads, tails, results = {
        "whole": (whole_kernel, [column, slab, slab], [], [slab, slab, column]),
        "begin": (begin_kernel, [column, slab, slab], [], [units, units, units, column]),
        "finish": (finish_kernel, [units, units, units], [slab, slab], [slab, slab]),
    }[stage]
    split = len(heads)
    return pl.pallas_call(
        functools.partial(kernel, groups),
        grid=(count // tile,),
        out_shape=[r[1] for r in results],
        in_specs=[h[0] for h in heads] + fixed + [t[0] for t in tails],
        out_specs=[r[0] for r in results],
        input_output_aliases={6: 0, 7: 1} if stage == "finish" else {},
        cost_estimate=pl.CostEstimate(
            flops=(12 if stage == "whole" else 6) * count * groups * width * hid,
            bytes_accessed=8 * count * groups * width,
            transcendentals=0 if stage == "finish" else count * hid,
        ),
        compiler_params=pltpu.CompilerParams(vmem_limit_bytes=60 << 20),
    )(*rows[:split], *weights, *rows[split:])


def local(tokens, grad_out, gates, expert_ids, gate_proj, up_proj, down_proj):
    rows, width = tokens.shape
    groups = lax.axis_size("etp")
    experts = lax.axis_size("ep")
    ring = experts // 2
    core = lax.rem(lax.axis_index("ep"), 2)
    depth = math.gcd(ring, 4)
    cols = ring // depth
    order = np.zeros(ring, np.int32)
    for pos in range(ring):
        x, t = pos // depth, pos % depth
        order[pos] = (t if x % 2 == 0 else depth - 1 - t) * cols + x
    inverse = np.argsort(order)
    count = ring * rows

    onehot = expert_ids[:, :, None] == jnp.arange(experts, dtype=jnp.int32)[None, None, :]
    table = jnp.sum(jnp.where(onehot, gates[:, :, None], 0.0), axis=1)
    mine = lax.all_to_all(table.T, "ep", split_axis=0, concat_axis=0, tiled=True)
    mine = mine.reshape(ring, 2, rows)
    mine = jnp.stack([mine[int(c)] for c in order]).transpose(1, 0, 2)
    mine = jnp.where(core == 0, mine, mine[::-1])

    flat = (groups, count, width)
    tok_own, tok_sib, grad_own, grad_sib = (
        a.reshape(flat) for a in gather(tokens, grad_out, ring, groups)
    )
    swap = [(i, i ^ 1) for i in range(experts)]
    weights = (gate_proj, up_proj, down_proj)
    *mids, score_own = expert("begin", flat, weights, mine[0].reshape(count, 1), tok_own, grad_own)
    out, inn, score_sib = expert("whole", flat, weights, mine[1].reshape(count, 1), tok_sib, grad_sib)
    got = (lax.ppermute(out, "ep", swap), lax.ppermute(inn, "ep", swap))
    out, inn = expert("finish", flat, weights, *mids, *got)
    scores = [score_own.reshape(ring, rows), score_sib.reshape(ring, rows)]
    shape = (groups, ring, 2, rows // 2, width)
    layer_out, token_grad = scatter(out.reshape(shape), inn.reshape(shape))

    score = jnp.stack(scores)
    score = jnp.where(core == 0, score, score[::-1]).transpose(1, 0, 2)
    score = jnp.stack([score[int(c)] for c in inverse]).reshape(experts, rows)
    score = lax.all_to_all(score, "ep", split_axis=0, concat_axis=0, tiled=True)
    score = lax.psum(score, "etp")
    picked = jnp.sum(jnp.where(onehot, score.T[:, None, :], 0.0), axis=2)
    return layer_out, token_grad, picked


class Stream:
    def __init__(self, ring, groups, slots, refs):
        self.ring, self.groups, self.slots = ring, groups, slots
        (
            self.tok_ref, self.grad_ref, self.gates, self.ids, self.gate_hbm, self.up_hbm, self.down_hbm,
            self.res_out, self.res_in, self.picked, self.inb, self.sib_in,
            self.gate_w, self.up_w, self.down_w, self.st, self.sst, self.r_out, self.r_in, self.y_in, self.y_out,
            self.table, self.gate_rows, self.score, self.score_in,
            self.local_sem, self.head_sem, self.hop_t, self.hop_g, self.fan_sem, self.sib_g,
            self.sib_r, self.swap_sem, self.ring_o, self.ring_i, self.tail_sem, self.gate_sem, self.score_sem,
        ) = refs
        self.at = at = Place(ring, groups)
        self.g = at.g
        self.me = lax.axis_index("ep")
        self.sib = at.sibling()
        self.near = [at.chip(1), at.chip(-1)]
        self.half, self.width = self.st.shape[5], self.st.shape[6]
        self.mates = range(1, groups)
        self.others_first = [k % groups for k in range(1, groups + 1)]

    def hop_tok(self, d, s, src=None):
        src = self.inb.at[s, 0, self.g, 0, d] if src is None else src
        return remote(
            src, self.inb.at[s + 1, 0, self.g, 0, d], self.hop_t.at[0, d, s], self.hop_t.at[1, d, s], self.near[d]
        )

    def hop_grad(self, k, d, s, src=None):
        q = self.at.group(k)
        src = self.inb.at[s, 1, q, 0, d] if src is None else src
        return remote(
            src, self.inb.at[s + 1, 1, q, 0, d], self.hop_g.at[0, k, d, s], self.hop_g.at[1, k, d, s], self.near[d]
        )

    def head(self, j):
        return remote(
            self.grad_ref, self.inb.at[0, 1, self.g, 0], self.head_sem.at[0, j - 1], self.head_sem.at[1, j - 1],
            self.at.partner(j),
        )

    def fan(self, j, s, src=None):
        block = self.inb.at[s, 0, self.g, 0]
        src = block if src is None else src
        return remote(src, block, self.fan_sem.at[0, j - 1, s], self.fan_sem.at[1, j - 1, s], self.at.partner(j))

    def sib_copy(self, kind, k, s, src=None):
        q = self.at.group(k)
        src = self.inb.at[s, kind, q, 0] if src is None else src
        return remote(
            src, self.inb.at[s, kind, q, 1], self.sib_g.at[0, kind, k, s], self.sib_g.at[1, kind, k, s], self.sib
        )

    def sib_res(self, kind, slot, s):
        return remote(
            self.st.at[slot, kind, :, 1], self.sib_in.at[s, kind], self.sib_r.at[0, kind, s], self.sib_r.at[1, kind, s],
            self.sib,
        )

    def swap(self, j, slot, s):
        return remote(
            self.st.at[slot, 1, self.at.group(j), 0], self.y_in.at[s, j - 1], self.swap_sem.at[0, j - 1, s],
            self.swap_sem.at[1, j - 1, s], self.at.partner(j),
        )

    def send_out(self, k, d, slot, s):
        q = self.at.group(k)
        return remote(
            self.st.at[slot, 0, q, 0, d], self.r_out.at[s - 1, d, q], self.ring_o.at[0, k, d, s],
            self.ring_o.at[1, k, d, s], self.near[d],
        )

    def send_in(self, d, slot, s):
        return remote(
            self.st.at[slot, 1, self.g, 0, d], self.r_in.at[s - 1, d], self.ring_i.at[0, d, s], self.ring_i.at[1, d, s],
            self.near[d],
        )

    def tail(self, j):
        return remote(
            self.st.at[0, 0, self.at.group(j), 0], self.y_out.at[j - 1], self.tail_sem.at[0, j - 1],
            self.tail_sem.at[1, j - 1], self.at.partner(j),
        )

    def send_gate(self, e, row):
        return remote(
            self.table.at[e], self.gate_rows.at[row], self.gate_sem.at[0, e], self.gate_sem.at[1, row], (e, self.g)
        )

    def send_score(self, y, e, from_y, row):
        return remote(
            self.score.at[e], self.score_in.at[from_y, row], self.score_sem.at[0, y, e],
            self.score_sem.at[1, from_y, row], (e, y),
        )

    def slot_of(self, j):
        return jnp.where(j == 0, 0, 1 + lax.rem(j + self.slots - 2, self.slots - 1))

    def free(self, b):
        slot = self.slot_of(b)
        for kind in range(2):
            self.sib_res(kind, slot, b).wait_send()
        for j in self.mates:
            self.swap(j, slot, b).wait_send()
        for d in range(2):
            for k in range(self.groups):
                self.send_out(k, d, slot, b).wait_send()
            self.send_in(d, slot, b).wait_send()

    def greet_all(self):
        barrier = pltpu.get_barrier_semaphore()
        experts = 2 * self.ring

        @pl.loop(0, experts * self.groups)
        def _(i):
            e, y = i // self.groups, lax.rem(i, self.groups)

            @pl.when((e != self.me) | (y != self.g))
            def _():
                pl.semaphore_signal(barrier, inc=1, device_id=(e, y), device_id_type=MESH)

        pl.semaphore_wait(barrier, experts * self.groups - 1)

    def total(self, target, others, dest=None):
        dest = target if dest is None else dest

        @pl.loop(0, self.half // 16)
        def _(i):
            part = pl.ds(pl.multiple_of(i * 16, 16), 16)
            acc = target[part, :].astype(F32)
            for other in others:
                acc = acc + other[part, :].astype(F32)
            dest[part, :] = acc.astype(BF)

    def forward_tok(self, i):
        for d in range(2):
            self.hop_tok(d, i - 1).wait_recv()

            @pl.when(i < self.ring - 1)
            def _():
                self.hop_tok(d, i).start()

        for j in self.mates:
            self.fan(j, i).start()
        self.sib_copy(0, 0, i).start()

    def forward_grad(self, k, i):
        for d in range(2):
            self.hop_grad(k, d, i - 1).wait_recv()

            @pl.when(i < self.ring - 1)
            def _():
                self.hop_grad(k, d, i).start()

        self.sib_copy(1, k, i).start()


def fused_kernel(ring, groups, slots, *refs):
    self = Stream(ring, groups, slots, refs)
    at, g, me, mates = self.at, self.g, self.me, self.mates
    st, sst, inb = self.st, self.sst, self.inb
    gate_w, up_w, down_w = self.gate_w, self.up_w, self.down_w
    half, width = self.half, self.width
    rows, experts = 4 * half, 2 * ring
    lag, pause = slots - 3, min(3, ring - 2)
    cuts = [slice(q * width, (q + 1) * width) for q in range(groups)]

    loads = [
        pltpu.make_async_copy(src.at[0], dst, self.local_sem.at[2 + k])
        for k, (src, dst) in enumerate([(self.gate_hbm, gate_w), (self.up_hbm, up_w), (self.down_hbm, down_w)])
    ]
    self.greet_all()
    for j in mates:
        self.head(j).start()
    for d in range(2):
        self.hop_tok(d, 0, self.tok_ref.at[d]).start()
    for d in range(2):
        self.hop_grad(0, d, 0, self.grad_ref.at[d]).start()
    self.sib_copy(0, 0, 0, self.tok_ref).start()
    self.sib_copy(1, 0, 0, self.grad_ref).start()
    for load in loads:
        load.start()

    def iota(shape, axis):
        return lax.broadcasted_iota(jnp.int32, shape, axis)

    diag = [iota((half, 2 * half), 0) + d * half == iota((half, 2 * half), 1) for d in range(2)]

    def as_row(column, mask):
        return jnp.sum(jnp.where(mask, column, 0.0), axis=0, keepdims=True)

    def as_column(row, mask):
        return jnp.sum(jnp.where(mask, row, 0.0), axis=1, keepdims=True)

    @pl.loop(0, experts)
    def _(e):
        mine = jnp.where(self.ids[...] == e, self.gates[...], 0.0)
        self.table[e] = jnp.sum(mine, axis=0, keepdims=True)
        self.score[e] = jnp.zeros((1, 2 * half), F32)

    @pl.loop(0, experts)
    def _(e):
        @pl.when(e != me)
        def _():
            self.send_gate(e, me).start()

    self.gate_rows[me] = self.table[me]
    self.forward_tok(1)
    for j in mates:
        self.fan(j, 0, self.tok_ref).start()
    for j in mates:
        self.head(j).wait_recv()
        for d in range(2):
            self.hop_grad(j, d, 0).start()
        self.sib_copy(1, j, 0).start()

    for k in range(groups):
        self.forward_grad(k, 1)

    @pl.loop(0, experts)
    def _(e):
        @pl.when(e != me)
        def _():
            self.send_gate(e, e).wait_recv()

    for w in loads:
        w.wait()

    def finish_in(j):
        slot = self.slot_of(j)
        for k in mates:
            self.swap(k, slot, j).wait_recv()
        for d in range(2):
            target = st.at[slot, 1, g, 0, d]
            swapped = [self.y_in.at[j, k - 1, d] for k in mates]

            @pl.when(j > 1)
            def _():
                self.send_in(d, slot, j - 1).wait_recv()
                self.total(target, swapped + [self.r_in.at[j - 2, d]])

            @pl.when(j == 1)
            def _():
                self.total(target, swapped)

            self.send_in(d, slot, j).start()

    def fetch(kind, j):
        self.sib_res(kind, self.slot_of(j), j).wait_recv()
        load = pltpu.make_async_copy(self.sib_in.at[j, kind], sst.at[kind], self.local_sem.at[kind])
        load.start()
        load.wait()

    def begin_in(j):
        slot = self.slot_of(j)
        fetch(1, j)
        for k in self.others_first:
            q = at.group(k)
            for d in range(2):
                self.total(st.at[slot, 1, q, 0, d], [sst.at[1, q, d]])
            if k > 0:
                self.swap(k, slot, j).start()

    def send_block(j):
        slot = self.slot_of(j)
        fetch(0, j)
        for k in self.others_first:
            q = at.group(k)
            for d in range(2):
                target, added = st.at[slot, 0, q, 0, d], sst.at[0, q, d]

                @pl.when(j > 1)
                def _():
                    self.send_out(k, d, slot, j - 1).wait_recv()
                    self.total(target, [added, self.r_out.at[j - 2, d, q]])

                @pl.when(j == 1)
                def _():
                    self.total(target, [added])

                self.send_out(k, d, slot, j).start()

    def block_at(n):
        return jnp.where(n < pause, n + 1, jnp.where(n == pause, 0, n))

    @pl.loop(0, ring)
    def _(n):
        j = block_at(n)
        i = j + 1
        slot = self.slot_of(j)
        gather_on = (j > 0) & (i < ring)

        @pl.when(gather_on)
        def _():
            self.forward_tok(i)

        @pl.when(n > 0)
        def _():
            begin_in(block_at(n - 1))

        @pl.when(n == pause + 1)
        def _():
            fetch(0, 0)
            for q in range(groups):
                for d in range(2):
                    self.total(st.at[0, 0, q, 0, d], [sst.at[0, q, d]])

        @pl.when(n > lag)
        def _():
            send_block(n - lag)

        for k in mates:
            self.fan(k, j).wait_recv()
            self.sib_copy(0, k, j).start()

        @pl.when(j >= slots)
        def _():
            self.free(j - slots + 1)

        load = [pltpu.make_async_copy(inb.at[j, kind], st.at[slot, kind], self.local_sem.at[kind]) for kind in range(2)]
        for kind, own in ((1, self.grad_ref), (0, self.tok_ref)):
            for k in range(groups):
                self.sib_copy(kind, k, j).wait_recv()

            @pl.when(j == 0)
            def _():
                pltpu.make_async_copy(own, st.at[0, kind, g, 0], self.local_sem.at[kind]).start()
                pieces = [(at.group(k), 0) for k in mates] + [(q, 1) for q in range(groups)]
                for q, c in pieces:
                    pltpu.make_async_copy(inb.at[0, kind, q, c], st.at[0, kind, q, c], self.local_sem.at[kind]).start()

            @pl.when(j > 0)
            def _():
                load[kind].start()

        load[0].wait()
        gate_pre = up_pre = raw = 0.0
        for q in range(groups):
            tok = st[slot, 0, q].reshape(rows, width)
            gate_pre = gate_pre + dot(tok, gate_w[cuts[q], :])
            up_pre = up_pre + dot(tok, up_w[cuts[q], :])

        @pl.when(gather_on)
        def _():
            self.forward_grad(0, i)

        load[1].wait()
        for q in range(groups):
            raw = raw + dot_t(st[slot, 1, q].reshape(rows, width), down_w[:, cuts[q]])
        spots = [
            (at.chip(-j if d == 0 else j)[0] + c * (1 - 2 * at.core), d) for c in range(2) for d in range(2)
        ]
        gate = jnp.concatenate([as_column(self.gate_rows[e], diag[d]) for e, d in spots], axis=0)
        sig = jax.nn.sigmoid(gate_pre)
        act = gate_pre * sig
        hidden = act * up_pre
        marks = jnp.sum(hidden * raw, axis=1, keepdims=True)
        for k, (e, d) in enumerate(spots):
            self.score[e] = self.score[e] + as_row(marks[k * half : (k + 1) * half], diag[d])

        @pl.when(j == ring - 1)
        def _():
            @pl.loop(0, experts * groups)
            def _(n):
                e, y = n // groups, lax.rem(n, groups)

                @pl.when((e != me) | (y != g))
                def _():
                    self.send_score(y, e, g, me).start()

            self.score_in[g, me] = self.score[me]

        back = raw * gate
        gate_grad = (back * up_pre * sig * (1.0 + gate_pre * (1.0 - sig))).astype(BF)
        up_grad = (back * act).astype(BF)
        hidden = (hidden * gate).astype(BF)

        @pl.when(gather_on)
        def _():
            for k in mates:
                self.forward_grad(k, i)

        shape = (2, 2, half, width)
        for q in range(groups):
            st[slot, 0, q] = dot(hidden, down_w[:, cuts[q]]).astype(BF).reshape(shape)
        self.sib_res(0, slot, j).start()

        @pl.when(n > lag)
        def _():
            finish_in(n - lag)

        for q in range(groups):
            res = dot_t(gate_grad, gate_w[cuts[q], :]) + dot_t(up_grad, up_w[cuts[q], :])
            st[slot, 1, q] = res.astype(BF).reshape(shape)
        self.sib_res(1, slot, j).start()

    begin_in(jnp.int32(ring - 1))

    @pl.loop(ring - lag, ring)
    def _(b):
        send_block(b)
        finish_in(b)

    for k in self.others_first:
        q = at.group(k)
        for d in range(2):
            self.send_out(k, d, 0, ring - 1).wait_recv()
            self.total(st.at[0, 0, q, 0, d], [self.r_out.at[ring - 2, d, q]])
        if k > 0:
            self.tail(k).start()
    for j in mates:
        self.swap(j, 0, 0).wait_recv()

    @pl.loop(0, experts * groups)
    def _(n):
        e, y = n // groups, lax.rem(n, groups)

        @pl.when((e != me) | (y != g))
        def _():
            self.send_score(y, e, y, e).wait_recv()

    self.picked[...] = jnp.zeros_like(self.picked)

    @pl.loop(0, experts)
    def _(e):
        row = self.score_in[0, e]
        for y in range(1, groups):
            row = row + self.score_in[y, e]
        self.picked[...] += jnp.where(self.ids[...] == e, row, 0.0)

    for d in range(2):
        self.send_in(d, 0, ring - 1).wait_recv()
        self.total(
            st.at[0, 1, g, 0, d],
            [self.y_in.at[0, j - 1, d] for j in mates] + [self.r_in.at[ring - 2, d]],
            self.res_in.at[d],
        )
    for j in mates:
        self.tail(j).wait_recv()
    for d in range(2):
        self.total(st.at[0, 0, g, 0, d], [self.y_out.at[j - 1, d] for j in mates], self.res_out.at[d])

    for kind in range(2):
        self.sib_res(kind, 0, 0).wait_send()
    for j in mates:
        self.swap(j, 0, 0).wait_send()
        self.head(j).wait_send()
        self.tail(j).wait_send()

    @pl.loop(max(1, ring - slots + 1), ring)
    def _(b):
        self.free(b)

    @pl.loop(0, ring)
    def _(s):
        for j in mates:
            self.fan(j, s).wait_send()
        for kind in range(2):
            for k in range(groups):
                self.sib_copy(kind, k, s).wait_send()

        @pl.when(s < ring - 1)
        def _():
            for d in range(2):
                self.hop_tok(d, s).wait_send()
                for k in range(groups):
                    self.hop_grad(k, d, s).wait_send()

    @pl.loop(0, experts * groups)
    def _(n):
        e, y = n // groups, lax.rem(n, groups)

        @pl.when((e != me) | (y != g))
        def _():
            self.send_score(y, e, g, me).wait_send()

        @pl.when((e != me) & (y == 0))
        def _():
            self.send_gate(e, me).wait_send()


SLOTS = 4


def streamed(tokens, grad_out, gates, expert_ids, gate_proj, up_proj, down_proj):
    rows, width = tokens.shape
    groups = lax.axis_size("etp")
    experts = lax.axis_size("ep")
    ring = experts // 2
    half = rows // 2
    weights = (gate_proj, up_proj, down_proj)
    depth, hid = gate_proj.shape[1:]
    res = jax.ShapeDtypeStruct((2, half, width), BF)
    block = (2, groups, 2, 2, half, width)
    dma = pltpu.SemaphoreType.DMA
    hbm = pl.BlockSpec(memory_space=pltpu.HBM)
    vmem = pl.BlockSpec(memory_space=pltpu.VMEM)
    mates = groups - 1
    count = experts * rows
    outs = pl.pallas_call(
        functools.partial(fused_kernel, ring, groups, SLOTS),
        out_shape=(
            res,
            res,
            jax.ShapeDtypeStruct(gates.shape[::-1], F32),
            jax.ShapeDtypeStruct((ring,) + block, BF),
            jax.ShapeDtypeStruct((ring, 2, groups, 2, half, width), BF),
        ),
        in_specs=[hbm, hbm, vmem, vmem, hbm, hbm, hbm],
        out_specs=(vmem, vmem, vmem, hbm, hbm),
        scratch_shapes=[
            pltpu.VMEM((depth, hid), BF),
            pltpu.VMEM((depth, hid), BF),
            pltpu.VMEM((hid, depth), BF),
            pltpu.VMEM((SLOTS,) + block, BF),
            pltpu.VMEM((2, groups, 2, half, width), BF),
            pltpu.VMEM((ring - 1, 2, groups, half, width), BF),
            pltpu.VMEM((ring - 1, 2, half, width), BF),
            pltpu.VMEM((ring, mates, 2, half, width), BF),
            pltpu.VMEM((mates, 2, half, width), BF),
            pltpu.VMEM((experts, 1, rows), F32),
            pltpu.VMEM((experts, 1, rows), F32),
            pltpu.VMEM((experts, 1, rows), F32),
            pltpu.VMEM((groups, experts, 1, rows), F32),
            dma((5,)),
            dma((2, mates)),
            dma((2, 2, ring)),
            dma((2, groups, 2, ring)),
            dma((2, mates, ring)),
            dma((2, 2, groups, ring)),
            dma((2, 2, ring)),
            dma((2, mates, ring)),
            dma((2, groups, 2, ring)),
            dma((2, 2, ring)),
            dma((2, mates)),
            dma((2, experts)),
            dma((2, groups, experts)),
        ],
        cost_estimate=pl.CostEstimate(
            flops=12 * count * groups * width * hid,
            bytes_accessed=16 * count * groups * width,
            transcendentals=count * hid,
        ),
        compiler_params=pltpu.CompilerParams(
            collective_id=2, has_side_effects=True, vmem_limit_bytes=63 << 20
        ),
    )(tokens.reshape(2, half, width), grad_out.reshape(2, half, width), gates.T, expert_ids.T, *weights)
    return outs[0].reshape(rows, width), outs[1].reshape(rows, width), outs[2].T


def solution(mesh):
    in_specs = (
        P("ep", "etp"),
        P("ep", "etp"),
        P("ep", None),
        P("ep", None),
        P("ep", None, "etp"),
        P("ep", None, "etp"),
        P("ep", "etp", None),
    )
    out_specs = (P("ep", "etp"), P("ep", "etp"), P("ep", None))
    body = streamed if mesh.shape["ep"] <= 16 else local
    return jax.shard_map(body, mesh=mesh, in_specs=in_specs, out_specs=out_specs, check_vma=False)
```

```python
import functools
import math

import jax
import jax.numpy as jnp
import numpy as np
from jax import lax
from jax.experimental import pallas as pl
from jax.experimental.pallas import tpu as pltpu
from jax.sharding import PartitionSpec as P

BF = jnp.bfloat16
F32 = jnp.float32
MESH = pl.DeviceIdType.MESH


class Place:
    def __init__(self, ring, groups):
        self.ring, self.groups = ring, groups
        self.depth = math.gcd(ring, 4)
        self.cols = ring // self.depth
        me = lax.axis_index("ep")
        self.g = lax.axis_index("etp")
        self.core = lax.rem(me, 2)
        chip = me // 2
        x, z = lax.rem(chip, self.cols), chip // self.cols
        self.p = x * self.depth + z + lax.rem(x, 2) * (self.depth - 1 - 2 * z)

    def at(self, offset):
        return lax.rem(self.p + offset + self.ring, self.ring)

    def chip(self, offset):
        pos = self.at(offset)
        x, t = pos // self.depth, lax.rem(pos, self.depth)
        z = t + lax.rem(x, 2) * (self.depth - 1 - 2 * t)
        return ((z * self.cols + x) * 2 + self.core, self.g)

    def sibling(self):
        return (lax.axis_index("ep") + 1 - 2 * self.core, self.g)

    def group(self, j):
        return lax.rem(self.g + j, self.groups)

    def partner(self, j):
        return (lax.axis_index("ep"), self.group(j))

    def greet(self, with_sibling):
        barrier = pltpu.get_barrier_semaphore()
        others = [self.chip(1), self.chip(-1)] + [self.partner(j) for j in range(1, self.groups)]
        if with_sibling:
            others.append(self.sibling())
        for other in others:
            pl.semaphore_signal(barrier, inc=1, device_id=other, device_id_type=MESH)
        pl.semaphore_wait(barrier, len(others))


def remote(src, dst, send, recv, where):
    return pltpu.make_async_remote_copy(
        src_ref=src, dst_ref=dst, send_sem=send, recv_sem=recv, device_id=where, device_id_type=MESH
    )


def gather_kernel(
    ring, groups, tok_ref, grad_ref, tok, tok_sib, grad, grad_sib, local_sem, first, rings, fans, late
):
    at = Place(ring, groups)
    at.greet(True)
    g = at.g
    sib = at.sibling()
    own_tok = pltpu.make_async_copy(tok_ref, tok.at[g, at.p], local_sem.at[0])
    own_grad = pltpu.make_async_copy(grad_ref, grad.at[g, at.p], local_sem.at[1])
    own_tok.start()
    own_grad.start()
    heads = []
    for j in range(1, groups):
        head = remote(
            grad_ref, grad.at[g, at.p], first.at[0, j - 1], first.at[1, j - 1], at.partner(j)
        )
        head.start()
        heads.append(head)
    own_tok.wait()

    def back(d, s):
        return at.at(-s if d == 0 else s)

    fan_y, fan_s, fan_t = {}, {}, {}

    def fan_tok(s):
        for d in range(2):
            b = back(d, s)
            fan_y[s, d] = []
            for j in range(1, groups):
                c = remote(
                    tok.at[g, b, d],
                    tok.at[g, b, d],
                    fans.at[0, j, d, s],
                    fans.at[1, j, d, s],
                    at.partner(j),
                )
                c.start()
                fan_y[s, d].append(c)

    def fan_grad(s):
        for d in range(2):
            b = back(d, s)
            c = remote(
                grad.at[:, b, d], grad_sib.at[:, b, d], fans.at[0, 0, d, s], fans.at[1, 0, d, s], sib
            )
            c.start()
            fan_s[s, d] = c

    def fan_late(s):
        for d in range(2):
            b = back(d, s)
            for c in fan_y[s, d]:
                c.wait_recv()
            c = remote(tok.at[:, b, d], tok_sib.at[:, b, d], late.at[0, d, s], late.at[1, d, s], sib)
            c.start()
            fan_t[s, d] = c

    hops = {}

    def hop(kind, d, s):
        b = back(d, s - 1)
        block = tok.at[g, b, d] if kind == 0 else grad.at[:, b, d]
        if s > 1:
            hops[kind, d, s - 1].wait_recv()
        if s < ring:
            c = remote(
                block,
                block,
                rings.at[0, kind, d, s - 1],
                rings.at[1, kind, d, s - 1],
                at.chip(1 if d == 0 else -1),
            )
            c.start()
            hops[kind, d, s] = c

    for s in range(1, ring + 1):
        hop(0, 0, s)
        hop(0, 1, s)
        if s == 1:
            own_grad.wait()
            for head in heads:
                head.wait_recv()
        if s < ring:
            fan_tok(s - 1)
        hop(1, 0, s)
        hop(1, 1, s)
        if s < ring:
            fan_grad(s - 1)
        if s >= 2:
            fan_late(s - 2)
    fan_tok(ring - 1)
    fan_grad(ring - 1)
    fan_late(ring - 1)
    for c in list(fan_s.values()) + list(fan_t.values()):
        c.wait()
    for group in fan_y.values():
        for c in group:
            c.wait_send()
    for c in list(hops.values()) + heads:
        c.wait_send()


def gather(tokens, grad_out, ring, groups):
    rows, width = tokens.shape
    half = rows // 2
    full = jax.ShapeDtypeStruct((groups, ring, 2, half, width), BF)
    dma = pltpu.SemaphoreType.DMA
    hbm = pl.BlockSpec(memory_space=pltpu.HBM)
    return pl.pallas_call(
        functools.partial(gather_kernel, ring, groups),
        out_shape=(full,) * 4,
        in_specs=[hbm, hbm],
        out_specs=(hbm,) * 4,
        scratch_shapes=[
            dma((2,)),
            dma((2, groups - 1)),
            dma((2, 2, 2, ring - 1)),
            dma((2, groups, 2, ring)),
            dma((2, 2, ring)),
        ],
        compiler_params=pltpu.CompilerParams(collective_id=0, has_side_effects=True),
    )(tokens.reshape(2, half, width), grad_out.reshape(2, half, width))


def scatter_kernel(
    ring, groups, s_out, s_in, res_out, res_in, v_out, v_in, r_out, r_in, y_in, y_out, loads, rings, ys, tail
):
    at = Place(ring, groups)
    g = at.g
    half = v_in.shape[2]

    def dest(d, s):
        return at.at(-s if d == 0 else s)

    load_out, load_in, swap = {}, {}, {}
    for s in range(1, ring + 1):
        for d in range(2):
            b = dest(d, s)
            load_out[s, d] = pltpu.make_async_copy(
                s_out.at[:, b, d], v_out.at[:, b, d], loads.at[0, d, s - 1]
            )
            load_in[s, d] = pltpu.make_async_copy(s_in.at[g, b, d], v_in.at[b, d], loads.at[1, d, s - 1])
            load_out[s, d].start()
            load_in[s, d].start()
    at.greet(False)
    for s in range(1, ring + 1):
        for d in range(2):
            b = dest(d, s)
            swap[s, d] = []
            for j in range(1, groups):
                c = remote(
                    s_in.at[at.group(j), b, d],
                    y_in.at[j - 1, b, d],
                    ys.at[0, j - 1, d, s - 1],
                    ys.at[1, j - 1, d, s - 1],
                    at.partner(j),
                )
                c.start()
                swap[s, d].append(c)

    def total(target, others):
        @pl.loop(0, half // 16)
        def _(i):
            rows = pl.ds(pl.multiple_of(i * 16, 16), 16)
            acc = target[rows, :].astype(F32)
            for other in others:
                acc = acc + other[rows, :].astype(F32)
            target[rows, :] = acc.astype(BF)

    hop_out, hop_in = {}, {}
    for s in range(1, ring + 1):
        for d in range(2):
            b = dest(d, s)
            load_out[s, d].wait()
            if s > 1:
                hop_out[s - 1, d].wait_recv()
                for q in range(groups):
                    total(v_out.at[q, b, d], [r_out.at[d, s - 2, q]])
            if s < ring:
                c = remote(
                    v_out.at[:, b, d],
                    r_out.at[d, s - 1],
                    rings.at[0, 0, d, s - 1],
                    rings.at[1, 0, d, s - 1],
                    at.chip(1 if d == 0 else -1),
                )
                c.start()
                hop_out[s, d] = c
        if s == ring:
            ends = []
            for d in range(2):
                for j in range(1, groups):
                    c = remote(
                        v_out.at[at.group(j), at.p, d],
                        y_out.at[j - 1, d],
                        tail.at[0, j - 1, d],
                        tail.at[1, j - 1, d],
                        at.partner(j),
                    )
                    c.start()
                    ends.append(c)
        for d in range(2):
            b = dest(d, s)
            load_in[s, d].wait()
            others = []
            for c in swap[s, d]:
                c.wait_recv()
            others = [y_in.at[j - 1, b, d] for j in range(1, groups)]
            if s > 1:
                hop_in[s - 1, d].wait_recv()
                others.append(r_in.at[d, s - 2])
            total(v_in.at[b, d], others)
            if s < ring:
                c = remote(
                    v_in.at[b, d],
                    r_in.at[d, s - 1],
                    rings.at[0, 1, d, s - 1],
                    rings.at[1, 1, d, s - 1],
                    at.chip(1 if d == 0 else -1),
                )
                c.start()
                hop_in[s, d] = c
    for d in range(2):
        res_in[d] = v_in[at.p, d]
    for c in ends:
        c.wait_recv()
    for d in range(2):
        total(v_out.at[g, at.p, d], [y_out.at[j - 1, d] for j in range(1, groups)])
        res_out[d] = v_out[g, at.p, d]
    for c in list(hop_out.values()) + list(hop_in.values()) + ends:
        c.wait_send()
    for group in swap.values():
        for c in group:
            c.wait_send()


def scatter(s_out, s_in):
    groups, ring, _, half, width = s_out.shape
    res = jax.ShapeDtypeStruct((2, half, width), BF)
    dma = pltpu.SemaphoreType.DMA
    hbm = pl.BlockSpec(memory_space=pltpu.HBM)
    vmem = pl.BlockSpec(memory_space=pltpu.VMEM)
    out, inn = pl.pallas_call(
        functools.partial(scatter_kernel, ring, groups),
        out_shape=(res, res),
        in_specs=[hbm, hbm],
        out_specs=(vmem, vmem),
        scratch_shapes=[
            pltpu.VMEM((groups, ring, 2, half, width), BF),
            pltpu.VMEM((ring, 2, half, width), BF),
            pltpu.VMEM((2, ring - 1, groups, half, width), BF),
            pltpu.VMEM((2, ring - 1, half, width), BF),
            pltpu.VMEM((groups - 1, ring, 2, half, width), BF),
            pltpu.VMEM((groups - 1, 2, half, width), BF),
            dma((2, 2, ring)),
            dma((2, 2, 2, ring - 1)),
            dma((2, groups - 1, 2, ring)),
            dma((2, groups - 1, 2)),
        ],
        compiler_params=pltpu.CompilerParams(
            collective_id=1, has_side_effects=True, vmem_limit_bytes=60 << 20
        ),
    )(s_out, s_in)
    return out.reshape(2 * half, width), inn.reshape(2 * half, width)


def dot(a, b):
    return lax.dot_general(a, b, (((1,), (0,)), ((), ())), preferred_element_type=F32)


def dot_t(a, b):
    return lax.dot_general(a, b, (((1,), (1,)), ((), ())), preferred_element_type=F32)


def first_half(groups, gate_ref, tok, grad, gate_w, up_w, down_w, score):
    width = tok.shape[2]
    cuts = [slice(g * width, (g + 1) * width) for g in range(groups)]
    gate_pre = sum(dot(tok[g], gate_w[cuts[g], :]) for g in range(groups))
    up_pre = sum(dot(tok[g], up_w[cuts[g], :]) for g in range(groups))
    raw = sum(dot_t(grad[g], down_w[:, cuts[g]]) for g in range(groups))
    gate = gate_ref[...]
    sig = jax.nn.sigmoid(gate_pre)
    act = gate_pre * sig
    hidden = act * up_pre
    score[...] = jnp.sum(hidden * raw, axis=1, keepdims=True)
    back = raw * gate
    gate_grad = back * up_pre * sig * (1.0 + gate_pre * (1.0 - sig))
    return (hidden * gate).astype(BF), gate_grad.astype(BF), (back * act).astype(BF)


def second_half(groups, hidden, gate_grad, up_grad, gate_w, up_w, down_w, out, inn, add=None):
    width = out.shape[2]
    for g in range(groups):
        cut = slice(g * width, (g + 1) * width)
        res = dot(hidden, down_w[:, cut])
        if add:
            res = res + add[0][g].astype(F32)
        out[g] = res.astype(BF)
        res = dot_t(gate_grad, gate_w[cut, :]) + dot_t(up_grad, up_w[cut, :])
        if add:
            res = res + add[1][g].astype(F32)
        inn[g] = res.astype(BF)


def whole_kernel(groups, gate, tok, grad, gate_w, up_w, down_w, out, inn, score):
    mids = first_half(groups, gate, tok, grad, gate_w, up_w, down_w, score)
    second_half(groups, *mids, gate_w, up_w, down_w, out, inn)


def begin_kernel(groups, gate, tok, grad, gate_w, up_w, down_w, hidden, gate_grad, up_grad, score):
    mids = first_half(groups, gate, tok, grad, gate_w, up_w, down_w, score)
    hidden[...], gate_grad[...], up_grad[...] = mids


def finish_kernel(groups, hidden, gate_grad, up_grad, gate_w, up_w, down_w, add_out, add_in, out, inn):
    second_half(
        groups,
        hidden[...],
        gate_grad[...],
        up_grad[...],
        gate_w,
        up_w,
        down_w,
        out,
        inn,
        (add_out, add_in),
    )


def expert(stage, shape, weights, *rows):
    groups, count, width = shape
    hid = weights[0].shape[2]
    tile = 256
    slab = (pl.BlockSpec((groups, tile, width), lambda i: (0, i, 0)), jax.ShapeDtypeStruct(shape, BF))
    column = (pl.BlockSpec((tile, 1), lambda i: (i, 0)), jax.ShapeDtypeStruct((count, 1), F32))
    units = (pl.BlockSpec((tile, hid), lambda i: (i, 0)), jax.ShapeDtypeStruct((count, hid), BF))
    fixed = [
        pl.BlockSpec((None,) + w.shape[1:], lambda i: (0, 0, 0), pipeline_mode=pl.Buffered(1))
        for w in weights
    ]
    kernel, heads, tails, results = {
        "whole": (whole_kernel, [column, slab, slab], [], [slab, slab, column]),
        "begin": (begin_kernel, [column, slab, slab], [], [units, units, units, column]),
        "finish": (finish_kernel, [units, units, units], [slab, slab], [slab, slab]),
    }[stage]
    split = len(heads)
    return pl.pallas_call(
        functools.partial(kernel, groups),
        grid=(count // tile,),
        out_shape=[r[1] for r in results],
        in_specs=[h[0] for h in heads] + fixed + [t[0] for t in tails],
        out_specs=[r[0] for r in results],
        input_output_aliases={6: 0, 7: 1} if stage == "finish" else {},
        cost_estimate=pl.CostEstimate(
            flops=(12 if stage == "whole" else 6) * count * groups * width * hid,
            bytes_accessed=8 * count * groups * width,
            transcendentals=0 if stage == "finish" else count * hid,
        ),
        compiler_params=pltpu.CompilerParams(vmem_limit_bytes=60 << 20),
    )(*rows[:split], *weights, *rows[split:])


def local(tokens, grad_out, gates, expert_ids, gate_proj, up_proj, down_proj):
    rows, width = tokens.shape
    groups = lax.axis_size("etp")
    experts = lax.axis_size("ep")
    ring = experts // 2
    core = lax.rem(lax.axis_index("ep"), 2)
    depth = math.gcd(ring, 4)
    cols = ring // depth
    order = np.zeros(ring, np.int32)
    for pos in range(ring):
        x, t = pos // depth, pos % depth
        order[pos] = (t if x % 2 == 0 else depth - 1 - t) * cols + x
    inverse = np.argsort(order)
    count = ring * rows

    onehot = expert_ids[:, :, None] == jnp.arange(experts, dtype=jnp.int32)[None, None, :]
    table = jnp.sum(jnp.where(onehot, gates[:, :, None], 0.0), axis=1)
    mine = lax.all_to_all(table.T, "ep", split_axis=0, concat_axis=0, tiled=True)
    mine = mine.reshape(ring, 2, rows)
    mine = jnp.stack([mine[int(c)] for c in order]).transpose(1, 0, 2)
    mine = jnp.where(core == 0, mine, mine[::-1])

    flat = (groups, count, width)
    tok_own, tok_sib, grad_own, grad_sib = (
        a.reshape(flat) for a in gather(tokens, grad_out, ring, groups)
    )
    swap = [(i, i ^ 1) for i in range(experts)]
    weights = (gate_proj, up_proj, down_proj)
    *mids, score_own = expert("begin", flat, weights, mine[0].reshape(count, 1), tok_own, grad_own)
    out, inn, score_sib = expert("whole", flat, weights, mine[1].reshape(count, 1), tok_sib, grad_sib)
    got = (lax.ppermute(out, "ep", swap), lax.ppermute(inn, "ep", swap))
    out, inn = expert("finish", flat, weights, *mids, *got)
    scores = [score_own.reshape(ring, rows), score_sib.reshape(ring, rows)]
    shape = (groups, ring, 2, rows // 2, width)
    layer_out, token_grad = scatter(out.reshape(shape), inn.reshape(shape))

    score = jnp.stack(scores)
    score = jnp.where(core == 0, score, score[::-1]).transpose(1, 0, 2)
    score = jnp.stack([score[int(c)] for c in inverse]).reshape(experts, rows)
    score = lax.all_to_all(score, "ep", split_axis=0, concat_axis=0, tiled=True)
    score = lax.psum(score, "etp")
    picked = jnp.sum(jnp.where(onehot, score.T[:, None, :], 0.0), axis=2)
    return layer_out, token_grad, picked


class Stream:
    def __init__(self, ring, groups, slots, refs):
        self.ring, self.groups, self.slots = ring, groups, slots
        (
            self.tok_ref, self.grad_ref, self.gates, self.ids, self.gate_hbm, self.up_hbm, self.down_hbm,
            self.res_out, self.res_in, self.picked, self.inb,
            self.gate_w, self.up_w, self.down_w, self.st, self.sst, self.r_out, self.r_in, self.y_in, self.y_out,
            self.y_low,
            self.table, self.gate_rows, self.score, self.score_in,
            self.local_sem, self.head_sem, self.hop_t, self.hop_g, self.fan_sem, self.sib_g,
            self.sib_r, self.swap_sem, self.ring_o, self.ring_i, self.tail_sem, self.gate_sem, self.score_sem,
            self.fan_g, self.sib_x, self.swap_o, self.credit,
        ) = refs
        self.at = at = Place(ring, groups)
        self.g = at.g
        self.me = lax.axis_index("ep")
        self.sib = at.sibling()
        self.near = [at.chip(1), at.chip(-1)]
        self.half, self.width = self.st.shape[5], self.st.shape[6]
        self.mates = range(1, groups)
        self.edge = self.y_low.shape[4]
        self.others_first = [k % groups for k in range(1, groups + 1)]

    def low(self, ref):
        return ref.at[(slice(None),) * (len(ref.shape) - 1) + (pl.ds(0, self.edge),)]

    def high(self, ref):
        return ref.at[(slice(None),) * (len(ref.shape) - 1) + (pl.ds(self.edge, self.width - self.edge),)]

    def ring_part(self, ref, k):
        return ref if k == 0 else self.high(ref)

    def hop_tok(self, d, s, src=None):
        src = self.inb.at[s, 0, self.g, 0, d] if src is None else src
        return remote(
            src, self.inb.at[s + 1, 0, self.g, 0, d], self.hop_t.at[0, d, s], self.hop_t.at[1, d, s], self.near[d]
        )

    def hop_grad(self, k, d, s, src=None):
        q = self.at.group(k)
        src = self.ring_part(self.inb.at[s, 1, q, 0, d], k) if src is None else src
        dst = self.ring_part(self.inb.at[s + 1, 1, q, 0, d], k)
        return remote(src, dst, self.hop_g.at[0, k, d, s], self.hop_g.at[1, k, d, s], self.near[d])

    def head(self, j):
        return remote(
            self.high(self.grad_ref), self.high(self.inb.at[0, 1, self.g, 0]), self.head_sem.at[0, j - 1],
            self.head_sem.at[1, j - 1], self.at.partner(j),
        )

    def fan(self, j, s, src=None):
        block = self.inb.at[s, 0, self.g, 0]
        src = block if src is None else src
        return remote(src, block, self.fan_sem.at[0, j - 1, s], self.fan_sem.at[1, j - 1, s], self.at.partner(j))

    def fan_grad(self, j, s, src=None):
        block = self.low(self.inb.at[s, 1, self.g, 0])
        src = block if src is None else src
        return remote(src, block, self.fan_g.at[0, j - 1, s], self.fan_g.at[1, j - 1, s], self.at.partner(j))

    def sib_copy(self, kind, k, s, src=None):
        q = self.at.group(k)
        part = k if kind == 1 else 0
        src = self.ring_part(self.inb.at[s, kind, q, 0], part) if src is None else src
        dst = self.ring_part(self.inb.at[s, kind, q, 1], part)
        return remote(src, dst, self.sib_g.at[0, kind, k, s], self.sib_g.at[1, kind, k, s], self.sib)

    def sib_low(self, k, s):
        q = self.at.group(k)
        return remote(
            self.low(self.inb.at[s, 1, q, 0]), self.low(self.inb.at[s, 1, q, 1]), self.sib_x.at[0, k - 1, s],
            self.sib_x.at[1, k - 1, s], self.sib,
        )

    def sib_res(self, kind, slot, s, turn):
        return remote(
            self.st.at[slot, kind, :, 1], self.sst.at[lax.rem(turn, 2), kind], self.sib_r.at[0, kind, s], self.sib_r.at[1, kind, s],
            self.sib,
        )

    def swap(self, j, slot, s):
        return remote(
            self.st.at[slot, 1, self.at.group(j), 0], self.y_in.at[s, j - 1], self.swap_sem.at[0, j - 1, s],
            self.swap_sem.at[1, j - 1, s], self.at.partner(j),
        )

    def swap_low(self, j, slot, s):
        return remote(
            self.low(self.st.at[slot, 0, self.at.group(j), 0]), self.y_low.at[s, j - 1], self.swap_o.at[0, j - 1, s],
            self.swap_o.at[1, j - 1, s], self.at.partner(j),
        )

    def send_out(self, k, d, slot, s):
        q = self.at.group(k)
        return remote(
            self.ring_part(self.st.at[slot, 0, q, 0, d], k), self.ring_part(self.r_out.at[s - 1, d, q], k),
            self.ring_o.at[0, k, d, s], self.ring_o.at[1, k, d, s], self.near[d],
        )

    def send_in(self, d, slot, s):
        return remote(
            self.st.at[slot, 1, self.g, 0, d], self.r_in.at[s - 1, d], self.ring_i.at[0, d, s], self.ring_i.at[1, d, s],
            self.near[d],
        )

    def tail(self, j):
        return remote(
            self.high(self.st.at[0, 0, self.at.group(j), 0]), self.y_out.at[j - 1], self.tail_sem.at[0, j - 1],
            self.tail_sem.at[1, j - 1], self.at.partner(j),
        )

    def send_gate(self, e, row):
        return remote(
            self.table.at[e], self.gate_rows.at[row], self.gate_sem.at[0, e], self.gate_sem.at[1, row], (e, self.g)
        )

    def send_score(self, y, e, from_y, row):
        return remote(
            self.score.at[e], self.score_in.at[from_y, row], self.score_sem.at[0, y, e],
            self.score_sem.at[1, from_y, row], (e, y),
        )

    def slot_of(self, j):
        return jnp.where(j == 0, 0, 1 + lax.rem(j + self.slots - 2, self.slots - 1))

    def free(self, b):
        slot = self.slot_of(b)
        for kind in range(2):
            self.sib_res(kind, slot, b, 0).wait_send()
        for j in self.mates:
            self.swap(j, slot, b).wait_send()
            self.swap_low(j, slot, b).wait_send()
        for d in range(2):
            for k in range(self.groups):
                self.send_out(k, d, slot, b).wait_send()
            self.send_in(d, slot, b).wait_send()

    def greet_all(self):
        barrier = pltpu.get_barrier_semaphore()
        experts = 2 * self.ring

        @pl.loop(0, experts * self.groups)
        def _(i):
            e, y = i // self.groups, lax.rem(i, self.groups)

            @pl.when((e != self.me) | (y != self.g))
            def _():
                pl.semaphore_signal(barrier, inc=1, device_id=(e, y), device_id_type=MESH)

        pl.semaphore_wait(barrier, experts * self.groups - 1)

    def total(self, target, others, dest=None):
        dest = target if dest is None else dest

        @pl.loop(0, self.half // 16)
        def _(i):
            part = pl.ds(pl.multiple_of(i * 16, 16), 16)
            acc = target[part, :].astype(F32)
            for other in others:
                acc = acc + other[part, :].astype(F32)
            dest[part, :] = acc.astype(BF)

    def forward_tok(self, i):
        for d in range(2):
            self.hop_tok(d, i - 1).wait_recv()

            @pl.when(i < self.ring - 1)
            def _():
                self.hop_tok(d, i).start()

        for j in self.mates:
            self.fan(j, i).start()
        self.sib_copy(0, 0, i).start()

    def forward_grad(self, k, i):
        for d in range(2):
            self.hop_grad(k, d, i - 1).wait_recv()

            @pl.when(i < self.ring - 1)
            def _():
                self.hop_grad(k, d, i).start()

        if k == 0:
            for j in self.mates:
                self.fan_grad(j, i).start()
        self.sib_copy(1, k, i).start()


def fused_kernel(ring, groups, slots, *refs):
    self = Stream(ring, groups, slots, refs)
    at, g, me, mates = self.at, self.g, self.me, self.mates
    st, sst, inb = self.st, self.sst, self.inb
    gate_w, up_w, down_w = self.gate_w, self.up_w, self.down_w
    half, width = self.half, self.width
    rows, experts = 4 * half, 2 * ring
    pause = min(PAUSE, ring - 2)
    cuts = [slice(q * width, (q + 1) * width) for q in range(groups)]

    loads = [
        pltpu.make_async_copy(src.at[0], dst, self.local_sem.at[2 + k])
        for k, (src, dst) in enumerate([(self.gate_hbm, gate_w), (self.up_hbm, up_w), (self.down_hbm, down_w)])
    ]
    self.greet_all()
    for j in mates:
        self.head(j).start()
    for d in range(2):
        self.hop_tok(d, 0, self.tok_ref.at[d]).start()
    for d in range(2):
        self.hop_grad(0, d, 0, self.grad_ref.at[d]).start()
    self.sib_copy(0, 0, 0, self.tok_ref).start()
    self.sib_copy(1, 0, 0, self.grad_ref).start()
    for load in loads:
        load.start()

    def iota(shape, axis):
        return lax.broadcasted_iota(jnp.int32, shape, axis)

    diag = [iota((half, 2 * half), 0) + d * half == iota((half, 2 * half), 1) for d in range(2)]

    def as_row(column, mask):
        return jnp.sum(jnp.where(mask, column, 0.0), axis=0, keepdims=True)

    def as_column(row, mask):
        return jnp.sum(jnp.where(mask, row, 0.0), axis=1, keepdims=True)

    @pl.loop(0, experts)
    def _(e):
        mine = jnp.where(self.ids[...] == e, self.gates[...], 0.0)
        self.table[e] = jnp.sum(mine, axis=0, keepdims=True)
        self.score[e] = jnp.zeros((1, 2 * half), F32)

    @pl.loop(0, experts)
    def _(e):
        @pl.when(e != me)
        def _():
            self.send_gate(e, me).start()

    self.gate_rows[me] = self.table[me]
    self.forward_tok(1)
    for j in mates:
        self.fan(j, 0, self.tok_ref).start()
        self.fan_grad(j, 0, self.low(self.grad_ref)).start()
    for j in mates:
        self.head(j).wait_recv()
        for d in range(2):
            self.hop_grad(j, d, 0).start()
        self.sib_copy(1, j, 0).start()

    for k in range(groups):
        self.forward_grad(k, 1)

    @pl.loop(0, experts)
    def _(e):
        @pl.when(e != me)
        def _():
            self.send_gate(e, e).wait_recv()

    for w in loads:
        w.wait()

    def finish_in(j):
        slot = self.slot_of(j)
        for k in mates:
            self.swap(k, slot, j).wait_recv()
        for d in range(2):
            target = st.at[slot, 1, g, 0, d]
            added = [self.y_in.at[j, k - 1, d] for k in mates]

            @pl.when(j > 1)
            def _():
                self.send_in(d, slot, j - 1).wait_recv()
                self.total(target, added + [self.r_in.at[j - 2, d]])

            @pl.when(j <= 1)
            def _():
                self.total(target, added)

            @pl.when(j > 0)
            def _():
                self.send_in(d, slot, j).start()

    def begin_out(j, turn):
        slot = self.slot_of(j)
        got = sst.at[lax.rem(turn, 2)]
        self.sib_res(0, slot, j, turn).wait_recv()
        for k in mates:
            q = at.group(k)
            for d in range(2):
                self.total(self.low(st.at[slot, 0, q, 0, d]), [self.low(got.at[0, q, d])])
            self.swap_low(k, slot, j).start()

    def begin_in(j, turn):
        slot = self.slot_of(j)
        got = sst.at[lax.rem(turn, 2)]
        self.sib_res(1, slot, j, turn).wait_recv()
        for k in self.others_first:
            q = at.group(k)
            for d in range(2):
                self.total(st.at[slot, 1, q, 0, d], [got.at[1, q, d]])
            if k > 0:
                self.swap(k, slot, j).start()

    def total_out(k, d, slot, j, turn):
        q = at.group(k)
        got = sst.at[lax.rem(turn, 2)]
        parts = [(self.high, [])]
        if k == 0:
            parts.append((self.low, [self.y_low.at[j, m - 1, d] for m in mates]))

        @pl.when(j > 1)
        def _():
            self.send_out(k, d, slot, j - 1).wait_recv()
            for part, more in parts:
                added = [part(got.at[0, q, d]), part(self.r_out.at[j - 2, d, q])]
                self.total(part(st.at[slot, 0, q, 0, d]), added + more)

        @pl.when(j <= 1)
        def _():
            for part, more in parts:
                self.total(part(st.at[slot, 0, q, 0, d]), [part(got.at[0, q, d])] + more)

        @pl.when(j > 0)
        def _():
            self.send_out(k, d, slot, j).start()

    def send_block(j, turn):
        for k in mates:
            for d in range(2):
                total_out(k, d, self.slot_of(j), j, turn)

    def finish_block(j, turn):
        for k in mates:
            self.swap_low(k, self.slot_of(j), j).wait_recv()
        for d in range(2):
            total_out(0, d, self.slot_of(j), j, turn)

    def block_at(n):
        return jnp.where(n < pause, n + 1, jnp.where(n == pause, 0, n))

    @pl.loop(0, ring)
    def _(n):
        j = block_at(n)
        i = j + 1
        slot = self.slot_of(j)
        gather_on = (j > 0) & (i < ring)
        before = block_at(n - 1)

        @pl.when(n > 0)
        def _():
            begin_out(before, n - 1)

        @pl.when(gather_on)
        def _():
            self.forward_tok(i)

        for k in mates:
            self.fan(k, j).wait_recv()
            self.sib_copy(0, k, j).start()
            self.fan_grad(k, j).wait_recv()
            self.sib_low(k, j).start()

        @pl.when(n > 0)
        def _():
            begin_in(before, n - 1)

        @pl.when(j >= slots)
        def _():
            self.free(j - slots + 1)

        load = [pltpu.make_async_copy(inb.at[j, kind], st.at[slot, kind], self.local_sem.at[kind]) for kind in range(2)]
        for kind, own in ((1, self.grad_ref), (0, self.tok_ref)):
            for k in range(groups):
                self.sib_copy(kind, k, j).wait_recv()
                if kind == 1 and k > 0:
                    self.sib_low(k, j).wait_recv()

            @pl.when(j == 0)
            def _():
                pltpu.make_async_copy(own, st.at[0, kind, g, 0], self.local_sem.at[kind]).start()
                pieces = [(at.group(k), 0) for k in mates] + [(q, 1) for q in range(groups)]
                for q, c in pieces:
                    pltpu.make_async_copy(inb.at[0, kind, q, c], st.at[0, kind, q, c], self.local_sem.at[kind]).start()

            @pl.when(j > 0)
            def _():
                load[kind].start()

        @pl.when(n > 0)
        def _():
            send_block(before, n - 1)

        load[0].wait()
        gate_pre = up_pre = raw = 0.0
        for q in range(groups):
            tok = st[slot, 0, q].reshape(rows, width)
            gate_pre = gate_pre + dot(tok, gate_w[cuts[q], :])
            up_pre = up_pre + dot(tok, up_w[cuts[q], :])

        @pl.when(n > 0)
        def _():
            finish_block(before, n - 1)

        @pl.when((n > 0) & (n < ring - 1))
        def _():
            pl.semaphore_signal(self.credit, inc=1, device_id=self.sib, device_id_type=MESH)

        @pl.when(gather_on)
        def _():
            self.forward_grad(0, i)

        load[1].wait()
        for q in range(groups):
            raw = raw + dot_t(st[slot, 1, q].reshape(rows, width), down_w[:, cuts[q]])
        spots = [
            (at.chip(-j if d == 0 else j)[0] + c * (1 - 2 * at.core), d) for c in range(2) for d in range(2)
        ]
        gate = jnp.concatenate([as_column(self.gate_rows[e], diag[d]) for e, d in spots], axis=0)
        sig = jax.nn.sigmoid(gate_pre)
        act = gate_pre * sig
        hidden = act * up_pre
        marks = jnp.sum(hidden * raw, axis=1, keepdims=True)
        for k, (e, d) in enumerate(spots):
            self.score[e] = self.score[e] + as_row(marks[k * half : (k + 1) * half], diag[d])

        @pl.when(j == ring - 1)
        def _():
            @pl.loop(0, experts * groups)
            def _(n):
                e, y = n // groups, lax.rem(n, groups)

                @pl.when((e != me) | (y != g))
                def _():
                    self.send_score(y, e, g, me).start()

            self.score_in[g, me] = self.score[me]

        back = raw * gate
        gate_grad = (back * up_pre * sig * (1.0 + gate_pre * (1.0 - sig))).astype(BF)
        up_grad = (back * act).astype(BF)
        hidden = (hidden * gate).astype(BF)

        @pl.when(gather_on)
        def _():
            for k in mates:
                self.forward_grad(k, i)

        shape = (2, 2, half, width)
        for q in range(groups):
            st[slot, 0, q] = dot(hidden, down_w[:, cuts[q]]).astype(BF).reshape(shape)

        @pl.when(n > 1)
        def _():
            pl.semaphore_wait(self.credit, 1)

        self.sib_res(0, slot, j, n).start()

        @pl.when(n > 1)
        def _():
            finish_in(block_at(n - 2))

        for q in range(groups):
            res = dot_t(gate_grad, gate_w[cuts[q], :]) + dot_t(up_grad, up_w[cuts[q], :])
            st[slot, 1, q] = res.astype(BF).reshape(shape)
        self.sib_res(1, slot, j, n).start()

    last = jnp.int32(ring - 1)
    begin_out(last, ring - 1)
    begin_in(last, ring - 1)
    finish_in(block_at(ring - 2))
    send_block(last, ring - 1)
    finish_block(last, ring - 1)
    finish_in(last)

    for k in self.others_first:
        q = at.group(k)
        for d in range(2):
            self.send_out(k, d, 0, ring - 1).wait_recv()
            part = self.ring_part(st.at[0, 0, q, 0, d], k)
            self.total(part, [self.ring_part(self.r_out.at[ring - 2, d, q], k)])
        if k > 0:
            self.tail(k).start()
    @pl.loop(0, experts * groups)
    def _(n):
        e, y = n // groups, lax.rem(n, groups)

        @pl.when((e != me) | (y != g))
        def _():
            self.send_score(y, e, y, e).wait_recv()

    self.picked[...] = jnp.zeros_like(self.picked)

    @pl.loop(0, experts)
    def _(e):
        row = self.score_in[0, e]
        for y in range(1, groups):
            row = row + self.score_in[y, e]
        self.picked[...] += jnp.where(self.ids[...] == e, row, 0.0)

    for d in range(2):
        self.send_in(d, 0, ring - 1).wait_recv()
        self.total(
            st.at[0, 1, g, 0, d],
            [self.r_in.at[ring - 2, d]],
            self.res_in.at[d],
        )
    for j in mates:
        self.tail(j).wait_recv()
    for d in range(2):
        own, done = st.at[0, 0, g, 0, d], self.res_out.at[d]
        self.total(self.low(own), [], self.low(done))
        self.total(self.high(own), [self.y_out.at[j - 1, d] for j in mates], self.high(done))

    for kind in range(2):
        self.sib_res(kind, 0, 0, 0).wait_send()
    for j in mates:
        self.swap(j, 0, 0).wait_send()
        self.swap_low(j, 0, 0).wait_send()
        self.head(j).wait_send()
        self.tail(j).wait_send()

    @pl.loop(max(1, ring - slots + 1), ring)
    def _(b):
        self.free(b)

    @pl.loop(0, ring)
    def _(s):
        for j in mates:
            self.fan(j, s).wait_send()
            self.fan_grad(j, s).wait_send()
            self.sib_low(j, s).wait_send()
        for kind in range(2):
            for k in range(groups):
                self.sib_copy(kind, k, s).wait_send()

        @pl.when(s < ring - 1)
        def _():
            for d in range(2):
                self.hop_tok(d, s).wait_send()
                for k in range(groups):
                    self.hop_grad(k, d, s).wait_send()

    @pl.loop(0, experts * groups)
    def _(n):
        e, y = n // groups, lax.rem(n, groups)

        @pl.when((e != me) | (y != g))
        def _():
            self.send_score(y, e, g, me).wait_send()

        @pl.when((e != me) & (y == 0))
        def _():
            self.send_gate(e, me).wait_send()


SLOTS = 4
PAUSE = 2
EDGE = 8


def streamed(tokens, grad_out, gates, expert_ids, gate_proj, up_proj, down_proj):
    rows, width = tokens.shape
    groups = lax.axis_size("etp")
    experts = lax.axis_size("ep")
    ring = experts // 2
    half = rows // 2
    weights = (gate_proj, up_proj, down_proj)
    depth, hid = gate_proj.shape[1:]
    res = jax.ShapeDtypeStruct((2, half, width), BF)
    block = (2, groups, 2, 2, half, width)
    dma = pltpu.SemaphoreType.DMA
    hbm = pl.BlockSpec(memory_space=pltpu.HBM)
    vmem = pl.BlockSpec(memory_space=pltpu.VMEM)
    mates = groups - 1
    edge = width // EDGE // 128 * 128
    count = experts * rows
    outs = pl.pallas_call(
        functools.partial(fused_kernel, ring, groups, SLOTS),
        out_shape=(
            res,
            res,
            jax.ShapeDtypeStruct(gates.shape[::-1], F32),
            jax.ShapeDtypeStruct((ring,) + block, BF),
        ),
        in_specs=[hbm, hbm, vmem, vmem, hbm, hbm, hbm],
        out_specs=(vmem, vmem, vmem, hbm),
        scratch_shapes=[
            pltpu.VMEM((depth, hid), BF),
            pltpu.VMEM((depth, hid), BF),
            pltpu.VMEM((hid, depth), BF),
            pltpu.VMEM((SLOTS,) + block, BF),
            pltpu.VMEM((2, 2, groups, 2, half, width), BF),
            pltpu.VMEM((ring - 1, 2, groups, half, width), BF),
            pltpu.VMEM((ring - 1, 2, half, width), BF),
            pltpu.VMEM((ring, mates, 2, half, width), BF),
            pltpu.VMEM((mates, 2, half, width - edge), BF),
            pltpu.VMEM((ring, mates, 2, half, edge), BF),
            pltpu.VMEM((experts, 1, rows), F32),
            pltpu.VMEM((experts, 1, rows), F32),
            pltpu.VMEM((experts, 1, rows), F32),
            pltpu.VMEM((groups, experts, 1, rows), F32),
            dma((5,)),
            dma((2, mates)),
            dma((2, 2, ring)),
            dma((2, groups, 2, ring)),
            dma((2, mates, ring)),
            dma((2, 2, groups, ring)),
            dma((2, 2, ring)),
            dma((2, mates, ring)),
            dma((2, groups, 2, ring)),
            dma((2, 2, ring)),
            dma((2, mates)),
            dma((2, experts)),
            dma((2, groups, experts)),
            dma((2, mates, ring)),
            dma((2, mates, ring)),
            dma((2, mates, ring)),
            pltpu.SemaphoreType.REGULAR,
        ],
        cost_estimate=pl.CostEstimate(
            flops=12 * count * groups * width * hid,
            bytes_accessed=16 * count * groups * width,
            transcendentals=count * hid,
        ),
        compiler_params=pltpu.CompilerParams(
            collective_id=2, has_side_effects=True, vmem_limit_bytes=63 << 20
        ),
    )(tokens.reshape(2, half, width), grad_out.reshape(2, half, width), gates.T, expert_ids.T, *weights)
    return outs[0].reshape(rows, width), outs[1].reshape(rows, width), outs[2].T


def solution(mesh):
    in_specs = (
        P("ep", "etp"),
        P("ep", "etp"),
        P("ep", None),
        P("ep", None),
        P("ep", None, "etp"),
        P("ep", None, "etp"),
        P("ep", "etp", None),
    )
    out_specs = (P("ep", "etp"), P("ep", "etp"), P("ep", None))
    body = streamed if mesh.shape["ep"] <= 16 else local
    return jax.shard_map(body, mesh=mesh, in_specs=in_specs, out_specs=out_specs, check_vma=False)
```

```python
import functools
import math

import jax
import jax.numpy as jnp
import numpy as np
from jax import lax
from jax.experimental import pallas as pl
from jax.experimental.pallas import tpu as pltpu
from jax.sharding import PartitionSpec as P

BF = jnp.bfloat16
F32 = jnp.float32
MESH = pl.DeviceIdType.MESH


class Place:
    def __init__(self, ring, groups):
        self.ring, self.groups = ring, groups
        self.depth = math.gcd(ring, 4)
        self.cols = ring // self.depth
        me = lax.axis_index("ep")
        self.g = lax.axis_index("etp")
        self.core = lax.rem(me, 2)
        chip = me // 2
        x, z = lax.rem(chip, self.cols), chip // self.cols
        self.p = x * self.depth + z + lax.rem(x, 2) * (self.depth - 1 - 2 * z)

    def at(self, offset):
        return lax.rem(self.p + offset + self.ring, self.ring)

    def chip(self, offset):
        pos = self.at(offset)
        x, t = pos // self.depth, lax.rem(pos, self.depth)
        z = t + lax.rem(x, 2) * (self.depth - 1 - 2 * t)
        return ((z * self.cols + x) * 2 + self.core, self.g)

    def sibling(self):
        return (lax.axis_index("ep") + 1 - 2 * self.core, self.g)

    def group(self, j):
        return lax.rem(self.g + j, self.groups)

    def partner(self, j):
        return (lax.axis_index("ep"), self.group(j))

    def greet(self, with_sibling):
        barrier = pltpu.get_barrier_semaphore()
        others = [self.chip(1), self.chip(-1)] + [self.partner(j) for j in range(1, self.groups)]
        if with_sibling:
            others.append(self.sibling())
        for other in others:
            pl.semaphore_signal(barrier, inc=1, device_id=other, device_id_type=MESH)
        pl.semaphore_wait(barrier, len(others))


def remote(src, dst, send, recv, where):
    return pltpu.make_async_remote_copy(
        src_ref=src, dst_ref=dst, send_sem=send, recv_sem=recv, device_id=where, device_id_type=MESH
    )


def gather_kernel(
    ring, groups, tok_ref, grad_ref, tok, tok_sib, grad, grad_sib, local_sem, first, rings, fans, late
):
    at = Place(ring, groups)
    at.greet(True)
    g = at.g
    sib = at.sibling()
    own_tok = pltpu.make_async_copy(tok_ref, tok.at[g, at.p], local_sem.at[0])
    own_grad = pltpu.make_async_copy(grad_ref, grad.at[g, at.p], local_sem.at[1])
    own_tok.start()
    own_grad.start()
    heads = []
    for j in range(1, groups):
        head = remote(
            grad_ref, grad.at[g, at.p], first.at[0, j - 1], first.at[1, j - 1], at.partner(j)
        )
        head.start()
        heads.append(head)
    own_tok.wait()

    def back(d, s):
        return at.at(-s if d == 0 else s)

    fan_y, fan_s, fan_t = {}, {}, {}

    def fan_tok(s):
        for d in range(2):
            b = back(d, s)
            fan_y[s, d] = []
            for j in range(1, groups):
                c = remote(
                    tok.at[g, b, d],
                    tok.at[g, b, d],
                    fans.at[0, j, d, s],
                    fans.at[1, j, d, s],
                    at.partner(j),
                )
                c.start()
                fan_y[s, d].append(c)

    def fan_grad(s):
        for d in range(2):
            b = back(d, s)
            c = remote(
                grad.at[:, b, d], grad_sib.at[:, b, d], fans.at[0, 0, d, s], fans.at[1, 0, d, s], sib
            )
            c.start()
            fan_s[s, d] = c

    def fan_late(s):
        for d in range(2):
            b = back(d, s)
            for c in fan_y[s, d]:
                c.wait_recv()
            c = remote(tok.at[:, b, d], tok_sib.at[:, b, d], late.at[0, d, s], late.at[1, d, s], sib)
            c.start()
            fan_t[s, d] = c

    hops = {}

    def hop(kind, d, s):
        b = back(d, s - 1)
        block = tok.at[g, b, d] if kind == 0 else grad.at[:, b, d]
        if s > 1:
            hops[kind, d, s - 1].wait_recv()
        if s < ring:
            c = remote(
                block,
                block,
                rings.at[0, kind, d, s - 1],
                rings.at[1, kind, d, s - 1],
                at.chip(1 if d == 0 else -1),
            )
            c.start()
            hops[kind, d, s] = c

    for s in range(1, ring + 1):
        hop(0, 0, s)
        hop(0, 1, s)
        if s == 1:
            own_grad.wait()
            for head in heads:
                head.wait_recv()
        if s < ring:
            fan_tok(s - 1)
        hop(1, 0, s)
        hop(1, 1, s)
        if s < ring:
            fan_grad(s - 1)
        if s >= 2:
            fan_late(s - 2)
    fan_tok(ring - 1)
    fan_grad(ring - 1)
    fan_late(ring - 1)
    for c in list(fan_s.values()) + list(fan_t.values()):
        c.wait()
    for group in fan_y.values():
        for c in group:
            c.wait_send()
    for c in list(hops.values()) + heads:
        c.wait_send()


def gather(tokens, grad_out, ring, groups):
    rows, width = tokens.shape
    half = rows // 2
    full = jax.ShapeDtypeStruct((groups, ring, 2, half, width), BF)
    dma = pltpu.SemaphoreType.DMA
    hbm = pl.BlockSpec(memory_space=pltpu.HBM)
    return pl.pallas_call(
        functools.partial(gather_kernel, ring, groups),
        out_shape=(full,) * 4,
        in_specs=[hbm, hbm],
        out_specs=(hbm,) * 4,
        scratch_shapes=[
            dma((2,)),
            dma((2, groups - 1)),
            dma((2, 2, 2, ring - 1)),
            dma((2, groups, 2, ring)),
            dma((2, 2, ring)),
        ],
        compiler_params=pltpu.CompilerParams(collective_id=0, has_side_effects=True),
    )(tokens.reshape(2, half, width), grad_out.reshape(2, half, width))


def scatter_kernel(
    ring, groups, s_out, s_in, res_out, res_in, v_out, v_in, r_out, r_in, y_in, y_out, loads, rings, ys, tail
):
    at = Place(ring, groups)
    g = at.g
    half = v_in.shape[2]

    def dest(d, s):
        return at.at(-s if d == 0 else s)

    load_out, load_in, swap = {}, {}, {}
    for s in range(1, ring + 1):
        for d in range(2):
            b = dest(d, s)
            load_out[s, d] = pltpu.make_async_copy(
                s_out.at[:, b, d], v_out.at[:, b, d], loads.at[0, d, s - 1]
            )
            load_in[s, d] = pltpu.make_async_copy(s_in.at[g, b, d], v_in.at[b, d], loads.at[1, d, s - 1])
            load_out[s, d].start()
            load_in[s, d].start()
    at.greet(False)
    for s in range(1, ring + 1):
        for d in range(2):
            b = dest(d, s)
            swap[s, d] = []
            for j in range(1, groups):
                c = remote(
                    s_in.at[at.group(j), b, d],
                    y_in.at[j - 1, b, d],
                    ys.at[0, j - 1, d, s - 1],
                    ys.at[1, j - 1, d, s - 1],
                    at.partner(j),
                )
                c.start()
                swap[s, d].append(c)

    def total(target, others):
        @pl.loop(0, half // 16)
        def _(i):
            rows = pl.ds(pl.multiple_of(i * 16, 16), 16)
            acc = target[rows, :].astype(F32)
            for other in others:
                acc = acc + other[rows, :].astype(F32)
            target[rows, :] = acc.astype(BF)

    hop_out, hop_in = {}, {}
    for s in range(1, ring + 1):
        for d in range(2):
            b = dest(d, s)
            load_out[s, d].wait()
            if s > 1:
                hop_out[s - 1, d].wait_recv()
                for q in range(groups):
                    total(v_out.at[q, b, d], [r_out.at[d, s - 2, q]])
            if s < ring:
                c = remote(
                    v_out.at[:, b, d],
                    r_out.at[d, s - 1],
                    rings.at[0, 0, d, s - 1],
                    rings.at[1, 0, d, s - 1],
                    at.chip(1 if d == 0 else -1),
                )
                c.start()
                hop_out[s, d] = c
        if s == ring:
            ends = []
            for d in range(2):
                for j in range(1, groups):
                    c = remote(
                        v_out.at[at.group(j), at.p, d],
                        y_out.at[j - 1, d],
                        tail.at[0, j - 1, d],
                        tail.at[1, j - 1, d],
                        at.partner(j),
                    )
                    c.start()
                    ends.append(c)
        for d in range(2):
            b = dest(d, s)
            load_in[s, d].wait()
            others = []
            for c in swap[s, d]:
                c.wait_recv()
            others = [y_in.at[j - 1, b, d] for j in range(1, groups)]
            if s > 1:
                hop_in[s - 1, d].wait_recv()
                others.append(r_in.at[d, s - 2])
            total(v_in.at[b, d], others)
            if s < ring:
                c = remote(
                    v_in.at[b, d],
                    r_in.at[d, s - 1],
                    rings.at[0, 1, d, s - 1],
                    rings.at[1, 1, d, s - 1],
                    at.chip(1 if d == 0 else -1),
                )
                c.start()
                hop_in[s, d] = c
    for d in range(2):
        res_in[d] = v_in[at.p, d]
    for c in ends:
        c.wait_recv()
    for d in range(2):
        total(v_out.at[g, at.p, d], [y_out.at[j - 1, d] for j in range(1, groups)])
        res_out[d] = v_out[g, at.p, d]
    for c in list(hop_out.values()) + list(hop_in.values()) + ends:
        c.wait_send()
    for group in swap.values():
        for c in group:
            c.wait_send()


def scatter(s_out, s_in):
    groups, ring, _, half, width = s_out.shape
    res = jax.ShapeDtypeStruct((2, half, width), BF)
    dma = pltpu.SemaphoreType.DMA
    hbm = pl.BlockSpec(memory_space=pltpu.HBM)
    vmem = pl.BlockSpec(memory_space=pltpu.VMEM)
    out, inn = pl.pallas_call(
        functools.partial(scatter_kernel, ring, groups),
        out_shape=(res, res),
        in_specs=[hbm, hbm],
        out_specs=(vmem, vmem),
        scratch_shapes=[
            pltpu.VMEM((groups, ring, 2, half, width), BF),
            pltpu.VMEM((ring, 2, half, width), BF),
            pltpu.VMEM((2, ring - 1, groups, half, width), BF),
            pltpu.VMEM((2, ring - 1, half, width), BF),
            pltpu.VMEM((groups - 1, ring, 2, half, width), BF),
            pltpu.VMEM((groups - 1, 2, half, width), BF),
            dma((2, 2, ring)),
            dma((2, 2, 2, ring - 1)),
            dma((2, groups - 1, 2, ring)),
            dma((2, groups - 1, 2)),
        ],
        compiler_params=pltpu.CompilerParams(
            collective_id=1, has_side_effects=True, vmem_limit_bytes=60 << 20
        ),
    )(s_out, s_in)
    return out.reshape(2 * half, width), inn.reshape(2 * half, width)


def dot(a, b):
    return lax.dot_general(a, b, (((1,), (0,)), ((), ())), preferred_element_type=F32)


def dot_t(a, b):
    return lax.dot_general(a, b, (((1,), (1,)), ((), ())), preferred_element_type=F32)


def first_half(groups, gate_ref, tok, grad, gate_w, up_w, down_w, score):
    width = tok.shape[2]
    cuts = [slice(g * width, (g + 1) * width) for g in range(groups)]
    gate_pre = sum(dot(tok[g], gate_w[cuts[g], :]) for g in range(groups))
    up_pre = sum(dot(tok[g], up_w[cuts[g], :]) for g in range(groups))
    raw = sum(dot_t(grad[g], down_w[:, cuts[g]]) for g in range(groups))
    gate = gate_ref[...]
    sig = jax.nn.sigmoid(gate_pre)
    act = gate_pre * sig
    hidden = act * up_pre
    score[...] = jnp.sum(hidden * raw, axis=1, keepdims=True)
    back = raw * gate
    gate_grad = back * up_pre * sig * (1.0 + gate_pre * (1.0 - sig))
    return (hidden * gate).astype(BF), gate_grad.astype(BF), (back * act).astype(BF)


def second_half(groups, hidden, gate_grad, up_grad, gate_w, up_w, down_w, out, inn, add=None):
    width = out.shape[2]
    for g in range(groups):
        cut = slice(g * width, (g + 1) * width)
        res = dot(hidden, down_w[:, cut])
        if add:
            res = res + add[0][g].astype(F32)
        out[g] = res.astype(BF)
        res = dot_t(gate_grad, gate_w[cut, :]) + dot_t(up_grad, up_w[cut, :])
        if add:
            res = res + add[1][g].astype(F32)
        inn[g] = res.astype(BF)


def whole_kernel(groups, gate, tok, grad, gate_w, up_w, down_w, out, inn, score):
    mids = first_half(groups, gate, tok, grad, gate_w, up_w, down_w, score)
    second_half(groups, *mids, gate_w, up_w, down_w, out, inn)


def begin_kernel(groups, gate, tok, grad, gate_w, up_w, down_w, hidden, gate_grad, up_grad, score):
    mids = first_half(groups, gate, tok, grad, gate_w, up_w, down_w, score)
    hidden[...], gate_grad[...], up_grad[...] = mids


def finish_kernel(groups, hidden, gate_grad, up_grad, gate_w, up_w, down_w, add_out, add_in, out, inn):
    second_half(
        groups,
        hidden[...],
        gate_grad[...],
        up_grad[...],
        gate_w,
        up_w,
        down_w,
        out,
        inn,
        (add_out, add_in),
    )


def expert(stage, shape, weights, *rows):
    groups, count, width = shape
    hid = weights[0].shape[2]
    tile = 256
    slab = (pl.BlockSpec((groups, tile, width), lambda i: (0, i, 0)), jax.ShapeDtypeStruct(shape, BF))
    column = (pl.BlockSpec((tile, 1), lambda i: (i, 0)), jax.ShapeDtypeStruct((count, 1), F32))
    units = (pl.BlockSpec((tile, hid), lambda i: (i, 0)), jax.ShapeDtypeStruct((count, hid), BF))
    fixed = [
        pl.BlockSpec((None,) + w.shape[1:], lambda i: (0, 0, 0), pipeline_mode=pl.Buffered(1))
        for w in weights
    ]
    kernel, heads, tails, results = {
        "whole": (whole_kernel, [column, slab, slab], [], [slab, slab, column]),
        "begin": (begin_kernel, [column, slab, slab], [], [units, units, units, column]),
        "finish": (finish_kernel, [units, units, units], [slab, slab], [slab, slab]),
    }[stage]
    split = len(heads)
    return pl.pallas_call(
        functools.partial(kernel, groups),
        grid=(count // tile,),
        out_shape=[r[1] for r in results],
        in_specs=[h[0] for h in heads] + fixed + [t[0] for t in tails],
        out_specs=[r[0] for r in results],
        input_output_aliases={6: 0, 7: 1} if stage == "finish" else {},
        cost_estimate=pl.CostEstimate(
            flops=(12 if stage == "whole" else 6) * count * groups * width * hid,
            bytes_accessed=8 * count * groups * width,
            transcendentals=0 if stage == "finish" else count * hid,
        ),
        compiler_params=pltpu.CompilerParams(vmem_limit_bytes=60 << 20),
    )(*rows[:split], *weights, *rows[split:])


def local(tokens, grad_out, gates, expert_ids, gate_proj, up_proj, down_proj):
    rows, width = tokens.shape
    groups = lax.axis_size("etp")
    experts = lax.axis_size("ep")
    ring = experts // 2
    core = lax.rem(lax.axis_index("ep"), 2)
    depth = math.gcd(ring, 4)
    cols = ring // depth
    order = np.zeros(ring, np.int32)
    for pos in range(ring):
        x, t = pos // depth, pos % depth
        order[pos] = (t if x % 2 == 0 else depth - 1 - t) * cols + x
    inverse = np.argsort(order)
    count = ring * rows

    onehot = expert_ids[:, :, None] == jnp.arange(experts, dtype=jnp.int32)[None, None, :]
    table = jnp.sum(jnp.where(onehot, gates[:, :, None], 0.0), axis=1)
    mine = lax.all_to_all(table.T, "ep", split_axis=0, concat_axis=0, tiled=True)
    mine = mine.reshape(ring, 2, rows)
    mine = jnp.stack([mine[int(c)] for c in order]).transpose(1, 0, 2)
    mine = jnp.where(core == 0, mine, mine[::-1])

    flat = (groups, count, width)
    tok_own, tok_sib, grad_own, grad_sib = (
        a.reshape(flat) for a in gather(tokens, grad_out, ring, groups)
    )
    swap = [(i, i ^ 1) for i in range(experts)]
    weights = (gate_proj, up_proj, down_proj)
    *mids, score_own = expert("begin", flat, weights, mine[0].reshape(count, 1), tok_own, grad_own)
    out, inn, score_sib = expert("whole", flat, weights, mine[1].reshape(count, 1), tok_sib, grad_sib)
    got = (lax.ppermute(out, "ep", swap), lax.ppermute(inn, "ep", swap))
    out, inn = expert("finish", flat, weights, *mids, *got)
    scores = [score_own.reshape(ring, rows), score_sib.reshape(ring, rows)]
    shape = (groups, ring, 2, rows // 2, width)
    layer_out, token_grad = scatter(out.reshape(shape), inn.reshape(shape))

    score = jnp.stack(scores)
    score = jnp.where(core == 0, score, score[::-1]).transpose(1, 0, 2)
    score = jnp.stack([score[int(c)] for c in inverse]).reshape(experts, rows)
    score = lax.all_to_all(score, "ep", split_axis=0, concat_axis=0, tiled=True)
    score = lax.psum(score, "etp")
    picked = jnp.sum(jnp.where(onehot, score.T[:, None, :], 0.0), axis=2)
    return layer_out, token_grad, picked


class Stream:
    def __init__(self, ring, groups, slots, refs):
        self.ring, self.groups, self.slots = ring, groups, slots
        (
            self.tok_ref, self.grad_ref, self.gates, self.ids, self.gate_hbm, self.up_hbm, self.down_hbm,
            self.res_out, self.res_in, self.picked, self.inb,
            self.gate_w, self.up_w, self.down_w, self.st, self.sst, self.r_out, self.r_in, self.y_in, self.y_out,
            self.y_low,
            self.table, self.gate_rows, self.score, self.score_in,
            self.local_sem, self.head_sem, self.hop_t, self.hop_g, self.fan_sem, self.sib_g,
            self.sib_r, self.swap_sem, self.ring_o, self.ring_i, self.tail_sem, self.gate_sem, self.score_sem,
            self.fan_g, self.sib_x, self.swap_o, self.credit,
        ) = refs
        self.at = at = Place(ring, groups)
        self.g = at.g
        self.me = lax.axis_index("ep")
        self.sib = at.sibling()
        self.near = [at.chip(1), at.chip(-1)]
        self.half, self.width = self.st.shape[5], self.st.shape[6]
        self.mates = range(1, groups)
        self.edge = self.y_low.shape[4]
        self.others_first = [k % groups for k in range(1, groups + 1)]

    def low(self, ref):
        return ref.at[(slice(None),) * (len(ref.shape) - 1) + (pl.ds(0, self.edge),)]

    def high(self, ref):
        return ref.at[(slice(None),) * (len(ref.shape) - 1) + (pl.ds(self.edge, self.width - self.edge),)]

    def ring_part(self, ref, k):
        return ref if k == 0 else self.high(ref)

    def hop_tok(self, d, s, src=None):
        src = self.inb.at[s, 0, self.g, 0, d] if src is None else src
        return remote(
            src, self.inb.at[s + 1, 0, self.g, 0, d], self.hop_t.at[0, d, s], self.hop_t.at[1, d, s], self.near[d]
        )

    def hop_grad(self, k, d, s, src=None):
        q = self.at.group(k)
        src = self.ring_part(self.inb.at[s, 1, q, 0, d], k) if src is None else src
        dst = self.ring_part(self.inb.at[s + 1, 1, q, 0, d], k)
        return remote(src, dst, self.hop_g.at[0, k, d, s], self.hop_g.at[1, k, d, s], self.near[d])

    def head(self, j):
        return remote(
            self.high(self.grad_ref), self.high(self.inb.at[0, 1, self.g, 0]), self.head_sem.at[0, j - 1],
            self.head_sem.at[1, j - 1], self.at.partner(j),
        )

    def fan(self, j, s, src=None):
        block = self.inb.at[s, 0, self.g, 0]
        src = block if src is None else src
        return remote(src, block, self.fan_sem.at[0, j - 1, s], self.fan_sem.at[1, j - 1, s], self.at.partner(j))

    def fan_grad(self, j, s, src=None):
        block = self.low(self.inb.at[s, 1, self.g, 0])
        src = block if src is None else src
        return remote(src, block, self.fan_g.at[0, j - 1, s], self.fan_g.at[1, j - 1, s], self.at.partner(j))

    def sib_copy(self, kind, k, s, src=None):
        q = self.at.group(k)
        part = k if kind == 1 else 0
        src = self.ring_part(self.inb.at[s, kind, q, 0], part) if src is None else src
        dst = self.ring_part(self.inb.at[s, kind, q, 1], part)
        return remote(src, dst, self.sib_g.at[0, kind, k, s], self.sib_g.at[1, kind, k, s], self.sib)

    def sib_low(self, k, s):
        q = self.at.group(k)
        return remote(
            self.low(self.inb.at[s, 1, q, 0]), self.low(self.inb.at[s, 1, q, 1]), self.sib_x.at[0, k - 1, s],
            self.sib_x.at[1, k - 1, s], self.sib,
        )

    def sib_res(self, kind, slot, s, turn):
        return remote(
            self.st.at[slot, kind, :, 1], self.sst.at[lax.rem(turn, 2), kind], self.sib_r.at[0, kind, s], self.sib_r.at[1, kind, s],
            self.sib,
        )

    def swap(self, j, slot, s):
        return remote(
            self.st.at[slot, 1, self.at.group(j), 0], self.y_in.at[s, j - 1], self.swap_sem.at[0, j - 1, s],
            self.swap_sem.at[1, j - 1, s], self.at.partner(j),
        )

    def swap_low(self, j, slot, s):
        return remote(
            self.low(self.st.at[slot, 0, self.at.group(j), 0]), self.y_low.at[s, j - 1], self.swap_o.at[0, j - 1, s],
            self.swap_o.at[1, j - 1, s], self.at.partner(j),
        )

    def send_out(self, k, d, slot, s):
        q = self.at.group(k)
        return remote(
            self.ring_part(self.st.at[slot, 0, q, 0, d], k), self.ring_part(self.r_out.at[s - 1, d, q], k),
            self.ring_o.at[0, k, d, s], self.ring_o.at[1, k, d, s], self.near[d],
        )

    def send_in(self, d, slot, s):
        return remote(
            self.st.at[slot, 1, self.g, 0, d], self.r_in.at[s - 1, d], self.ring_i.at[0, d, s], self.ring_i.at[1, d, s],
            self.near[d],
        )

    def tail(self, j):
        return remote(
            self.high(self.st.at[0, 0, self.at.group(j), 0]), self.y_out.at[j - 1], self.tail_sem.at[0, j - 1],
            self.tail_sem.at[1, j - 1], self.at.partner(j),
        )

    def send_gate(self, e, row):
        return remote(
            self.table.at[e], self.gate_rows.at[row], self.gate_sem.at[0, e], self.gate_sem.at[1, row], (e, self.g)
        )

    def send_score(self, y, e, from_y, row):
        return remote(
            self.score.at[e], self.score_in.at[from_y, row], self.score_sem.at[0, y, e],
            self.score_sem.at[1, from_y, row], (e, y),
        )

    def slot_of(self, j):
        return jnp.where(j == 0, 0, 1 + lax.rem(j + self.slots - 2, self.slots - 1))

    def free(self, b):
        slot = self.slot_of(b)
        for kind in range(2):
            self.sib_res(kind, slot, b, 0).wait_send()
        for j in self.mates:
            self.swap(j, slot, b).wait_send()
            self.swap_low(j, slot, b).wait_send()
        for d in range(2):
            for k in range(self.groups):
                self.send_out(k, d, slot, b).wait_send()
            self.send_in(d, slot, b).wait_send()

    def greet_all(self):
        barrier = pltpu.get_barrier_semaphore()
        experts = 2 * self.ring

        @pl.loop(0, experts * self.groups)
        def _(i):
            e, y = i // self.groups, lax.rem(i, self.groups)

            @pl.when((e != self.me) | (y != self.g))
            def _():
                pl.semaphore_signal(barrier, inc=1, device_id=(e, y), device_id_type=MESH)

        pl.semaphore_wait(barrier, experts * self.groups - 1)

    def total(self, target, others, dest=None):
        dest = target if dest is None else dest

        @pl.loop(0, self.half // 16)
        def _(i):
            part = pl.ds(pl.multiple_of(i * 16, 16), 16)
            acc = target[part, :].astype(F32)
            for other in others:
                acc = acc + other[part, :].astype(F32)
            dest[part, :] = acc.astype(BF)

    def forward_tok(self, i):
        for d in range(2):
            self.hop_tok(d, i - 1).wait_recv()

            @pl.when(i < self.ring - 1)
            def _():
                self.hop_tok(d, i).start()

        for j in self.mates:
            self.fan(j, i).start()
        self.sib_copy(0, 0, i).start()

    def forward_grad(self, k, i):
        for d in range(2):
            self.hop_grad(k, d, i - 1).wait_recv()

            @pl.when(i < self.ring - 1)
            def _():
                self.hop_grad(k, d, i).start()

        if k == 0:
            for j in self.mates:
                self.fan_grad(j, i).start()
        self.sib_copy(1, k, i).start()


def fused_kernel(ring, groups, slots, *refs):
    self = Stream(ring, groups, slots, refs)
    at, g, me, mates = self.at, self.g, self.me, self.mates
    st, sst, inb = self.st, self.sst, self.inb
    gate_w, up_w, down_w = self.gate_w, self.up_w, self.down_w
    half, width = self.half, self.width
    rows, experts = 4 * half, 2 * ring
    pause = min(PAUSE, ring - 2)
    cuts = [slice(q * width, (q + 1) * width) for q in range(groups)]

    loads = [
        pltpu.make_async_copy(src.at[0], dst, self.local_sem.at[2 + k])
        for k, (src, dst) in enumerate([(self.gate_hbm, gate_w), (self.up_hbm, up_w), (self.down_hbm, down_w)])
    ]
    self.greet_all()
    for j in mates:
        self.head(j).start()
    for d in range(2):
        self.hop_tok(d, 0, self.tok_ref.at[d]).start()
    for d in range(2):
        self.hop_grad(0, d, 0, self.grad_ref.at[d]).start()
    self.sib_copy(0, 0, 0, self.tok_ref).start()
    self.sib_copy(1, 0, 0, self.grad_ref).start()
    for load in loads:
        load.start()

    def iota(shape, axis):
        return lax.broadcasted_iota(jnp.int32, shape, axis)

    diag = [iota((half, 2 * half), 0) + d * half == iota((half, 2 * half), 1) for d in range(2)]

    def as_row(column, mask):
        return jnp.sum(jnp.where(mask, column, 0.0), axis=0, keepdims=True)

    def as_column(row, mask):
        return jnp.sum(jnp.where(mask, row, 0.0), axis=1, keepdims=True)

    @pl.loop(0, experts)
    def _(e):
        mine = jnp.where(self.ids[...] == e, self.gates[...], 0.0)
        self.table[e] = jnp.sum(mine, axis=0, keepdims=True)
        self.score[e] = jnp.zeros((1, 2 * half), F32)

    @pl.loop(0, experts)
    def _(e):
        @pl.when(e != me)
        def _():
            self.send_gate(e, me).start()

    self.gate_rows[me] = self.table[me]
    self.forward_tok(1)
    for j in mates:
        self.fan(j, 0, self.tok_ref).start()
        self.fan_grad(j, 0, self.low(self.grad_ref)).start()
    for j in mates:
        self.head(j).wait_recv()
        for d in range(2):
            self.hop_grad(j, d, 0).start()
        self.sib_copy(1, j, 0).start()

    for k in range(groups):
        self.forward_grad(k, 1)

    @pl.loop(0, experts)
    def _(e):
        @pl.when(e != me)
        def _():
            self.send_gate(e, e).wait_recv()

    for w in loads:
        w.wait()

    def finish_in(j):
        slot = self.slot_of(j)
        for k in mates:
            self.swap(k, slot, j).wait_recv()
        for d in range(2):
            target = st.at[slot, 1, g, 0, d]
            added = [self.y_in.at[j, k - 1, d] for k in mates]

            @pl.when(j > 1)
            def _():
                self.send_in(d, slot, j - 1).wait_recv()
                self.total(target, added + [self.r_in.at[j - 2, d]])

            @pl.when(j <= 1)
            def _():
                self.total(target, added)

            @pl.when(j > 0)
            def _():
                self.send_in(d, slot, j).start()

    def begin_out(j, turn):
        slot = self.slot_of(j)
        got = sst.at[lax.rem(turn, 2)]
        self.sib_res(0, slot, j, turn).wait_recv()
        for k in mates:
            q = at.group(k)
            for d in range(2):
                self.total(self.low(st.at[slot, 0, q, 0, d]), [self.low(got.at[0, q, d])])
            self.swap_low(k, slot, j).start()

    def begin_in(j, turn):
        slot = self.slot_of(j)
        got = sst.at[lax.rem(turn, 2)]
        self.sib_res(1, slot, j, turn).wait_recv()
        for k in self.others_first:
            q = at.group(k)
            for d in range(2):
                self.total(st.at[slot, 1, q, 0, d], [got.at[1, q, d]])
            if k > 0:
                self.swap(k, slot, j).start()

    def total_out(k, d, slot, j, turn):
        q = at.group(k)
        got = sst.at[lax.rem(turn, 2)]
        parts = [(self.high, [])]
        if k == 0:
            parts.append((self.low, [self.y_low.at[j, m - 1, d] for m in mates]))

        @pl.when(j > 1)
        def _():
            self.send_out(k, d, slot, j - 1).wait_recv()
            for part, more in parts:
                added = [part(got.at[0, q, d]), part(self.r_out.at[j - 2, d, q])]
                self.total(part(st.at[slot, 0, q, 0, d]), added + more)

        @pl.when(j <= 1)
        def _():
            for part, more in parts:
                self.total(part(st.at[slot, 0, q, 0, d]), [part(got.at[0, q, d])] + more)

        @pl.when(j > 0)
        def _():
            self.send_out(k, d, slot, j).start()

    def send_block(j, turn):
        for k in mates:
            for d in range(2):
                total_out(k, d, self.slot_of(j), j, turn)

    def finish_block(j, turn):
        for k in mates:
            self.swap_low(k, self.slot_of(j), j).wait_recv()
        for d in range(2):
            total_out(0, d, self.slot_of(j), j, turn)

    def block_at(n):
        return jnp.where(n < pause, n + 1, jnp.where(n == pause, 0, n))

    @pl.loop(0, ring)
    def _(n):
        j = block_at(n)
        i = j + 1
        slot = self.slot_of(j)
        gather_on = (j > 0) & (i < ring)
        before = block_at(n - 1)

        @pl.when(n > 0)
        def _():
            begin_out(before, n - 1)

        @pl.when(gather_on)
        def _():
            self.forward_tok(i)

        for k in mates:
            self.fan(k, j).wait_recv()
            self.sib_copy(0, k, j).start()
            self.fan_grad(k, j).wait_recv()
            self.sib_low(k, j).start()

        @pl.when(n > 0)
        def _():
            begin_in(before, n - 1)

        @pl.when(j >= slots)
        def _():
            self.free(j - slots + 1)

        load = [pltpu.make_async_copy(inb.at[j, kind], st.at[slot, kind], self.local_sem.at[kind]) for kind in range(2)]
        for kind, own in ((1, self.grad_ref), (0, self.tok_ref)):
            for k in range(groups):
                self.sib_copy(kind, k, j).wait_recv()
                if kind == 1 and k > 0:
                    self.sib_low(k, j).wait_recv()

            @pl.when(j == 0)
            def _():
                pltpu.make_async_copy(own, st.at[0, kind, g, 0], self.local_sem.at[kind]).start()
                pieces = [(at.group(k), 0) for k in mates] + [(q, 1) for q in range(groups)]
                for q, c in pieces:
                    pltpu.make_async_copy(inb.at[0, kind, q, c], st.at[0, kind, q, c], self.local_sem.at[kind]).start()

            @pl.when(j > 0)
            def _():
                load[kind].start()

        @pl.when(n > 0)
        def _():
            send_block(before, n - 1)

        load[0].wait()
        gate_pre = up_pre = raw = 0.0
        for q in range(groups):
            tok = st[slot, 0, q].reshape(rows, width)
            gate_pre = gate_pre + dot(tok, gate_w[cuts[q], :])
            up_pre = up_pre + dot(tok, up_w[cuts[q], :])

        @pl.when(n > 0)
        def _():
            finish_block(before, n - 1)

        @pl.when(n > 1)
        def _():
            finish_in(block_at(n - 2))

        @pl.when((n > 0) & (n < ring - 1))
        def _():
            pl.semaphore_signal(self.credit, inc=1, device_id=self.sib, device_id_type=MESH)

        @pl.when(gather_on)
        def _():
            self.forward_grad(0, i)

        load[1].wait()
        for q in range(groups):
            raw = raw + dot_t(st[slot, 1, q].reshape(rows, width), down_w[:, cuts[q]])
        spots = [
            (at.chip(-j if d == 0 else j)[0] + c * (1 - 2 * at.core), d) for c in range(2) for d in range(2)
        ]
        gate = jnp.concatenate([as_column(self.gate_rows[e], diag[d]) for e, d in spots], axis=0)
        sig = jax.nn.sigmoid(gate_pre)
        act = gate_pre * sig
        hidden = act * up_pre
        marks = jnp.sum(hidden * raw, axis=1, keepdims=True)
        for k, (e, d) in enumerate(spots):
            self.score[e] = self.score[e] + as_row(marks[k * half : (k + 1) * half], diag[d])

        @pl.when(j == ring - 1)
        def _():
            @pl.loop(0, experts * groups)
            def _(n):
                e, y = n // groups, lax.rem(n, groups)

                @pl.when((e != me) | (y != g))
                def _():
                    self.send_score(y, e, g, me).start()

            self.score_in[g, me] = self.score[me]

        back = raw * gate
        gate_grad = (back * up_pre * sig * (1.0 + gate_pre * (1.0 - sig))).astype(BF)
        up_grad = (back * act).astype(BF)
        hidden = (hidden * gate).astype(BF)

        @pl.when(gather_on)
        def _():
            for k in mates:
                self.forward_grad(k, i)

        shape = (2, 2, half, width)
        for q in range(groups):
            st[slot, 0, q] = dot(hidden, down_w[:, cuts[q]]).astype(BF).reshape(shape)

        @pl.when(n > 1)
        def _():
            pl.semaphore_wait(self.credit, 1)

        self.sib_res(0, slot, j, n).start()

        for q in range(groups):
            res = dot_t(gate_grad, gate_w[cuts[q], :]) + dot_t(up_grad, up_w[cuts[q], :])
            st[slot, 1, q] = res.astype(BF).reshape(shape)
        self.sib_res(1, slot, j, n).start()

    last = jnp.int32(ring - 1)
    begin_out(last, ring - 1)
    begin_in(last, ring - 1)
    send_block(last, ring - 1)
    finish_in(block_at(ring - 2))
    finish_block(last, ring - 1)
    finish_in(last)

    for k in self.others_first:
        q = at.group(k)
        for d in range(2):
            self.send_out(k, d, 0, ring - 1).wait_recv()
            part = self.ring_part(st.at[0, 0, q, 0, d], k)
            self.total(part, [self.ring_part(self.r_out.at[ring - 2, d, q], k)])
        if k > 0:
            self.tail(k).start()
    @pl.loop(0, experts * groups)
    def _(n):
        e, y = n // groups, lax.rem(n, groups)

        @pl.when((e != me) | (y != g))
        def _():
            self.send_score(y, e, y, e).wait_recv()

    self.picked[...] = jnp.zeros_like(self.picked)

    @pl.loop(0, experts)
    def _(e):
        row = self.score_in[0, e]
        for y in range(1, groups):
            row = row + self.score_in[y, e]
        self.picked[...] += jnp.where(self.ids[...] == e, row, 0.0)

    for d in range(2):
        self.send_in(d, 0, ring - 1).wait_recv()
        self.total(
            st.at[0, 1, g, 0, d],
            [self.r_in.at[ring - 2, d]],
            self.res_in.at[d],
        )
    for j in mates:
        self.tail(j).wait_recv()
    for d in range(2):
        own, done = st.at[0, 0, g, 0, d], self.res_out.at[d]
        self.total(self.low(own), [], self.low(done))
        self.total(self.high(own), [self.y_out.at[j - 1, d] for j in mates], self.high(done))

    for kind in range(2):
        self.sib_res(kind, 0, 0, 0).wait_send()
    for j in mates:
        self.swap(j, 0, 0).wait_send()
        self.swap_low(j, 0, 0).wait_send()
        self.head(j).wait_send()
        self.tail(j).wait_send()

    @pl.loop(max(1, ring - slots + 1), ring)
    def _(b):
        self.free(b)

    @pl.loop(0, ring)
    def _(s):
        for j in mates:
            self.fan(j, s).wait_send()
            self.fan_grad(j, s).wait_send()
            self.sib_low(j, s).wait_send()
        for kind in range(2):
            for k in range(groups):
                self.sib_copy(kind, k, s).wait_send()

        @pl.when(s < ring - 1)
        def _():
            for d in range(2):
                self.hop_tok(d, s).wait_send()
                for k in range(groups):
                    self.hop_grad(k, d, s).wait_send()

    @pl.loop(0, experts * groups)
    def _(n):
        e, y = n // groups, lax.rem(n, groups)

        @pl.when((e != me) | (y != g))
        def _():
            self.send_score(y, e, g, me).wait_send()

        @pl.when((e != me) & (y == 0))
        def _():
            self.send_gate(e, me).wait_send()


SLOTS = 4
PAUSE = 2
EDGE = 8


def streamed(tokens, grad_out, gates, expert_ids, gate_proj, up_proj, down_proj):
    rows, width = tokens.shape
    groups = lax.axis_size("etp")
    experts = lax.axis_size("ep")
    ring = experts // 2
    half = rows // 2
    weights = (gate_proj, up_proj, down_proj)
    depth, hid = gate_proj.shape[1:]
    res = jax.ShapeDtypeStruct((2, half, width), BF)
    block = (2, groups, 2, 2, half, width)
    dma = pltpu.SemaphoreType.DMA
    hbm = pl.BlockSpec(memory_space=pltpu.HBM)
    vmem = pl.BlockSpec(memory_space=pltpu.VMEM)
    mates = groups - 1
    edge = width // EDGE // 128 * 128
    count = experts * rows
    outs = pl.pallas_call(
        functools.partial(fused_kernel, ring, groups, SLOTS),
        out_shape=(
            res,
            res,
            jax.ShapeDtypeStruct(gates.shape[::-1], F32),
            jax.ShapeDtypeStruct((ring,) + block, BF),
        ),
        in_specs=[hbm, hbm, vmem, vmem, hbm, hbm, hbm],
        out_specs=(vmem, vmem, vmem, hbm),
        scratch_shapes=[
            pltpu.VMEM((depth, hid), BF),
            pltpu.VMEM((depth, hid), BF),
            pltpu.VMEM((hid, depth), BF),
            pltpu.VMEM((SLOTS,) + block, BF),
            pltpu.VMEM((2, 2, groups, 2, half, width), BF),
            pltpu.VMEM((ring - 1, 2, groups, half, width), BF),
            pltpu.VMEM((ring - 1, 2, half, width), BF),
            pltpu.VMEM((ring, mates, 2, half, width), BF),
            pltpu.VMEM((mates, 2, half, width - edge), BF),
            pltpu.VMEM((ring, mates, 2, half, edge), BF),
            pltpu.VMEM((experts, 1, rows), F32),
            pltpu.VMEM((experts, 1, rows), F32),
            pltpu.VMEM((experts, 1, rows), F32),
            pltpu.VMEM((groups, experts, 1, rows), F32),
            dma((5,)),
            dma((2, mates)),
            dma((2, 2, ring)),
            dma((2, groups, 2, ring)),
            dma((2, mates, ring)),
            dma((2, 2, groups, ring)),
            dma((2, 2, ring)),
            dma((2, mates, ring)),
            dma((2, groups, 2, ring)),
            dma((2, 2, ring)),
            dma((2, mates)),
            dma((2, experts)),
            dma((2, groups, experts)),
            dma((2, mates, ring)),
            dma((2, mates, ring)),
            dma((2, mates, ring)),
            pltpu.SemaphoreType.REGULAR,
        ],
        cost_estimate=pl.CostEstimate(
            flops=12 * count * groups * width * hid,
            bytes_accessed=16 * count * groups * width,
            transcendentals=count * hid,
        ),
        compiler_params=pltpu.CompilerParams(
            collective_id=2, has_side_effects=True, vmem_limit_bytes=63 << 20
        ),
    )(tokens.reshape(2, half, width), grad_out.reshape(2, half, width), gates.T, expert_ids.T, *weights)
    return outs[0].reshape(rows, width), outs[1].reshape(rows, width), outs[2].T


def solution(mesh):
    in_specs = (
        P("ep", "etp"),
        P("ep", "etp"),
        P("ep", None),
        P("ep", None),
        P("ep", None, "etp"),
        P("ep", None, "etp"),
        P("ep", "etp", None),
    )
    out_specs = (P("ep", "etp"), P("ep", "etp"), P("ep", None))
    body = streamed if mesh.shape["ep"] <= 16 else local
    return jax.shard_map(body, mesh=mesh, in_specs=in_specs, out_specs=out_specs, check_vma=False)
```

```python
import functools
import math

import jax
import jax.numpy as jnp
import numpy as np
from jax import lax
from jax.experimental import pallas as pl
from jax.experimental.pallas import tpu as pltpu
from jax.sharding import PartitionSpec as P

BF = jnp.bfloat16
F32 = jnp.float32
MESH = pl.DeviceIdType.MESH


class Place:
    def __init__(self, ring, groups):
        self.ring, self.groups = ring, groups
        self.depth = math.gcd(ring, 4)
        self.cols = ring // self.depth
        me = lax.axis_index("ep")
        self.g = lax.axis_index("etp")
        self.core = lax.rem(me, 2)
        chip = me // 2
        x, z = lax.rem(chip, self.cols), chip // self.cols
        self.p = x * self.depth + z + lax.rem(x, 2) * (self.depth - 1 - 2 * z)

    def at(self, offset):
        return lax.rem(self.p + offset + self.ring, self.ring)

    def chip(self, offset):
        pos = self.at(offset)
        x, t = pos // self.depth, lax.rem(pos, self.depth)
        z = t + lax.rem(x, 2) * (self.depth - 1 - 2 * t)
        return ((z * self.cols + x) * 2 + self.core, self.g)

    def sibling(self):
        return (lax.axis_index("ep") + 1 - 2 * self.core, self.g)

    def group(self, j):
        return lax.rem(self.g + j, self.groups)

    def partner(self, j):
        return (lax.axis_index("ep"), self.group(j))

    def greet(self, with_sibling):
        barrier = pltpu.get_barrier_semaphore()
        others = [self.chip(1), self.chip(-1)] + [self.partner(j) for j in range(1, self.groups)]
        if with_sibling:
            others.append(self.sibling())
        for other in others:
            pl.semaphore_signal(barrier, inc=1, device_id=other, device_id_type=MESH)
        pl.semaphore_wait(barrier, len(others))


def remote(src, dst, send, recv, where):
    return pltpu.make_async_remote_copy(
        src_ref=src, dst_ref=dst, send_sem=send, recv_sem=recv, device_id=where, device_id_type=MESH
    )


def gather_kernel(
    ring, groups, tok_ref, grad_ref, tok, tok_sib, grad, grad_sib, local_sem, first, rings, fans, late
):
    at = Place(ring, groups)
    at.greet(True)
    g = at.g
    sib = at.sibling()
    own_tok = pltpu.make_async_copy(tok_ref, tok.at[g, at.p], local_sem.at[0])
    own_grad = pltpu.make_async_copy(grad_ref, grad.at[g, at.p], local_sem.at[1])
    own_tok.start()
    own_grad.start()
    heads = []
    for j in range(1, groups):
        head = remote(
            grad_ref, grad.at[g, at.p], first.at[0, j - 1], first.at[1, j - 1], at.partner(j)
        )
        head.start()
        heads.append(head)
    own_tok.wait()

    def back(d, s):
        return at.at(-s if d == 0 else s)

    fan_y, fan_s, fan_t = {}, {}, {}

    def fan_tok(s):
        for d in range(2):
            b = back(d, s)
            fan_y[s, d] = []
            for j in range(1, groups):
                c = remote(
                    tok.at[g, b, d],
                    tok.at[g, b, d],
                    fans.at[0, j, d, s],
                    fans.at[1, j, d, s],
                    at.partner(j),
                )
                c.start()
                fan_y[s, d].append(c)

    def fan_grad(s):
        for d in range(2):
            b = back(d, s)
            c = remote(
                grad.at[:, b, d], grad_sib.at[:, b, d], fans.at[0, 0, d, s], fans.at[1, 0, d, s], sib
            )
            c.start()
            fan_s[s, d] = c

    def fan_late(s):
        for d in range(2):
            b = back(d, s)
            for c in fan_y[s, d]:
                c.wait_recv()
            c = remote(tok.at[:, b, d], tok_sib.at[:, b, d], late.at[0, d, s], late.at[1, d, s], sib)
            c.start()
            fan_t[s, d] = c

    hops = {}

    def hop(kind, d, s):
        b = back(d, s - 1)
        block = tok.at[g, b, d] if kind == 0 else grad.at[:, b, d]
        if s > 1:
            hops[kind, d, s - 1].wait_recv()
        if s < ring:
            c = remote(
                block,
                block,
                rings.at[0, kind, d, s - 1],
                rings.at[1, kind, d, s - 1],
                at.chip(1 if d == 0 else -1),
            )
            c.start()
            hops[kind, d, s] = c

    for s in range(1, ring + 1):
        hop(0, 0, s)
        hop(0, 1, s)
        if s == 1:
            own_grad.wait()
            for head in heads:
                head.wait_recv()
        if s < ring:
            fan_tok(s - 1)
        hop(1, 0, s)
        hop(1, 1, s)
        if s < ring:
            fan_grad(s - 1)
        if s >= 2:
            fan_late(s - 2)
    fan_tok(ring - 1)
    fan_grad(ring - 1)
    fan_late(ring - 1)
    for c in list(fan_s.values()) + list(fan_t.values()):
        c.wait()
    for group in fan_y.values():
        for c in group:
            c.wait_send()
    for c in list(hops.values()) + heads:
        c.wait_send()


def gather(tokens, grad_out, ring, groups):
    rows, width = tokens.shape
    half = rows // 2
    full = jax.ShapeDtypeStruct((groups, ring, 2, half, width), BF)
    dma = pltpu.SemaphoreType.DMA
    hbm = pl.BlockSpec(memory_space=pltpu.HBM)
    return pl.pallas_call(
        functools.partial(gather_kernel, ring, groups),
        out_shape=(full,) * 4,
        in_specs=[hbm, hbm],
        out_specs=(hbm,) * 4,
        scratch_shapes=[
            dma((2,)),
            dma((2, groups - 1)),
            dma((2, 2, 2, ring - 1)),
            dma((2, groups, 2, ring)),
            dma((2, 2, ring)),
        ],
        compiler_params=pltpu.CompilerParams(collective_id=0, has_side_effects=True),
    )(tokens.reshape(2, half, width), grad_out.reshape(2, half, width))


def scatter_kernel(
    ring, groups, s_out, s_in, res_out, res_in, v_out, v_in, r_out, r_in, y_in, y_out, loads, rings, ys, tail
):
    at = Place(ring, groups)
    g = at.g
    half = v_in.shape[2]

    def dest(d, s):
        return at.at(-s if d == 0 else s)

    load_out, load_in, swap = {}, {}, {}
    for s in range(1, ring + 1):
        for d in range(2):
            b = dest(d, s)
            load_out[s, d] = pltpu.make_async_copy(
                s_out.at[:, b, d], v_out.at[:, b, d], loads.at[0, d, s - 1]
            )
            load_in[s, d] = pltpu.make_async_copy(s_in.at[g, b, d], v_in.at[b, d], loads.at[1, d, s - 1])
            load_out[s, d].start()
            load_in[s, d].start()
    at.greet(False)
    for s in range(1, ring + 1):
        for d in range(2):
            b = dest(d, s)
            swap[s, d] = []
            for j in range(1, groups):
                c = remote(
                    s_in.at[at.group(j), b, d],
                    y_in.at[j - 1, b, d],
                    ys.at[0, j - 1, d, s - 1],
                    ys.at[1, j - 1, d, s - 1],
                    at.partner(j),
                )
                c.start()
                swap[s, d].append(c)

    def total(target, others):
        @pl.loop(0, half // 16)
        def _(i):
            rows = pl.ds(pl.multiple_of(i * 16, 16), 16)
            acc = target[rows, :].astype(F32)
            for other in others:
                acc = acc + other[rows, :].astype(F32)
            target[rows, :] = acc.astype(BF)

    hop_out, hop_in = {}, {}
    for s in range(1, ring + 1):
        for d in range(2):
            b = dest(d, s)
            load_out[s, d].wait()
            if s > 1:
                hop_out[s - 1, d].wait_recv()
                for q in range(groups):
                    total(v_out.at[q, b, d], [r_out.at[d, s - 2, q]])
            if s < ring:
                c = remote(
                    v_out.at[:, b, d],
                    r_out.at[d, s - 1],
                    rings.at[0, 0, d, s - 1],
                    rings.at[1, 0, d, s - 1],
                    at.chip(1 if d == 0 else -1),
                )
                c.start()
                hop_out[s, d] = c
        if s == ring:
            ends = []
            for d in range(2):
                for j in range(1, groups):
                    c = remote(
                        v_out.at[at.group(j), at.p, d],
                        y_out.at[j - 1, d],
                        tail.at[0, j - 1, d],
                        tail.at[1, j - 1, d],
                        at.partner(j),
                    )
                    c.start()
                    ends.append(c)
        for d in range(2):
            b = dest(d, s)
            load_in[s, d].wait()
            others = []
            for c in swap[s, d]:
                c.wait_recv()
            others = [y_in.at[j - 1, b, d] for j in range(1, groups)]
            if s > 1:
                hop_in[s - 1, d].wait_recv()
                others.append(r_in.at[d, s - 2])
            total(v_in.at[b, d], others)
            if s < ring:
                c = remote(
                    v_in.at[b, d],
                    r_in.at[d, s - 1],
                    rings.at[0, 1, d, s - 1],
                    rings.at[1, 1, d, s - 1],
                    at.chip(1 if d == 0 else -1),
                )
                c.start()
                hop_in[s, d] = c
    for d in range(2):
        res_in[d] = v_in[at.p, d]
    for c in ends:
        c.wait_recv()
    for d in range(2):
        total(v_out.at[g, at.p, d], [y_out.at[j - 1, d] for j in range(1, groups)])
        res_out[d] = v_out[g, at.p, d]
    for c in list(hop_out.values()) + list(hop_in.values()) + ends:
        c.wait_send()
    for group in swap.values():
        for c in group:
            c.wait_send()


def scatter(s_out, s_in):
    groups, ring, _, half, width = s_out.shape
    res = jax.ShapeDtypeStruct((2, half, width), BF)
    dma = pltpu.SemaphoreType.DMA
    hbm = pl.BlockSpec(memory_space=pltpu.HBM)
    vmem = pl.BlockSpec(memory_space=pltpu.VMEM)
    out, inn = pl.pallas_call(
        functools.partial(scatter_kernel, ring, groups),
        out_shape=(res, res),
        in_specs=[hbm, hbm],
        out_specs=(vmem, vmem),
        scratch_shapes=[
            pltpu.VMEM((groups, ring, 2, half, width), BF),
            pltpu.VMEM((ring, 2, half, width), BF),
            pltpu.VMEM((2, ring - 1, groups, half, width), BF),
            pltpu.VMEM((2, ring - 1, half, width), BF),
            pltpu.VMEM((groups - 1, ring, 2, half, width), BF),
            pltpu.VMEM((groups - 1, 2, half, width), BF),
            dma((2, 2, ring)),
            dma((2, 2, 2, ring - 1)),
            dma((2, groups - 1, 2, ring)),
            dma((2, groups - 1, 2)),
        ],
        compiler_params=pltpu.CompilerParams(
            collective_id=1, has_side_effects=True, vmem_limit_bytes=60 << 20
        ),
    )(s_out, s_in)
    return out.reshape(2 * half, width), inn.reshape(2 * half, width)


def dot(a, b):
    return lax.dot_general(a, b, (((1,), (0,)), ((), ())), preferred_element_type=F32)


def dot_t(a, b):
    return lax.dot_general(a, b, (((1,), (1,)), ((), ())), preferred_element_type=F32)


def first_half(groups, gate_ref, tok, grad, gate_w, up_w, down_w, score):
    width = tok.shape[2]
    cuts = [slice(g * width, (g + 1) * width) for g in range(groups)]
    gate_pre = sum(dot(tok[g], gate_w[cuts[g], :]) for g in range(groups))
    up_pre = sum(dot(tok[g], up_w[cuts[g], :]) for g in range(groups))
    raw = sum(dot_t(grad[g], down_w[:, cuts[g]]) for g in range(groups))
    gate = gate_ref[...]
    sig = jax.nn.sigmoid(gate_pre)
    act = gate_pre * sig
    hidden = act * up_pre
    score[...] = jnp.sum(hidden * raw, axis=1, keepdims=True)
    back = raw * gate
    gate_grad = back * up_pre * sig * (1.0 + gate_pre * (1.0 - sig))
    return (hidden * gate).astype(BF), gate_grad.astype(BF), (back * act).astype(BF)


def second_half(groups, hidden, gate_grad, up_grad, gate_w, up_w, down_w, out, inn, add=None):
    width = out.shape[2]
    for g in range(groups):
        cut = slice(g * width, (g + 1) * width)
        res = dot(hidden, down_w[:, cut])
        if add:
            res = res + add[0][g].astype(F32)
        out[g] = res.astype(BF)
        res = dot_t(gate_grad, gate_w[cut, :]) + dot_t(up_grad, up_w[cut, :])
        if add:
            res = res + add[1][g].astype(F32)
        inn[g] = res.astype(BF)


def whole_kernel(groups, gate, tok, grad, gate_w, up_w, down_w, out, inn, score):
    mids = first_half(groups, gate, tok, grad, gate_w, up_w, down_w, score)
    second_half(groups, *mids, gate_w, up_w, down_w, out, inn)


def begin_kernel(groups, gate, tok, grad, gate_w, up_w, down_w, hidden, gate_grad, up_grad, score):
    mids = first_half(groups, gate, tok, grad, gate_w, up_w, down_w, score)
    hidden[...], gate_grad[...], up_grad[...] = mids


def finish_kernel(groups, hidden, gate_grad, up_grad, gate_w, up_w, down_w, add_out, add_in, out, inn):
    second_half(
        groups,
        hidden[...],
        gate_grad[...],
        up_grad[...],
        gate_w,
        up_w,
        down_w,
        out,
        inn,
        (add_out, add_in),
    )


def expert(stage, shape, weights, *rows):
    groups, count, width = shape
    hid = weights[0].shape[2]
    tile = 256
    slab = (pl.BlockSpec((groups, tile, width), lambda i: (0, i, 0)), jax.ShapeDtypeStruct(shape, BF))
    column = (pl.BlockSpec((tile, 1), lambda i: (i, 0)), jax.ShapeDtypeStruct((count, 1), F32))
    units = (pl.BlockSpec((tile, hid), lambda i: (i, 0)), jax.ShapeDtypeStruct((count, hid), BF))
    fixed = [
        pl.BlockSpec((None,) + w.shape[1:], lambda i: (0, 0, 0), pipeline_mode=pl.Buffered(1))
        for w in weights
    ]
    kernel, heads, tails, results = {
        "whole": (whole_kernel, [column, slab, slab], [], [slab, slab, column]),
        "begin": (begin_kernel, [column, slab, slab], [], [units, units, units, column]),
        "finish": (finish_kernel, [units, units, units], [slab, slab], [slab, slab]),
    }[stage]
    split = len(heads)
    return pl.pallas_call(
        functools.partial(kernel, groups),
        grid=(count // tile,),
        out_shape=[r[1] for r in results],
        in_specs=[h[0] for h in heads] + fixed + [t[0] for t in tails],
        out_specs=[r[0] for r in results],
        input_output_aliases={6: 0, 7: 1} if stage == "finish" else {},
        cost_estimate=pl.CostEstimate(
            flops=(12 if stage == "whole" else 6) * count * groups * width * hid,
            bytes_accessed=8 * count * groups * width,
            transcendentals=0 if stage == "finish" else count * hid,
        ),
        compiler_params=pltpu.CompilerParams(vmem_limit_bytes=60 << 20),
    )(*rows[:split], *weights, *rows[split:])


def local(tokens, grad_out, gates, expert_ids, gate_proj, up_proj, down_proj):
    rows, width = tokens.shape
    groups = lax.axis_size("etp")
    experts = lax.axis_size("ep")
    ring = experts // 2
    core = lax.rem(lax.axis_index("ep"), 2)
    depth = math.gcd(ring, 4)
    cols = ring // depth
    order = np.zeros(ring, np.int32)
    for pos in range(ring):
        x, t = pos // depth, pos % depth
        order[pos] = (t if x % 2 == 0 else depth - 1 - t) * cols + x
    inverse = np.argsort(order)
    count = ring * rows

    onehot = expert_ids[:, :, None] == jnp.arange(experts, dtype=jnp.int32)[None, None, :]
    table = jnp.sum(jnp.where(onehot, gates[:, :, None], 0.0), axis=1)
    mine = lax.all_to_all(table.T, "ep", split_axis=0, concat_axis=0, tiled=True)
    mine = mine.reshape(ring, 2, rows)
    mine = jnp.stack([mine[int(c)] for c in order]).transpose(1, 0, 2)
    mine = jnp.where(core == 0, mine, mine[::-1])

    flat = (groups, count, width)
    tok_own, tok_sib, grad_own, grad_sib = (
        a.reshape(flat) for a in gather(tokens, grad_out, ring, groups)
    )
    swap = [(i, i ^ 1) for i in range(experts)]
    weights = (gate_proj, up_proj, down_proj)
    *mids, score_own = expert("begin", flat, weights, mine[0].reshape(count, 1), tok_own, grad_own)
    out, inn, score_sib = expert("whole", flat, weights, mine[1].reshape(count, 1), tok_sib, grad_sib)
    got = (lax.ppermute(out, "ep", swap), lax.ppermute(inn, "ep", swap))
    out, inn = expert("finish", flat, weights, *mids, *got)
    scores = [score_own.reshape(ring, rows), score_sib.reshape(ring, rows)]
    shape = (groups, ring, 2, rows // 2, width)
    layer_out, token_grad = scatter(out.reshape(shape), inn.reshape(shape))

    score = jnp.stack(scores)
    score = jnp.where(core == 0, score, score[::-1]).transpose(1, 0, 2)
    score = jnp.stack([score[int(c)] for c in inverse]).reshape(experts, rows)
    score = lax.all_to_all(score, "ep", split_axis=0, concat_axis=0, tiled=True)
    score = lax.psum(score, "etp")
    picked = jnp.sum(jnp.where(onehot, score.T[:, None, :], 0.0), axis=2)
    return layer_out, token_grad, picked


class Stream:
    def __init__(self, ring, groups, slots, refs):
        self.ring, self.groups, self.slots = ring, groups, slots
        (
            self.tok_ref, self.grad_ref, self.gates, self.ids, self.gate_hbm, self.up_hbm, self.down_hbm,
            self.res_out, self.res_in, self.picked, self.inb,
            self.gate_w, self.up_w, self.down_w, self.st, self.sst, self.r_out, self.r_in, self.y_in, self.y_out,
            self.y_low,
            self.table, self.gate_rows, self.score, self.score_in,
            self.local_sem, self.head_sem, self.hop_t, self.hop_g, self.fan_sem, self.sib_g,
            self.sib_r, self.swap_sem, self.ring_o, self.ring_i, self.tail_sem, self.gate_sem, self.score_sem,
            self.fan_g, self.sib_x, self.swap_o, self.credit,
        ) = refs
        self.at = at = Place(ring, groups)
        self.g = at.g
        self.me = lax.axis_index("ep")
        self.sib = at.sibling()
        self.near = [at.chip(1), at.chip(-1)]
        self.half, self.width = self.st.shape[5], self.st.shape[6]
        self.mates = range(1, groups)
        self.edge = self.y_low.shape[4]
        self.others_first = [k % groups for k in range(1, groups + 1)]

    def low(self, ref):
        return ref.at[(slice(None),) * (len(ref.shape) - 1) + (pl.ds(0, self.edge),)]

    def high(self, ref):
        return ref.at[(slice(None),) * (len(ref.shape) - 1) + (pl.ds(self.edge, self.width - self.edge),)]

    def ring_part(self, ref, k):
        return ref if k == 0 else self.high(ref)

    def hop_tok(self, d, s, src=None):
        src = self.inb.at[s, 0, self.g, 0, d] if src is None else src
        return remote(
            src, self.inb.at[s + 1, 0, self.g, 0, d], self.hop_t.at[0, d, s], self.hop_t.at[1, d, s], self.near[d]
        )

    def hop_grad(self, k, d, s, src=None):
        q = self.at.group(k)
        src = self.ring_part(self.inb.at[s, 1, q, 0, d], k) if src is None else src
        dst = self.ring_part(self.inb.at[s + 1, 1, q, 0, d], k)
        return remote(src, dst, self.hop_g.at[0, k, d, s], self.hop_g.at[1, k, d, s], self.near[d])

    def head(self, j):
        return remote(
            self.high(self.grad_ref), self.high(self.inb.at[0, 1, self.g, 0]), self.head_sem.at[0, j - 1],
            self.head_sem.at[1, j - 1], self.at.partner(j),
        )

    def fan(self, j, s, src=None):
        block = self.inb.at[s, 0, self.g, 0]
        src = block if src is None else src
        return remote(src, block, self.fan_sem.at[0, j - 1, s], self.fan_sem.at[1, j - 1, s], self.at.partner(j))

    def fan_grad(self, j, s, src=None):
        block = self.low(self.inb.at[s, 1, self.g, 0])
        src = block if src is None else src
        return remote(src, block, self.fan_g.at[0, j - 1, s], self.fan_g.at[1, j - 1, s], self.at.partner(j))

    def sib_copy(self, kind, k, s, src=None):
        q = self.at.group(k)
        part = k if kind == 1 else 0
        src = self.ring_part(self.inb.at[s, kind, q, 0], part) if src is None else src
        dst = self.ring_part(self.inb.at[s, kind, q, 1], part)
        return remote(src, dst, self.sib_g.at[0, kind, k, s], self.sib_g.at[1, kind, k, s], self.sib)

    def sib_low(self, k, s):
        q = self.at.group(k)
        return remote(
            self.low(self.inb.at[s, 1, q, 0]), self.low(self.inb.at[s, 1, q, 1]), self.sib_x.at[0, k - 1, s],
            self.sib_x.at[1, k - 1, s], self.sib,
        )

    def sib_res(self, kind, slot, s, turn):
        return remote(
            self.st.at[slot, kind, :, 1], self.sst.at[lax.rem(turn, 2), kind], self.sib_r.at[0, kind, s], self.sib_r.at[1, kind, s],
            self.sib,
        )

    def swap(self, j, slot, s):
        return remote(
            self.st.at[slot, 1, self.at.group(j), 0], self.y_in.at[s, j - 1], self.swap_sem.at[0, j - 1, s],
            self.swap_sem.at[1, j - 1, s], self.at.partner(j),
        )

    def swap_low(self, j, slot, s):
        return remote(
            self.low(self.st.at[slot, 0, self.at.group(j), 0]), self.y_low.at[s, j - 1], self.swap_o.at[0, j - 1, s],
            self.swap_o.at[1, j - 1, s], self.at.partner(j),
        )

    def send_out(self, k, d, slot, s):
        q = self.at.group(k)
        return remote(
            self.ring_part(self.st.at[slot, 0, q, 0, d], k), self.ring_part(self.r_out.at[s - 1, d, q], k),
            self.ring_o.at[0, k, d, s], self.ring_o.at[1, k, d, s], self.near[d],
        )

    def send_in(self, d, slot, s):
        return remote(
            self.st.at[slot, 1, self.g, 0, d], self.r_in.at[s - 1, d], self.ring_i.at[0, d, s], self.ring_i.at[1, d, s],
            self.near[d],
        )

    def tail(self, j):
        return remote(
            self.high(self.st.at[0, 0, self.at.group(j), 0]), self.y_out.at[j - 1], self.tail_sem.at[0, j - 1],
            self.tail_sem.at[1, j - 1], self.at.partner(j),
        )

    def send_gate(self, e, row):
        return remote(
            self.table.at[e], self.gate_rows.at[row], self.gate_sem.at[0, e], self.gate_sem.at[1, row], (e, self.g)
        )

    def send_score(self, y, e, from_y, row):
        return remote(
            self.score.at[e], self.score_in.at[from_y, row], self.score_sem.at[0, y, e],
            self.score_sem.at[1, from_y, row], (e, y),
        )

    def slot_of(self, j):
        return jnp.where(j == 0, 0, 1 + lax.rem(j + self.slots - 2, self.slots - 1))

    def free(self, b):
        slot = self.slot_of(b)
        for kind in range(2):
            self.sib_res(kind, slot, b, 0).wait_send()
        for j in self.mates:
            self.swap(j, slot, b).wait_send()
            self.swap_low(j, slot, b).wait_send()
        for d in range(2):
            for k in range(self.groups):
                self.send_out(k, d, slot, b).wait_send()
            self.send_in(d, slot, b).wait_send()

    def greet_all(self):
        barrier = pltpu.get_barrier_semaphore()
        experts = 2 * self.ring

        @pl.loop(0, experts * self.groups)
        def _(i):
            e, y = i // self.groups, lax.rem(i, self.groups)

            @pl.when((e != self.me) | (y != self.g))
            def _():
                pl.semaphore_signal(barrier, inc=1, device_id=(e, y), device_id_type=MESH)

        pl.semaphore_wait(barrier, experts * self.groups - 1)

    def total(self, target, others, dest=None):
        dest = target if dest is None else dest

        @pl.loop(0, self.half // 16)
        def _(i):
            part = pl.ds(pl.multiple_of(i * 16, 16), 16)
            acc = target[part, :].astype(F32)
            for other in others:
                acc = acc + other[part, :].astype(F32)
            dest[part, :] = acc.astype(BF)

    def forward_tok(self, i):
        for d in range(2):
            self.hop_tok(d, i - 1).wait_recv()

            @pl.when(i < self.ring - 1)
            def _():
                self.hop_tok(d, i).start()

        for j in self.mates:
            self.fan(j, i).start()
        self.sib_copy(0, 0, i).start()

    def forward_grad(self, k, i):
        for d in range(2):
            self.hop_grad(k, d, i - 1).wait_recv()

            @pl.when(i < self.ring - 1)
            def _():
                self.hop_grad(k, d, i).start()

        if k == 0:
            for j in self.mates:
                self.fan_grad(j, i).start()
        self.sib_copy(1, k, i).start()


def fused_kernel(ring, groups, slots, *refs):
    self = Stream(ring, groups, slots, refs)
    at, g, me, mates = self.at, self.g, self.me, self.mates
    st, sst, inb = self.st, self.sst, self.inb
    gate_w, up_w, down_w = self.gate_w, self.up_w, self.down_w
    half, width = self.half, self.width
    rows, experts = 4 * half, 2 * ring
    pause = min(PAUSE, ring - 2)
    cuts = [slice(q * width, (q + 1) * width) for q in range(groups)]

    loads = [
        pltpu.make_async_copy(src.at[0], dst, self.local_sem.at[2 + k])
        for k, (src, dst) in enumerate([(self.gate_hbm, gate_w), (self.up_hbm, up_w), (self.down_hbm, down_w)])
    ]
    self.greet_all()
    for j in mates:
        self.head(j).start()
    for d in range(2):
        self.hop_tok(d, 0, self.tok_ref.at[d]).start()
    for d in range(2):
        self.hop_grad(0, d, 0, self.grad_ref.at[d]).start()
    self.sib_copy(0, 0, 0, self.tok_ref).start()
    self.sib_copy(1, 0, 0, self.grad_ref).start()
    for load in loads:
        load.start()

    def iota(shape, axis):
        return lax.broadcasted_iota(jnp.int32, shape, axis)

    diag = [iota((half, 2 * half), 0) + d * half == iota((half, 2 * half), 1) for d in range(2)]

    def as_row(column, mask):
        return jnp.sum(jnp.where(mask, column, 0.0), axis=0, keepdims=True)

    def as_column(row, mask):
        return jnp.sum(jnp.where(mask, row, 0.0), axis=1, keepdims=True)

    @pl.loop(0, experts)
    def _(e):
        mine = jnp.where(self.ids[...] == e, self.gates[...], 0.0)
        self.table[e] = jnp.sum(mine, axis=0, keepdims=True)
        self.score[e] = jnp.zeros((1, 2 * half), F32)

    @pl.loop(0, experts)
    def _(e):
        @pl.when(e != me)
        def _():
            self.send_gate(e, me).start()

    self.gate_rows[me] = self.table[me]
    self.forward_tok(1)
    for j in mates:
        self.fan(j, 0, self.tok_ref).start()
        self.fan_grad(j, 0, self.low(self.grad_ref)).start()
    for j in mates:
        self.head(j).wait_recv()
        for d in range(2):
            self.hop_grad(j, d, 0).start()
        self.sib_copy(1, j, 0).start()

    for k in range(groups):
        self.forward_grad(k, 1)

    @pl.loop(0, experts)
    def _(e):
        @pl.when(e != me)
        def _():
            self.send_gate(e, e).wait_recv()

    for w in loads:
        w.wait()

    def finish_in(j):
        slot = self.slot_of(j)
        for k in mates:
            self.swap(k, slot, j).wait_recv()
        for d in range(2):
            target = st.at[slot, 1, g, 0, d]
            added = [self.y_in.at[j, k - 1, d] for k in mates]

            @pl.when(j > 1)
            def _():
                self.send_in(d, slot, j - 1).wait_recv()
                self.total(target, added + [self.r_in.at[j - 2, d]])

            @pl.when(j <= 1)
            def _():
                self.total(target, added)

            @pl.when(j > 0)
            def _():
                self.send_in(d, slot, j).start()

    def begin_out(j, turn):
        slot = self.slot_of(j)
        got = sst.at[lax.rem(turn, 2)]
        self.sib_res(0, slot, j, turn).wait_recv()
        for k in mates:
            q = at.group(k)
            for d in range(2):
                self.total(self.low(st.at[slot, 0, q, 0, d]), [self.low(got.at[0, q, d])])
            self.swap_low(k, slot, j).start()

    def begin_in(j, turn):
        slot = self.slot_of(j)
        got = sst.at[lax.rem(turn, 2)]
        self.sib_res(1, slot, j, turn).wait_recv()
        for k in self.others_first:
            q = at.group(k)
            for d in range(2):
                self.total(st.at[slot, 1, q, 0, d], [got.at[1, q, d]])
            if k > 0:
                self.swap(k, slot, j).start()

    def total_out(k, d, slot, j, turn):
        q = at.group(k)
        got = sst.at[lax.rem(turn, 2)]
        parts = [(self.high, [])]
        if k == 0:
            parts.append((self.low, [self.y_low.at[j, m - 1, d] for m in mates]))

        @pl.when(j > 1)
        def _():
            self.send_out(k, d, slot, j - 1).wait_recv()
            for part, more in parts:
                added = [part(got.at[0, q, d]), part(self.r_out.at[j - 2, d, q])]
                self.total(part(st.at[slot, 0, q, 0, d]), added + more)

        @pl.when(j <= 1)
        def _():
            for part, more in parts:
                self.total(part(st.at[slot, 0, q, 0, d]), [part(got.at[0, q, d])] + more)

        @pl.when(j > 0)
        def _():
            self.send_out(k, d, slot, j).start()

    def send_block(j, turn):
        for k in mates:
            for d in range(2):
                total_out(k, d, self.slot_of(j), j, turn)

    def finish_block(j, turn):
        for k in mates:
            self.swap_low(k, self.slot_of(j), j).wait_recv()
        for d in range(2):
            total_out(0, d, self.slot_of(j), j, turn)

    def block_at(n):
        return jnp.where(n < pause, n + 1, jnp.where(n == pause, 0, n))

    @pl.loop(0, ring)
    def _(n):
        j = block_at(n)
        i = j + 1
        slot = self.slot_of(j)
        gather_on = (j > 0) & (i < ring)
        before = block_at(n - 1)

        @pl.when(n > 0)
        def _():
            begin_out(before, n - 1)

        @pl.when(gather_on)
        def _():
            self.forward_tok(i)

        for k in mates:
            self.fan(k, j).wait_recv()
            self.sib_copy(0, k, j).start()
            self.fan_grad(k, j).wait_recv()
            self.sib_low(k, j).start()

        @pl.when(n > 0)
        def _():
            begin_in(before, n - 1)

        @pl.when(j >= slots)
        def _():
            self.free(j - slots + 1)

        load = [pltpu.make_async_copy(inb.at[j, kind], st.at[slot, kind], self.local_sem.at[kind]) for kind in range(2)]
        for kind, own in ((1, self.grad_ref), (0, self.tok_ref)):
            for k in range(groups):
                self.sib_copy(kind, k, j).wait_recv()
                if kind == 1 and k > 0:
                    self.sib_low(k, j).wait_recv()

            @pl.when(j == 0)
            def _():
                pltpu.make_async_copy(own, st.at[0, kind, g, 0], self.local_sem.at[kind]).start()
                pieces = [(at.group(k), 0) for k in mates] + [(q, 1) for q in range(groups)]
                for q, c in pieces:
                    pltpu.make_async_copy(inb.at[0, kind, q, c], st.at[0, kind, q, c], self.local_sem.at[kind]).start()

            @pl.when(j > 0)
            def _():
                load[kind].start()

        @pl.when(n > 0)
        def _():
            send_block(before, n - 1)

        load[0].wait()
        gate_pre = up_pre = raw = 0.0
        for q in range(groups):
            tok = st[slot, 0, q].reshape(rows, width)
            gate_pre = gate_pre + dot(tok, gate_w[cuts[q], :])
            up_pre = up_pre + dot(tok, up_w[cuts[q], :])

        @pl.when(n > 0)
        def _():
            finish_block(before, n - 1)

        @pl.when(n > 1)
        def _():
            finish_in(block_at(n - 2))

        @pl.when((n > 0) & (n < ring - 1))
        def _():
            pl.semaphore_signal(self.credit, inc=1, device_id=self.sib, device_id_type=MESH)

        @pl.when(gather_on)
        def _():
            self.forward_grad(0, i)

        load[1].wait()
        for q in range(groups):
            raw = raw + dot_t(st[slot, 1, q].reshape(rows, width), down_w[:, cuts[q]])
        spots = [
            (at.chip(-j if d == 0 else j)[0] + c * (1 - 2 * at.core), d) for c in range(2) for d in range(2)
        ]
        gate = jnp.concatenate([as_column(self.gate_rows[e], diag[d]) for e, d in spots], axis=0)
        sig = jax.nn.sigmoid(gate_pre)
        act = gate_pre * sig
        hidden = act * up_pre
        marks = jnp.sum(hidden * raw, axis=1, keepdims=True)
        for k, (e, d) in enumerate(spots):
            self.score[e] = self.score[e] + as_row(marks[k * half : (k + 1) * half], diag[d])

        @pl.when(j == ring - 1)
        def _():
            @pl.loop(0, experts * groups)
            def _(n):
                e, y = n // groups, lax.rem(n, groups)

                @pl.when((e != me) | (y != g))
                def _():
                    self.send_score(y, e, g, me).start()

            self.score_in[g, me] = self.score[me]

        back = raw * gate
        gate_grad = (back * up_pre * sig * (1.0 + gate_pre * (1.0 - sig))).astype(BF)
        up_grad = (back * act).astype(BF)
        hidden = (hidden * gate).astype(BF)

        @pl.when(gather_on)
        def _():
            for k in mates:
                self.forward_grad(k, i)

        shape = (2, 2, half, width)
        for q in range(groups):
            st[slot, 0, q] = dot(hidden, down_w[:, cuts[q]]).astype(BF).reshape(shape)

        @pl.when(n > 1)
        def _():
            pl.semaphore_wait(self.credit, 1)

        self.sib_res(0, slot, j, n).start()

        for q in range(groups):
            res = dot_t(gate_grad, gate_w[cuts[q], :]) + dot_t(up_grad, up_w[cuts[q], :])
            st[slot, 1, q] = res.astype(BF).reshape(shape)
        self.sib_res(1, slot, j, n).start()

    last = jnp.int32(ring - 1)
    begin_out(last, ring - 1)
    begin_in(last, ring - 1)
    send_block(last, ring - 1)
    finish_in(block_at(ring - 2))
    finish_block(last, ring - 1)
    finish_in(last)

    for k in self.others_first:
        q = at.group(k)
        for d in range(2):
            self.send_out(k, d, 0, ring - 1).wait_recv()
            part = self.ring_part(st.at[0, 0, q, 0, d], k)
            self.total(part, [self.ring_part(self.r_out.at[ring - 2, d, q], k)])
        if k > 0:
            self.tail(k).start()
    @pl.loop(0, experts * groups)
    def _(n):
        e, y = n // groups, lax.rem(n, groups)

        @pl.when((e != me) | (y != g))
        def _():
            self.send_score(y, e, y, e).wait_recv()

    self.picked[...] = jnp.zeros_like(self.picked)

    @pl.loop(0, experts)
    def _(e):
        row = self.score_in[0, e]
        for y in range(1, groups):
            row = row + self.score_in[y, e]
        self.picked[...] += jnp.where(self.ids[...] == e, row, 0.0)

    @pl.loop(0, ring)
    def _(s):
        for j in mates:
            self.fan(j, s).wait_send()
            self.fan_grad(j, s).wait_send()
            self.sib_low(j, s).wait_send()
        for kind in range(2):
            for k in range(groups):
                self.sib_copy(kind, k, s).wait_send()

        @pl.when(s < ring - 1)
        def _():
            for d in range(2):
                self.hop_tok(d, s).wait_send()
                for k in range(groups):
                    self.hop_grad(k, d, s).wait_send()

    @pl.loop(0, experts * groups)
    def _(n):
        e, y = n // groups, lax.rem(n, groups)

        @pl.when((e != me) | (y != g))
        def _():
            self.send_score(y, e, g, me).wait_send()

        @pl.when((e != me) & (y == 0))
        def _():
            self.send_gate(e, me).wait_send()

    for d in range(2):
        self.send_in(d, 0, ring - 1).wait_recv()
        self.total(
            st.at[0, 1, g, 0, d],
            [self.r_in.at[ring - 2, d]],
            self.res_in.at[d],
        )
    for j in mates:
        self.tail(j).wait_recv()
    for d in range(2):
        own, done = st.at[0, 0, g, 0, d], self.res_out.at[d]
        self.total(self.low(own), [], self.low(done))
        self.total(self.high(own), [self.y_out.at[j - 1, d] for j in mates], self.high(done))

    for kind in range(2):
        self.sib_res(kind, 0, 0, 0).wait_send()
    for j in mates:
        self.swap(j, 0, 0).wait_send()
        self.swap_low(j, 0, 0).wait_send()
        self.head(j).wait_send()
        self.tail(j).wait_send()

    @pl.loop(max(1, ring - slots + 1), ring)
    def _(b):
        self.free(b)


SLOTS = 4
PAUSE = 2
EDGE = 8


def streamed(tokens, grad_out, gates, expert_ids, gate_proj, up_proj, down_proj):
    rows, width = tokens.shape
    groups = lax.axis_size("etp")
    experts = lax.axis_size("ep")
    ring = experts // 2
    half = rows // 2
    weights = (gate_proj, up_proj, down_proj)
    depth, hid = gate_proj.shape[1:]
    res = jax.ShapeDtypeStruct((2, half, width), BF)
    block = (2, groups, 2, 2, half, width)
    dma = pltpu.SemaphoreType.DMA
    hbm = pl.BlockSpec(memory_space=pltpu.HBM)
    vmem = pl.BlockSpec(memory_space=pltpu.VMEM)
    mates = groups - 1
    edge = width // EDGE // 128 * 128
    count = experts * rows
    outs = pl.pallas_call(
        functools.partial(fused_kernel, ring, groups, SLOTS),
        out_shape=(
            res,
            res,
            jax.ShapeDtypeStruct(gates.shape[::-1], F32),
            jax.ShapeDtypeStruct((ring,) + block, BF),
        ),
        in_specs=[hbm, hbm, vmem, vmem, hbm, hbm, hbm],
        out_specs=(vmem, vmem, vmem, hbm),
        scratch_shapes=[
            pltpu.VMEM((depth, hid), BF),
            pltpu.VMEM((depth, hid), BF),
            pltpu.VMEM((hid, depth), BF),
            pltpu.VMEM((SLOTS,) + block, BF),
            pltpu.VMEM((2, 2, groups, 2, half, width), BF),
            pltpu.VMEM((ring - 1, 2, groups, half, width), BF),
            pltpu.VMEM((ring - 1, 2, half, width), BF),
            pltpu.VMEM((ring, mates, 2, half, width), BF),
            pltpu.VMEM((mates, 2, half, width - edge), BF),
            pltpu.VMEM((ring, mates, 2, half, edge), BF),
            pltpu.VMEM((experts, 1, rows), F32),
            pltpu.VMEM((experts, 1, rows), F32),
            pltpu.VMEM((experts, 1, rows), F32),
            pltpu.VMEM((groups, experts, 1, rows), F32),
            dma((5,)),
            dma((2, mates)),
            dma((2, 2, ring)),
            dma((2, groups, 2, ring)),
            dma((2, mates, ring)),
            dma((2, 2, groups, ring)),
            dma((2, 2, ring)),
            dma((2, mates, ring)),
            dma((2, groups, 2, ring)),
            dma((2, 2, ring)),
            dma((2, mates)),
            dma((2, experts)),
            dma((2, groups, experts)),
            dma((2, mates, ring)),
            dma((2, mates, ring)),
            dma((2, mates, ring)),
            pltpu.SemaphoreType.REGULAR,
        ],
        cost_estimate=pl.CostEstimate(
            flops=12 * count * groups * width * hid,
            bytes_accessed=16 * count * groups * width,
            transcendentals=count * hid,
        ),
        compiler_params=pltpu.CompilerParams(
            collective_id=2, has_side_effects=True, vmem_limit_bytes=63 << 20
        ),
    )(tokens.reshape(2, half, width), grad_out.reshape(2, half, width), gates.T, expert_ids.T, *weights)
    return outs[0].reshape(rows, width), outs[1].reshape(rows, width), outs[2].T


def solution(mesh):
    in_specs = (
        P("ep", "etp"),
        P("ep", "etp"),
        P("ep", None),
        P("ep", None),
        P("ep", None, "etp"),
        P("ep", None, "etp"),
        P("ep", "etp", None),
    )
    out_specs = (P("ep", "etp"), P("ep", "etp"), P("ep", None))
    body = streamed if mesh.shape["ep"] <= 16 else local
    return jax.shard_map(body, mesh=mesh, in_specs=in_specs, out_specs=out_specs, check_vma=False)
```
